128 devices in a mesh: grp: 8 (over z_lo, x), blk: 16 (over z_hi, y, core).
Axes of the slice: x: 4, y: 4, z: 4 (z_hi: 2, z_lo: 2; z = z_hi * 2 + z_lo), core: 2. Of those that a mesh axis runs over, the one named last changes fastest.
Arguments:
- feats: bfloat16 [131072, 256], P(('grp', 'blk')), may hold values from -6 to 6
- weight: bfloat16 [256, 256], replicated, may hold values from -0.375 to 0.375
- cotangent: bfloat16 [131072, 256], P(('grp', 'blk')), may hold values from -6 to 6
- labels: int32 [131072], P(('grp', 'blk')), may hold values from -86 to 171
- tile_vals: bfloat16 [8, 16, 16, 32, 128, 128], P('grp', 'blk'), may hold values from -0.0625 to 0.0625
- tile_row: int32 [8, 16, 16, 32], P('grp', 'blk'), may hold values from 0 to 7
- tile_col: int32 [8, 16, 16, 32], P('grp', 'blk'), may hold values from 0 to 7
- tile_count: int32 [8, 16, 16], P('grp', 'blk'), may hold values from 1 to 32, as said below
- hub_vals: bfloat16 [8, 16, 16, 128, 128], P('grp', 'blk'), may hold values from -0.0625 to 0.0625
- hub_col: int32 [8, 16, 16], P('grp', 'blk'), may hold values from 0 to 7
- hub_dest: int32 [8, 16, 16, 1], P(None, 'blk'), may hold values from 0 to 7; in each aligned block of 16 rows (0 to 15, 16 to 31, ..., all dimensions but the last counted through in order) at most 4 rows name the same one
- hub_row: int32 [8, 16, 16], P(None, 'blk'), may hold values from 0 to 7
Outputs:
- layer_out: bfloat16 [131072, 256], P(('grp', 'blk'))
- grad_feats: bfloat16 [131072, 256], P(('grp', 'blk'))
- grad_weight: float32 [256, 256], replicated
The draws below stay inside these ranges and needn't reach their ends.
Inputs may be any that keep to these rules, and one draw needn't show every extreme that they name: Only the first tile_count slots of a device's list for a source block are used; some device uses all 32. `hub_dest`: at most 4 of the 16 hub tiles of one device name the same group, and exactly 4 in some devices.
All inputs are finite; a program needn't handle non-finite values.
Results may differ from the reference program's by a relative error of at most 0.007.
Values may be sent and summed in bfloat16 or wider, within the bound.
A program may use at most 192 MiB of HBM per device.

```python
import math
import jax
import jax.numpy as jnp
import numpy as np
from jax import lax

F = 256
TILE = 128
RT = 8
TPB = 32
HUB = 16
CAP = 4
NODES = 131072
N_GRP = 8
N_BLK = 16


def draw_tile_count(key, part):
    total = N_GRP * N_BLK * N_BLK
    base = jax.random.randint(key, (total,), max(1, TPB // 4), TPB + 1)
    where = jax.random.randint(jax.random.fold_in(key, 7), (), 0, total)
    filled = jnp.where(jnp.arange(total) == where, TPB, base)
    return filled.reshape(N_GRP, N_BLK, N_BLK).astype(jnp.int32)


def plant(values, stream_key, low, largest):
    shape = values.shape
    place = [jax.random.randint(jax.random.fold_in(stream_key, axis), (), 0, shape[axis]) for axis in range(len(shape))]
    values = values.at[tuple(place)].set(low)
    longest = shape.index(max(shape))
    place[longest] = (place[longest] + 1) % shape[longest]
    return values.at[tuple(place)].set(largest)


def steps_of(key, shape, cuts, smallest, top_value):
    level, own = 1.0, jax.random.fold_in(key, 6)
    for dim, parts in cuts:
        steps = jnp.exp(jax.random.uniform(jax.random.fold_in(own, dim), (parts,), jnp.float32, smallest / len(cuts), top_value / len(cuts)))
        level = level * jnp.repeat(steps, shape[dim] // parts).reshape([-1 if axis == dim else 1 for axis in range(len(shape))])
    return level


def assign_block(key, own, number, rows, amount, top, reach, lean):
    sequence = jax.random.permutation(key, amount)
    crowded, common = shares(amount, rows * top, reach, lean, True), shares(amount, rows * top, reach, lean, False)
    places = jnp.arange(amount)

    def named(tallies, rotation):
        used = int((tallies > 0).sum())
        fixed = max(1, used // 4)
        passed = fixed + (places - fixed + rotation * (used - fixed)) % max(1, amount - fixed)
        return jnp.zeros((amount,), jnp.int32).at[sequence[jnp.where(places < fixed, places, passed)]].set(jnp.asarray(tallies, jnp.int32))

    tallies = jnp.where(number % 4 == 0, named(crowded, number // 4), named(common, number - number // 4 - 1))
    mixed = jax.random.permutation(jax.random.fold_in(own, 3), amount)
    donor, taker = mixed[0:amount // 2 * 2:2], mixed[1:amount // 2 * 2:2]
    slack = jnp.minimum(tallies[donor] - 1, reach - tallies[taker]) // 2
    slack = jnp.where((donor == sequence[0]) | (taker == sequence[0]) | (tallies[taker] == 0), 0, jnp.maximum(slack, 0))
    passed = jax.random.randint(jax.random.fold_in(own, 4), (amount // 2,), 0, 1 << 20) % (slack + 1)
    tallies = tallies.at[donor].add(-passed).at[taker].add(passed)
    members = jnp.searchsorted(jnp.cumsum(tallies), jnp.arange(rows * top), side="right").astype(jnp.int32)
    listing = members.reshape(top, rows).T
    listing = listing[jax.random.permutation(jax.random.fold_in(own, 1), rows)]
    rotation = jax.random.randint(jax.random.fold_in(own, 2), (rows, 1), 0, top)
    return jnp.take_along_axis(listing, (jnp.arange(top)[None, :] + rotation) % top, axis=1)


def shares(count, total, reach, skew, full):
    weights = [(1 << 20) // math.isqrt(rank ** skew) + 1 for rank in range(1, count + 1)]
    largest = reach if full else min(reach, max(-(-total // count), total * weights[0] // sum(weights)))
    least = 1 if total - largest >= count - 1 else 0
    counts, surplus = [largest] + [least] * (count - 1), total - largest - least * (count - 1)
    while surplus > 0:
        free = [i for i in range(1, count) if counts[i] < largest] or [i for i in range(1, count) if counts[i] < reach]
        mass, left = sum([weights[i] for i in free]), surplus
        for i in free:
            more = min(reach - counts[i], max(1, left * weights[i] // mass), surplus)
            counts[i] = counts[i] + more
            surplus = surplus - more
    return np.array(counts)


def bell_draw(key, shape, width, most, split=(), dtype=jnp.bfloat16):
    values = jax.random.normal(key, shape, jnp.float32) * width
    if len(split) > 0:
        values = steps_of(key, shape, split, -0.22, 0.18) * values
    return jnp.clip(values, min=-most, max=most).astype(dtype)


def setup_inputs(seed: int = 0) -> dict:
    splits = jax.random.split(jax.random.key(seed), 13)
    feats = bell_draw(splits[0], (NODES, F), 1.0, 6.0, ((0, 128),))
    weight = bell_draw(splits[1], (F, F), F ** -0.5, 0.375)
    cotangent = bell_draw(splits[2], (NODES, F), 1.0, 6.0, ((0, 128),))
    labels = plant(jax.random.randint(splits[3], (NODES,), -86, 172), jax.random.fold_in(splits[3], 1), -86, 171).astype(jnp.int32)
    tile_vals = bell_draw(splits[4], (N_GRP, N_BLK, N_BLK, TPB, TILE, TILE), (N_BLK * TPB * TILE // RT) ** -0.5, 0.0625, ((0, 8), (1, 16)))
    tile_row = plant(jax.random.randint(splits[5], (N_GRP, N_BLK, N_BLK, TPB), 0, RT), jax.random.fold_in(splits[5], 1), 0, RT - 1).astype(jnp.int32)
    tile_col = plant(jax.random.randint(splits[6], (N_GRP, N_BLK, N_BLK, TPB), 0, RT), jax.random.fold_in(splits[6], 1), 0, RT - 1).astype(jnp.int32)
    tile_count = draw_tile_count(jax.random.fold_in(splits[12], 71), 0)
    hub_vals = bell_draw(splits[8], (N_GRP, N_BLK, HUB, TILE, TILE), (N_BLK * TPB * TILE // RT) ** -0.5, 0.0625, ((0, 8), (1, 16)))
    hub_col = plant(jax.random.randint(splits[9], (N_GRP, N_BLK, HUB), 0, RT), jax.random.fold_in(splits[9], 1), 0, RT - 1).astype(jnp.int32)
    hub_dest_keys = jax.random.split(jax.random.fold_in(splits[10], 1), N_GRP * N_BLK * HUB // HUB)
    hub_dest_turns = jax.random.permutation(jax.random.fold_in(splits[10], 3), N_GRP * N_BLK * HUB // HUB)
    hub_dest = jax.vmap(lambda own, number: assign_block(jax.random.fold_in(splits[10], 2), own, number, HUB, N_GRP, 1, CAP, 2))(hub_dest_keys, hub_dest_turns).reshape((N_GRP, N_BLK, HUB, 1))
    hub_row = plant(jax.random.randint(splits[11], (N_GRP, N_BLK, HUB), 0, RT), jax.random.fold_in(splits[11], 1), 0, RT - 1).astype(jnp.int32)
    return {"feats": feats, "weight": weight, "cotangent": cotangent, "labels": labels, "tile_vals": tile_vals, "tile_row": tile_row, "tile_col": tile_col, "tile_count": tile_count, "hub_vals": hub_vals, "hub_col": hub_col, "hub_dest": hub_dest, "hub_row": hub_row}


def forward_device(inputs):
    dev_vals, dev_rows, dev_cols, dev_count, panels = inputs
    picked = panels[jnp.arange(N_BLK)[:, None], dev_cols]
    product = jnp.einsum('ctij,ctjf->ctif', dev_vals.astype(jnp.float32), picked.astype(jnp.float32))
    live_mask = (jnp.arange(TPB)[None, :] < dev_count[:, None]).astype(jnp.float32)
    placing = (dev_rows[..., None] == jnp.arange(RT)[None, None, :]).astype(jnp.float32) * live_mask[..., None]
    return jnp.einsum('ctr,ctif->rif', placing, product)

def backward_group(inputs):
    grp_vals, grp_rows, grp_cols, grp_count, grp_grad = inputs

    def add_block(carry, xs):
        dev_vals, dev_rows, dev_cols, dev_count, grad_tiles = xs
        picked = grad_tiles[dev_rows]
        product = jnp.einsum('ctij,ctif->ctjf', dev_vals.astype(jnp.float32), picked.astype(jnp.float32))
        live_mask = (jnp.arange(TPB)[None, :] < dev_count[:, None]).astype(jnp.float32)
        placing = (dev_cols[..., None] == jnp.arange(RT)[None, None, :]).astype(jnp.float32) * live_mask[..., None]
        return (carry + jnp.einsum('ctr,ctjf->crjf', placing, product), None)
    start_acc = jnp.zeros((N_BLK, RT, TILE, F), jnp.float32)
    result, _ = lax.scan(add_block, start_acc, (grp_vals, grp_rows, grp_cols, grp_count, grp_grad))
    return result

def reference(feats, weight, cotangent, labels, tile_vals, tile_row, tile_col, tile_count, hub_vals, hub_col, hub_dest, hub_row):
    proj = jnp.dot(feats, weight, preferred_element_type=jnp.float32).astype(jnp.bfloat16)
    proj_tiles = proj.reshape(N_GRP, N_BLK, RT, TILE, F)
    group_of = jnp.repeat(jnp.arange(N_GRP), N_BLK)
    panels_all = proj_tiles[group_of]
    agg = lax.map(forward_device, (tile_vals.reshape(N_GRP * N_BLK, N_BLK, TPB, TILE, TILE), tile_row.reshape(N_GRP * N_BLK, N_BLK, TPB), tile_col.reshape(N_GRP * N_BLK, N_BLK, TPB), tile_count.reshape(N_GRP * N_BLK, N_BLK), panels_all))
    agg = agg.reshape(N_GRP, N_BLK, RT, TILE, F)
    grp_index = jnp.arange(N_GRP)[:, None, None]
    blk_index = jnp.arange(N_BLK)[None, :, None]
    dest = hub_dest[..., 0]
    hub_src = proj_tiles[grp_index, blk_index, hub_col]
    hub_part = jnp.einsum('gbhij,gbhjf->gbhif', hub_vals.astype(jnp.float32), hub_src.astype(jnp.float32))
    agg = agg.at[dest, blk_index, hub_row].add(hub_part)
    agg_rows = agg.reshape(NODES, F)
    layer_out = jax.nn.silu(agg_rows).astype(jnp.bfloat16)
    sigmoid_z = jax.nn.sigmoid(agg_rows)
    slope = sigmoid_z * (1.0 + agg_rows * (1.0 - sigmoid_z))
    keep = (labels >= 0).astype(jnp.float32)[:, None]
    grad_agg = (cotangent.astype(jnp.float32) * keep * slope).astype(jnp.bfloat16)
    grad_tiles = grad_agg.reshape(N_GRP, N_BLK, RT, TILE, F)
    grad_proj = lax.map(backward_group, (tile_vals, tile_row, tile_col, tile_count, grad_tiles))
    hub_grad = grad_tiles[dest, blk_index, hub_row]
    hub_back = jnp.einsum('gbhij,gbhif->gbhjf', hub_vals.astype(jnp.float32), hub_grad.astype(jnp.float32))
    grad_proj = grad_proj.at[grp_index, blk_index, hub_col].add(hub_back)
    grad_rows = grad_proj.reshape(NODES, F).astype(jnp.bfloat16)
    grad_weight = jnp.dot(feats.T, grad_rows, preferred_element_type=jnp.float32) * (1.0 / math.sqrt(NODES))
    grad_feats = jnp.dot(grad_rows, weight.T, preferred_element_type=jnp.float32).astype(jnp.bfloat16)
    return (layer_out, grad_feats, grad_weight)
```

```python
import functools
import math

import jax
import jax.numpy as jnp
from jax import lax
from jax.experimental import pallas as pl
from jax.experimental.pallas import tpu as pltpu
from jax.sharding import PartitionSpec as P


def forward_kernel(rows_ref, cols_ref, count_ref, vals_ref, panel_ref, out_ref):
    c = pl.program_id(0)
    slots = vals_ref.shape[1]

    @pl.when(c == 0)
    def _():
        out_ref[...] = jnp.zeros_like(out_ref)

    def body(t, carry):
        r = rows_ref[c * slots + t]
        k = cols_ref[c * slots + t]
        out_ref[r] += jnp.dot(vals_ref[0, t], panel_ref[0, k], preferred_element_type=jnp.float32)
        return carry

    lax.fori_loop(0, count_ref[c], body, 0)


def backward_kernel(rows_ref, cols_ref, count_ref, vals_ref, grad_ref, out_ref):
    c = pl.program_id(0)
    slots = vals_ref.shape[1]
    out_ref[...] = jnp.zeros_like(out_ref)

    def body(t, carry):
        r = rows_ref[c * slots + t]
        k = cols_ref[c * slots + t]
        out_ref[0, k] += lax.dot_general(
            vals_ref[0, t], grad_ref[r], (((0,), (0,)), ((), ())), preferred_element_type=jnp.float32
        )
        return carry

    lax.fori_loop(0, count_ref[c], body, 0)


def tile_forward(rows, cols, count, vals, panels):
    n_src, slots, tile, _ = vals.shape
    row_tiles, width = panels.shape[1], panels.shape[3]
    grid_spec = pltpu.PrefetchScalarGridSpec(
        num_scalar_prefetch=3,
        grid=(n_src,),
        in_specs=[
            pl.BlockSpec((1, slots, tile, tile), lambda c, *_: (c, 0, 0, 0)),
            pl.BlockSpec((1, row_tiles, tile, width), lambda c, *_: (c, 0, 0, 0)),
        ],
        out_specs=pl.BlockSpec((row_tiles, tile, width), lambda c, *_: (0, 0, 0)),
    )
    flops = 2 * n_src * slots * tile * tile * width
    return pl.pallas_call(
        forward_kernel,
        out_shape=jax.ShapeDtypeStruct((row_tiles, tile, width), jnp.float32),
        grid_spec=grid_spec,
        cost_estimate=pl.CostEstimate(
            flops=flops, transcendentals=0, bytes_accessed=vals.size * 2 + panels.size * 2
        ),
    )(rows, cols, count, vals, panels)


def tile_backward(rows, cols, count, vals, grad_tiles):
    n_src, slots, tile, _ = vals.shape
    row_tiles, width = grad_tiles.shape[0], grad_tiles.shape[2]
    grid_spec = pltpu.PrefetchScalarGridSpec(
        num_scalar_prefetch=3,
        grid=(n_src,),
        in_specs=[
            pl.BlockSpec((1, slots, tile, tile), lambda c, *_: (c, 0, 0, 0)),
            pl.BlockSpec((row_tiles, tile, width), lambda c, *_: (0, 0, 0)),
        ],
        out_specs=pl.BlockSpec((1, row_tiles, tile, width), lambda c, *_: (c, 0, 0, 0)),
    )
    flops = 2 * n_src * slots * tile * tile * width
    return pl.pallas_call(
        backward_kernel,
        out_shape=jax.ShapeDtypeStruct((n_src, row_tiles, tile, width), jnp.float32),
        grid_spec=grid_spec,
        cost_estimate=pl.CostEstimate(
            flops=flops, transcendentals=0, bytes_accessed=vals.size * 2 + n_src * row_tiles * tile * width * 4
        ),
    )(rows, cols, count, vals, grad_tiles)


def local(
    feats,
    weight,
    cotangent,
    labels,
    tile_vals,
    tile_row,
    tile_col,
    tile_count,
    hub_vals,
    hub_col,
    hub_dest,
    hub_row,
):
    n_blocks = lax.axis_size("blk")
    n_groups = lax.axis_size("grp")
    my_group = lax.axis_index("grp")
    rows_dev = feats.shape[0]
    width = feats.shape[1]
    tile_size = tile_vals.shape[-1]
    row_tiles = rows_dev // tile_size
    hub_count = hub_vals.shape[2]
    capacity = max(2, hub_count // 4)
    highest = lax.Precision.HIGHEST
    dev_vals = tile_vals[0, 0]
    dev_rows = tile_row[0, 0].reshape(-1)
    dev_cols = tile_col[0, 0].reshape(-1)
    dev_count = tile_count[0, 0]
    tile_range = jnp.arange(row_tiles, dtype=jnp.int32)
    proj = jnp.dot(feats, weight, preferred_element_type=jnp.float32).astype(jnp.bfloat16)
    own_panel = proj.reshape(row_tiles, tile_size, width)

    panels = lax.all_gather(proj, "blk", axis=0, tiled=True)
    panels = panels.reshape(n_blocks, row_tiles, tile_size, width)
    agg_sum = tile_forward(dev_rows, dev_cols, dev_count, dev_vals, panels)

    dest_all = hub_dest[:, 0, :, 0]
    hub_rows_all = hub_row[:, 0, :]
    hub_range = jnp.arange(hub_count, dtype=jnp.int32)
    earlier = hub_range[None, :] < hub_range[:, None]
    same_dest = dest_all[:, :, None] == dest_all[:, None, :]
    rank_all = jnp.sum((same_dest & earlier[None, :, :]).astype(jnp.int32), axis=-1)
    my_dest = lax.dynamic_index_in_dim(dest_all, my_group, 0, keepdims=False)
    my_rank = lax.dynamic_index_in_dim(rank_all, my_group, 0, keepdims=False)
    slot_of = my_dest * capacity + my_rank
    send_place = (
        slot_of[:, None] == jnp.arange(n_groups * capacity, dtype=jnp.int32)[None, :]
    ).astype(jnp.float32)
    hub_tiles = hub_vals[0, 0]
    hub_cols = hub_col[0, 0]
    hub_src = jnp.take(own_panel, hub_cols, axis=0)
    hub_part = jnp.einsum("hij,hjf->hif", hub_tiles, hub_src, preferred_element_type=jnp.float32)
    send_buf = jnp.einsum("hs,hif->sif", send_place, hub_part, precision=highest)
    send_buf = send_buf.reshape(n_groups, capacity, tile_size, width)
    received = lax.all_to_all(send_buf, "grp", split_axis=0, concat_axis=0, tiled=True)
    chosen = (dest_all == my_group).astype(jnp.float32)
    slot_hot = (rank_all[..., None] == jnp.arange(capacity, dtype=jnp.int32)).astype(
        jnp.float32
    ) * chosen[..., None]
    row_hot = (hub_rows_all[..., None] == tile_range).astype(jnp.float32)
    routing = jnp.einsum("shc,shr->scr", slot_hot, row_hot, precision=highest)
    agg_sum = agg_sum + jnp.einsum("scr,scif->rif", routing, received, precision=highest)
    agg_rows = agg_sum.reshape(rows_dev, width)
    layer_out = jax.nn.silu(agg_rows).astype(jnp.bfloat16)
    sigmoid_z = jax.nn.sigmoid(agg_rows)
    slope = sigmoid_z * (1.0 + agg_rows * (1.0 - sigmoid_z))
    keep = (labels >= 0).astype(jnp.float32)[:, None]
    grad_agg = (cotangent.astype(jnp.float32) * keep * slope).astype(jnp.bfloat16)
    grad_tiles = grad_agg.reshape(row_tiles, tile_size, width)

    partials = tile_backward(dev_rows, dev_cols, dev_count, dev_vals, grad_tiles)
    grad_sum = lax.psum_scatter(partials, "blk", scatter_dimension=0, tiled=True)[0]

    back_send = jnp.einsum(
        "scr,rif->scif",
        routing.astype(jnp.bfloat16),
        grad_tiles,
        preferred_element_type=jnp.float32,
    ).astype(jnp.bfloat16)
    back_recv = lax.all_to_all(back_send, "grp", split_axis=0, concat_axis=0, tiled=True)
    back_flat = back_recv.reshape(n_groups * capacity, tile_size, width)
    own_pick = jnp.einsum(
        "hs,sif->hif",
        send_place.astype(jnp.bfloat16),
        back_flat,
        preferred_element_type=jnp.float32,
    ).astype(jnp.bfloat16)
    hub_back = jnp.einsum("hij,hif->hjf", hub_tiles, own_pick, preferred_element_type=jnp.float32)
    col_hot = (hub_cols[:, None] == tile_range[None, :]).astype(jnp.float32)
    grad_sum = grad_sum + jnp.einsum("hr,hjf->rjf", col_hot, hub_back, precision=highest)
    grad_rows = grad_sum.reshape(rows_dev, width).astype(jnp.bfloat16)
    weight_term = lax.dot_general(
        feats, grad_rows, (((0,), (0,)), ((), ())), preferred_element_type=jnp.float32
    )
    grad_scale = 1.0 / math.sqrt(rows_dev * n_blocks * n_groups)
    grad_weight = lax.psum(weight_term, ("grp", "blk")) * grad_scale
    grad_feats = lax.dot_general(
        grad_rows, weight, (((1,), (1,)), ((), ())), preferred_element_type=jnp.float32
    ).astype(jnp.bfloat16)
    return (layer_out, grad_feats, grad_weight)


def solution(mesh):
    in_specs = (
        P(("grp", "blk"), None),
        P(),
        P(("grp", "blk"), None),
        P(("grp", "blk")),
        P("grp", "blk", None, None, None, None),
        P("grp", "blk", None, None),
        P("grp", "blk", None, None),
        P("grp", "blk", None),
        P("grp", "blk", None, None, None),
        P("grp", "blk", None),
        P(None, "blk", None, None),
        P(None, "blk", None),
    )
    out_specs = (P(("grp", "blk"), None), P(("grp", "blk"), None), P())
    return jax.shard_map(local, mesh=mesh, in_specs=in_specs, out_specs=out_specs, check_vma=False)
```

```python
import functools
import math

import jax
import jax.numpy as jnp
from jax import lax
from jax.experimental import pallas as pl
from jax.experimental.pallas import tpu as pltpu
from jax.sharding import PartitionSpec as P


UNROLL = 4


def grouped_slots(count, slots, visit):
    def body(g, carry):
        terms = []
        for j in range(UNROLL):
            t = g * UNROLL + j
            terms.append((t, t < count))
        visit(terms)
        return carry

    lax.fori_loop(0, (count + UNROLL - 1) // UNROLL, body, 0)


def clamp_tile(index, limit):
    return jnp.minimum(jnp.maximum(index, 0), limit - 1)


def forward_kernel(rows_ref, cols_ref, count_ref, vals_ref, panel_ref, out_ref):
    c = pl.program_id(0)
    slots = vals_ref.shape[1]
    row_tiles = out_ref.shape[0]

    @pl.when(c == 0)
    def _():
        out_ref[...] = jnp.zeros_like(out_ref)

    def visit(terms):
        parts = []
        for t, valid in terms:
            r = clamp_tile(rows_ref[c * slots + t], row_tiles)
            k = clamp_tile(cols_ref[c * slots + t], row_tiles)
            prod = jnp.dot(vals_ref[0, t], panel_ref[0, k], preferred_element_type=jnp.float32)
            parts.append((r, jnp.where(valid, prod, 0.0)))
        for r, prod in parts:
            out_ref[r] += prod

    grouped_slots(count_ref[c], slots, visit)


def backward_kernel(rows_ref, cols_ref, count_ref, vals_ref, grad_ref, out_ref):
    c = pl.program_id(0)
    slots = vals_ref.shape[1]
    row_tiles = grad_ref.shape[0]
    out_ref[...] = jnp.zeros_like(out_ref)

    def visit(terms):
        parts = []
        for t, valid in terms:
            r = clamp_tile(rows_ref[c * slots + t], row_tiles)
            k = clamp_tile(cols_ref[c * slots + t], row_tiles)
            prod = lax.dot_general(
                vals_ref[0, t], grad_ref[r], (((0,), (0,)), ((), ())), preferred_element_type=jnp.float32
            )
            parts.append((k, jnp.where(valid, prod, 0.0)))
        for k, prod in parts:
            out_ref[0, k] += prod

    grouped_slots(count_ref[c], slots, visit)


def tile_forward(rows, cols, count, vals, panels):
    n_src, slots, tile, _ = vals.shape
    row_tiles, width = panels.shape[1], panels.shape[3]
    grid_spec = pltpu.PrefetchScalarGridSpec(
        num_scalar_prefetch=3,
        grid=(n_src,),
        in_specs=[
            pl.BlockSpec((1, slots, tile, tile), lambda c, *_: (c, 0, 0, 0)),
            pl.BlockSpec((1, row_tiles, tile, width), lambda c, *_: (c, 0, 0, 0)),
        ],
        out_specs=pl.BlockSpec((row_tiles, tile, width), lambda c, *_: (0, 0, 0)),
    )
    flops = 2 * n_src * slots * tile * tile * width
    return pl.pallas_call(
        forward_kernel,
        out_shape=jax.ShapeDtypeStruct((row_tiles, tile, width), jnp.float32),
        grid_spec=grid_spec,
        cost_estimate=pl.CostEstimate(
            flops=flops, transcendentals=0, bytes_accessed=vals.size * 2 + panels.size * 2
        ),
    )(rows, cols, count, vals, panels)


def tile_backward(rows, cols, count, vals, grad_tiles):
    n_src, slots, tile, _ = vals.shape
    row_tiles, width = grad_tiles.shape[0], grad_tiles.shape[2]
    grid_spec = pltpu.PrefetchScalarGridSpec(
        num_scalar_prefetch=3,
        grid=(n_src,),
        in_specs=[
            pl.BlockSpec((1, slots, tile, tile), lambda c, *_: (c, 0, 0, 0)),
            pl.BlockSpec((row_tiles, tile, width), lambda c, *_: (0, 0, 0)),
        ],
        out_specs=pl.BlockSpec((1, row_tiles, tile, width), lambda c, *_: (c, 0, 0, 0)),
    )
    flops = 2 * n_src * slots * tile * tile * width
    return pl.pallas_call(
        backward_kernel,
        out_shape=jax.ShapeDtypeStruct((n_src, row_tiles, tile, width), jnp.float32),
        grid_spec=grid_spec,
        cost_estimate=pl.CostEstimate(
            flops=flops, transcendentals=0, bytes_accessed=vals.size * 2 + n_src * row_tiles * tile * width * 4
        ),
    )(rows, cols, count, vals, grad_tiles)


def local(
    feats,
    weight,
    cotangent,
    labels,
    tile_vals,
    tile_row,
    tile_col,
    tile_count,
    hub_vals,
    hub_col,
    hub_dest,
    hub_row,
):
    n_blocks = lax.axis_size("blk")
    n_groups = lax.axis_size("grp")
    my_group = lax.axis_index("grp")
    rows_dev = feats.shape[0]
    width = feats.shape[1]
    tile_size = tile_vals.shape[-1]
    row_tiles = rows_dev // tile_size
    hub_count = hub_vals.shape[2]
    capacity = max(2, hub_count // 4)
    highest = lax.Precision.HIGHEST
    dev_vals = tile_vals[0, 0]
    dev_rows = tile_row[0, 0].reshape(-1)
    dev_cols = tile_col[0, 0].reshape(-1)
    dev_count = tile_count[0, 0]
    tile_range = jnp.arange(row_tiles, dtype=jnp.int32)
    proj = jnp.dot(feats, weight, preferred_element_type=jnp.float32).astype(jnp.bfloat16)
    own_panel = proj.reshape(row_tiles, tile_size, width)

    panels = lax.all_gather(proj, "blk", axis=0, tiled=True)
    panels = panels.reshape(n_blocks, row_tiles, tile_size, width)
    agg_sum = tile_forward(dev_rows, dev_cols, dev_count, dev_vals, panels)

    dest_all = hub_dest[:, 0, :, 0]
    hub_rows_all = hub_row[:, 0, :]
    hub_range = jnp.arange(hub_count, dtype=jnp.int32)
    earlier = hub_range[None, :] < hub_range[:, None]
    same_dest = dest_all[:, :, None] == dest_all[:, None, :]
    rank_all = jnp.sum((same_dest & earlier[None, :, :]).astype(jnp.int32), axis=-1)
    my_dest = lax.dynamic_index_in_dim(dest_all, my_group, 0, keepdims=False)
    my_rank = lax.dynamic_index_in_dim(rank_all, my_group, 0, keepdims=False)
    slot_of = my_dest * capacity + my_rank
    send_place = (
        slot_of[:, None] == jnp.arange(n_groups * capacity, dtype=jnp.int32)[None, :]
    ).astype(jnp.float32)
    hub_tiles = hub_vals[0, 0]
    hub_cols = hub_col[0, 0]
    hub_src = jnp.take(own_panel, hub_cols, axis=0)
    hub_part = jnp.einsum("hij,hjf->hif", hub_tiles, hub_src, preferred_element_type=jnp.float32)
    send_buf = jnp.einsum("hs,hif->sif", send_place, hub_part, precision=highest)
    send_buf = send_buf.reshape(n_groups, capacity, tile_size, width)
    received = lax.all_to_all(send_buf, "grp", split_axis=0, concat_axis=0, tiled=True)
    chosen = (dest_all == my_group).astype(jnp.float32)
    slot_hot = (rank_all[..., None] == jnp.arange(capacity, dtype=jnp.int32)).astype(
        jnp.float32
    ) * chosen[..., None]
    row_hot = (hub_rows_all[..., None] == tile_range).astype(jnp.float32)
    routing = jnp.einsum("shc,shr->scr", slot_hot, row_hot, precision=highest)
    agg_sum = agg_sum + jnp.einsum("scr,scif->rif", routing, received, precision=highest)
    agg_rows = agg_sum.reshape(rows_dev, width)
    layer_out = jax.nn.silu(agg_rows).astype(jnp.bfloat16)
    sigmoid_z = jax.nn.sigmoid(agg_rows)
    slope = sigmoid_z * (1.0 + agg_rows * (1.0 - sigmoid_z))
    keep = (labels >= 0).astype(jnp.float32)[:, None]
    grad_agg = (cotangent.astype(jnp.float32) * keep * slope).astype(jnp.bfloat16)
    grad_tiles = grad_agg.reshape(row_tiles, tile_size, width)

    partials = tile_backward(dev_rows, dev_cols, dev_count, dev_vals, grad_tiles)
    grad_sum = lax.psum_scatter(partials, "blk", scatter_dimension=0, tiled=True)[0]

    back_send = jnp.einsum(
        "scr,rif->scif",
        routing.astype(jnp.bfloat16),
        grad_tiles,
        preferred_element_type=jnp.float32,
    ).astype(jnp.bfloat16)
    back_recv = lax.all_to_all(back_send, "grp", split_axis=0, concat_axis=0, tiled=True)
    back_flat = back_recv.reshape(n_groups * capacity, tile_size, width)
    own_pick = jnp.einsum(
        "hs,sif->hif",
        send_place.astype(jnp.bfloat16),
        back_flat,
        preferred_element_type=jnp.float32,
    ).astype(jnp.bfloat16)
    hub_back = jnp.einsum("hij,hif->hjf", hub_tiles, own_pick, preferred_element_type=jnp.float32)
    col_hot = (hub_cols[:, None] == tile_range[None, :]).astype(jnp.float32)
    grad_sum = grad_sum + jnp.einsum("hr,hjf->rjf", col_hot, hub_back, precision=highest)
    grad_rows = grad_sum.reshape(rows_dev, width).astype(jnp.bfloat16)
    weight_term = lax.dot_general(
        feats, grad_rows, (((0,), (0,)), ((), ())), preferred_element_type=jnp.float32
    )
    grad_scale = 1.0 / math.sqrt(rows_dev * n_blocks * n_groups)
    grad_weight = lax.psum(lax.psum(weight_term, "blk"), "grp") * grad_scale
    grad_feats = lax.dot_general(
        grad_rows, weight, (((1,), (1,)), ((), ())), preferred_element_type=jnp.float32
    ).astype(jnp.bfloat16)
    return (layer_out, grad_feats, grad_weight)


def solution(mesh):
    in_specs = (
        P(("grp", "blk"), None),
        P(),
        P(("grp", "blk"), None),
        P(("grp", "blk")),
        P("grp", "blk", None, None, None, None),
        P("grp", "blk", None, None),
        P("grp", "blk", None, None),
        P("grp", "blk", None),
        P("grp", "blk", None, None, None),
        P("grp", "blk", None),
        P(None, "blk", None, None),
        P(None, "blk", None),
    )
    out_specs = (P(("grp", "blk"), None), P(("grp", "blk"), None), P())
    return jax.shard_map(local, mesh=mesh, in_specs=in_specs, out_specs=out_specs, check_vma=False)
```

```python
import functools
import math

import jax
import jax.numpy as jnp
from jax import lax
from jax.experimental import pallas as pl
from jax.experimental.pallas import tpu as pltpu
from jax.sharding import PartitionSpec as P


UNROLL = 4


def grouped_slots(count, slots, visit):
    def body(g, carry):
        terms = []
        for j in range(UNROLL):
            t = g * UNROLL + j
            terms.append((t, t < count))
        visit(terms)
        return carry

    lax.fori_loop(0, (count + UNROLL - 1) // UNROLL, body, 0)


def clamp_tile(index, limit):
    return jnp.minimum(jnp.maximum(index, 0), limit - 1)


def forward_kernel(rows_ref, cols_ref, count_ref, vals_ref, panel_ref, out_ref):
    c = pl.program_id(0)
    slots = vals_ref.shape[1]
    row_tiles = out_ref.shape[0]

    @pl.when(c == 0)
    def _():
        out_ref[...] = jnp.zeros_like(out_ref)

    def visit(terms):
        parts = []
        for t, valid in terms:
            r = clamp_tile(rows_ref[c * slots + t], row_tiles)
            k = clamp_tile(cols_ref[c * slots + t], row_tiles)
            prod = jnp.dot(vals_ref[0, t], panel_ref[0, k], preferred_element_type=jnp.float32)
            parts.append((r, jnp.where(valid, prod, 0.0)))
        for r, prod in parts:
            out_ref[r] += prod

    grouped_slots(count_ref[c], slots, visit)


def backward_kernel(rows_ref, cols_ref, count_ref, vals_ref, grad_ref, out_ref):
    c = pl.program_id(0)
    slots = vals_ref.shape[1]
    row_tiles = grad_ref.shape[0]
    out_ref[...] = jnp.zeros_like(out_ref)

    def visit(terms):
        parts = []
        for t, valid in terms:
            r = clamp_tile(rows_ref[c * slots + t], row_tiles)
            k = clamp_tile(cols_ref[c * slots + t], row_tiles)
            prod = lax.dot_general(
                vals_ref[0, t], grad_ref[r], (((0,), (0,)), ((), ())), preferred_element_type=jnp.float32
            )
            parts.append((k, jnp.where(valid, prod, 0.0)))
        for k, prod in parts:
            out_ref[0, k] += prod

    grouped_slots(count_ref[c], slots, visit)


def tile_forward(rows, cols, count, vals, panels):
    n_src, slots, tile, _ = vals.shape
    row_tiles, width = panels.shape[1], panels.shape[3]
    grid_spec = pltpu.PrefetchScalarGridSpec(
        num_scalar_prefetch=3,
        grid=(n_src,),
        in_specs=[
            pl.BlockSpec((1, slots, tile, tile), lambda c, *_: (c, 0, 0, 0)),
            pl.BlockSpec((1, row_tiles, tile, width), lambda c, *_: (c, 0, 0, 0)),
        ],
        out_specs=pl.BlockSpec((row_tiles, tile, width), lambda c, *_: (0, 0, 0)),
    )
    flops = 2 * n_src * slots * tile * tile * width
    return pl.pallas_call(
        forward_kernel,
        out_shape=jax.ShapeDtypeStruct((row_tiles, tile, width), jnp.float32),
        grid_spec=grid_spec,
        cost_estimate=pl.CostEstimate(
            flops=flops, transcendentals=0, bytes_accessed=vals.size * 2 + panels.size * 2
        ),
    )(rows, cols, count, vals, panels)


def tile_backward(rows, cols, count, vals, grad_tiles):
    n_src, slots, tile, _ = vals.shape
    row_tiles, width = grad_tiles.shape[0], grad_tiles.shape[2]
    grid_spec = pltpu.PrefetchScalarGridSpec(
        num_scalar_prefetch=3,
        grid=(n_src,),
        in_specs=[
            pl.BlockSpec((1, slots, tile, tile), lambda c, *_: (c, 0, 0, 0)),
            pl.BlockSpec((row_tiles, tile, width), lambda c, *_: (0, 0, 0)),
        ],
        out_specs=pl.BlockSpec((1, row_tiles, tile, width), lambda c, *_: (c, 0, 0, 0)),
    )
    flops = 2 * n_src * slots * tile * tile * width
    return pl.pallas_call(
        backward_kernel,
        out_shape=jax.ShapeDtypeStruct((n_src, row_tiles, tile, width), jnp.float32),
        grid_spec=grid_spec,
        cost_estimate=pl.CostEstimate(
            flops=flops, transcendentals=0, bytes_accessed=vals.size * 2 + n_src * row_tiles * tile * width * 4
        ),
    )(rows, cols, count, vals, grad_tiles)

MESH_ID = pl.DeviceIdType.MESH


def weight_sum_kernel(n_grp, n_blk, x_ref, out_ref, part, grp_part, whole, sems):
    g = lax.axis_index("grp")
    b = lax.axis_index("blk")
    send1, recv1, send2, recv2, send3, recv3 = sems
    barrier = pltpu.get_barrier_semaphore()
    for i in range(1, n_blk):
        pl.semaphore_signal(barrier, 1, device_id=(g, (b + i) % n_blk), device_id_type=MESH_ID)
    for i in range(1, n_grp):
        pl.semaphore_signal(barrier, 1, device_id=((g + i) % n_grp, b), device_id_type=MESH_ID)
    pl.semaphore_wait(barrier, n_blk - 1 + n_grp - 1)

    def blk_copy(src, dst, send, recv, to, slot):
        return pltpu.make_async_remote_copy(
            src_ref=src, dst_ref=dst, send_sem=send.at[to], recv_sem=recv.at[slot],
            device_id=(g, to), device_id_type=MESH_ID,
        )

    def grp_copy(src, dst, send, recv, to, slot):
        return pltpu.make_async_remote_copy(
            src_ref=src, dst_ref=dst, send_sem=send.at[to], recv_sem=recv.at[slot],
            device_id=(to, b), device_id_type=MESH_ID,
        )

    out1 = []
    for i in range(1, n_blk):
        to = (b + i) % n_blk
        cp = blk_copy(x_ref.at[to], part.at[b], send1, recv1, to, b)
        cp.start()
        out1.append(cp)
    part[b] = x_ref[b]
    for i in range(1, n_blk):
        src = (b + n_blk - i) % n_blk
        blk_copy(x_ref.at[b], part.at[src], send1, recv1, src, src).wait_recv()
    for cp in out1:
        cp.wait_send()
    acc = part[0]
    for j in range(1, n_blk):
        acc = acc + part[j]
    grp_part[g] = acc

    out2 = []
    for i in range(1, n_grp):
        to = (g + i) % n_grp
        cp = grp_copy(grp_part.at[g], grp_part.at[g], send2, recv2, to, g)
        cp.start()
        out2.append(cp)
    for i in range(1, n_grp):
        src = (g + n_grp - i) % n_grp
        grp_copy(grp_part.at[src], grp_part.at[src], send2, recv2, src, src).wait_recv()
    for cp in out2:
        cp.wait_send()
    acc = grp_part[0]
    for j in range(1, n_grp):
        acc = acc + grp_part[j]
    whole[b] = acc

    out3 = []
    for i in range(1, n_blk):
        to = (b + i) % n_blk
        cp = blk_copy(whole.at[b], whole.at[b], send3, recv3, to, b)
        cp.start()
        out3.append(cp)
    for i in range(1, n_blk):
        src = (b + n_blk - i) % n_blk
        blk_copy(whole.at[src], whole.at[src], send3, recv3, src, src).wait_recv()
    for cp in out3:
        cp.wait_send()
    out_ref[...] = whole[...]


def weight_sum(term, n_grp, n_blk):
    rows, cols = term.shape
    chunk = rows * cols // (n_blk * 128)
    x = term.reshape(n_blk, chunk, 128)
    vmem = pl.BlockSpec(memory_space=pltpu.VMEM)
    out = pl.pallas_call(
        functools.partial(weight_sum_kernel, n_grp, n_blk),
        out_shape=jax.ShapeDtypeStruct(x.shape, jnp.float32),
        in_specs=[vmem],
        out_specs=vmem,
        scratch_shapes=[
            pltpu.VMEM(x.shape, jnp.float32),
            pltpu.VMEM((n_grp, chunk, 128), jnp.float32),
            pltpu.VMEM(x.shape, jnp.float32),
            [pltpu.SemaphoreType.DMA((n_blk,)), pltpu.SemaphoreType.DMA((n_blk,)),
             pltpu.SemaphoreType.DMA((n_grp,)), pltpu.SemaphoreType.DMA((n_grp,)),
             pltpu.SemaphoreType.DMA((n_blk,)), pltpu.SemaphoreType.DMA((n_blk,))],
        ],
        compiler_params=pltpu.CompilerParams(collective_id=0, has_side_effects=True),
    )(x)
    return out.reshape(rows, cols)


def local(
    feats,
    weight,
    cotangent,
    labels,
    tile_vals,
    tile_row,
    tile_col,
    tile_count,
    hub_vals,
    hub_col,
    hub_dest,
    hub_row,
):
    n_blocks = lax.axis_size("blk")
    n_groups = lax.axis_size("grp")
    my_group = lax.axis_index("grp")
    rows_dev = feats.shape[0]
    width = feats.shape[1]
    tile_size = tile_vals.shape[-1]
    row_tiles = rows_dev // tile_size
    hub_count = hub_vals.shape[2]
    capacity = max(2, hub_count // 4)
    highest = lax.Precision.HIGHEST
    dev_vals = tile_vals[0, 0]
    dev_rows = tile_row[0, 0].reshape(-1)
    dev_cols = tile_col[0, 0].reshape(-1)
    dev_count = tile_count[0, 0]
    tile_range = jnp.arange(row_tiles, dtype=jnp.int32)
    proj = jnp.dot(feats, weight, preferred_element_type=jnp.float32).astype(jnp.bfloat16)
    own_panel = proj.reshape(row_tiles, tile_size, width)

    panels = lax.all_gather(proj, "blk", axis=0, tiled=True)
    panels = panels.reshape(n_blocks, row_tiles, tile_size, width)
    agg_sum = tile_forward(dev_rows, dev_cols, dev_count, dev_vals, panels)

    dest_all = hub_dest[:, 0, :, 0]
    hub_rows_all = hub_row[:, 0, :]
    hub_range = jnp.arange(hub_count, dtype=jnp.int32)
    earlier = hub_range[None, :] < hub_range[:, None]
    same_dest = dest_all[:, :, None] == dest_all[:, None, :]
    rank_all = jnp.sum((same_dest & earlier[None, :, :]).astype(jnp.int32), axis=-1)
    my_dest = lax.dynamic_index_in_dim(dest_all, my_group, 0, keepdims=False)
    my_rank = lax.dynamic_index_in_dim(rank_all, my_group, 0, keepdims=False)
    slot_of = my_dest * capacity + my_rank
    send_place = (
        slot_of[:, None] == jnp.arange(n_groups * capacity, dtype=jnp.int32)[None, :]
    ).astype(jnp.float32)
    hub_tiles = hub_vals[0, 0]
    hub_cols = hub_col[0, 0]
    hub_src = jnp.take(own_panel, hub_cols, axis=0)
    hub_part = jnp.einsum("hij,hjf->hif", hub_tiles, hub_src, preferred_element_type=jnp.float32)
    send_buf = jnp.einsum("hs,hif->sif", send_place, hub_part, precision=highest)
    send_buf = send_buf.reshape(n_groups, capacity, tile_size, width)
    received = lax.all_to_all(send_buf, "grp", split_axis=0, concat_axis=0, tiled=True)
    chosen = (dest_all == my_group).astype(jnp.float32)
    slot_hot = (rank_all[..., None] == jnp.arange(capacity, dtype=jnp.int32)).astype(
        jnp.float32
    ) * chosen[..., None]
    row_hot = (hub_rows_all[..., None] == tile_range).astype(jnp.float32)
    routing = jnp.einsum("shc,shr->scr", slot_hot, row_hot, precision=highest)
    agg_sum = agg_sum + jnp.einsum("scr,scif->rif", routing, received, precision=highest)
    agg_rows = agg_sum.reshape(rows_dev, width)
    layer_out = jax.nn.silu(agg_rows).astype(jnp.bfloat16)
    sigmoid_z = jax.nn.sigmoid(agg_rows)
    slope = sigmoid_z * (1.0 + agg_rows * (1.0 - sigmoid_z))
    keep = (labels >= 0).astype(jnp.float32)[:, None]
    grad_agg = (cotangent.astype(jnp.float32) * keep * slope).astype(jnp.bfloat16)
    grad_tiles = grad_agg.reshape(row_tiles, tile_size, width)

    partials = tile_backward(dev_rows, dev_cols, dev_count, dev_vals, grad_tiles)
    grad_sum = lax.psum_scatter(partials, "blk", scatter_dimension=0, tiled=True)[0]

    back_send = jnp.einsum(
        "scr,rif->scif",
        routing.astype(jnp.bfloat16),
        grad_tiles,
        preferred_element_type=jnp.float32,
    ).astype(jnp.bfloat16)
    back_recv = lax.all_to_all(back_send, "grp", split_axis=0, concat_axis=0, tiled=True)
    back_flat = back_recv.reshape(n_groups * capacity, tile_size, width)
    own_pick = jnp.einsum(
        "hs,sif->hif",
        send_place.astype(jnp.bfloat16),
        back_flat,
        preferred_element_type=jnp.float32,
    ).astype(jnp.bfloat16)
    hub_back = jnp.einsum("hij,hif->hjf", hub_tiles, own_pick, preferred_element_type=jnp.float32)
    col_hot = (hub_cols[:, None] == tile_range[None, :]).astype(jnp.float32)
    grad_sum = grad_sum + jnp.einsum("hr,hjf->rjf", col_hot, hub_back, precision=highest)
    grad_rows = grad_sum.reshape(rows_dev, width).astype(jnp.bfloat16)
    weight_term = lax.dot_general(
        feats, grad_rows, (((0,), (0,)), ((), ())), preferred_element_type=jnp.float32
    )
    grad_scale = 1.0 / math.sqrt(rows_dev * n_blocks * n_groups)
    grad_weight = weight_sum(weight_term, n_groups, n_blocks) * grad_scale
    grad_feats = lax.dot_general(
        grad_rows, weight, (((1,), (1,)), ((), ())), preferred_element_type=jnp.float32
    ).astype(jnp.bfloat16)
    return (layer_out, grad_feats, grad_weight)


def solution(mesh):
    in_specs = (
        P(("grp", "blk"), None),
        P(),
        P(("grp", "blk"), None),
        P(("grp", "blk")),
        P("grp", "blk", None, None, None, None),
        P("grp", "blk", None, None),
        P("grp", "blk", None, None),
        P("grp", "blk", None),
        P("grp", "blk", None, None, None),
        P("grp", "blk", None),
        P(None, "blk", None, None),
        P(None, "blk", None),
    )
    out_specs = (P(("grp", "blk"), None), P(("grp", "blk"), None), P())
    return jax.shard_map(local, mesh=mesh, in_specs=in_specs, out_specs=out_specs, check_vma=False)
```

```python
import functools
import math

import jax
import jax.numpy as jnp
from jax import lax
from jax.experimental import pallas as pl
from jax.experimental.pallas import tpu as pltpu
from jax.sharding import PartitionSpec as P


UNROLL = 4


def grouped_slots(count, slots, visit):
    def body(g, carry):
        terms = []
        for j in range(UNROLL):
            t = g * UNROLL + j
            terms.append((t, t < count))
        visit(terms)
        return carry

    lax.fori_loop(0, (count + UNROLL - 1) // UNROLL, body, 0)


def clamp_tile(index, limit):
    return jnp.minimum(jnp.maximum(index, 0), limit - 1)


def forward_kernel(rows_ref, cols_ref, count_ref, vals_ref, panel_ref, out_ref):
    c = pl.program_id(0)
    slots = vals_ref.shape[1]
    row_tiles = out_ref.shape[0]

    @pl.when(c == 0)
    def _():
        out_ref[...] = jnp.zeros_like(out_ref)

    def visit(terms):
        parts = []
        for t, valid in terms:
            r = clamp_tile(rows_ref[c * slots + t], row_tiles)
            k = clamp_tile(cols_ref[c * slots + t], row_tiles)
            prod = jnp.dot(vals_ref[0, t], panel_ref[0, k], preferred_element_type=jnp.float32)
            parts.append((r, jnp.where(valid, prod, 0.0)))
        for r, prod in parts:
            out_ref[r] += prod

    grouped_slots(count_ref[c], slots, visit)


def backward_kernel(rows_ref, cols_ref, count_ref, vals_ref, grad_ref, out_ref, acc_ref):
    c = pl.program_id(0)
    slots = vals_ref.shape[1]
    row_tiles = grad_ref.shape[0]
    acc_ref[...] = jnp.zeros_like(acc_ref)

    def visit(terms):
        parts = []
        for t, valid in terms:
            r = clamp_tile(rows_ref[c * slots + t], row_tiles)
            k = clamp_tile(cols_ref[c * slots + t], row_tiles)
            prod = lax.dot_general(
                vals_ref[0, t], grad_ref[r], (((0,), (0,)), ((), ())), preferred_element_type=jnp.float32
            )
            parts.append((k, jnp.where(valid, prod, 0.0)))
        for k, prod in parts:
            acc_ref[k] += prod

    grouped_slots(count_ref[c], slots, visit)
    out_ref[0] = acc_ref[...].astype(out_ref.dtype)


def tile_forward(rows, cols, count, vals, panels):
    n_src, slots, tile, _ = vals.shape
    row_tiles, width = panels.shape[1], panels.shape[3]
    grid_spec = pltpu.PrefetchScalarGridSpec(
        num_scalar_prefetch=3,
        grid=(n_src,),
        in_specs=[
            pl.BlockSpec((1, slots, tile, tile), lambda c, *_: (c, 0, 0, 0)),
            pl.BlockSpec((1, row_tiles, tile, width), lambda c, *_: (c, 0, 0, 0)),
        ],
        out_specs=pl.BlockSpec((row_tiles, tile, width), lambda c, *_: (0, 0, 0)),
    )
    flops = 2 * n_src * slots * tile * tile * width
    return pl.pallas_call(
        forward_kernel,
        out_shape=jax.ShapeDtypeStruct((row_tiles, tile, width), jnp.float32),
        grid_spec=grid_spec,
        cost_estimate=pl.CostEstimate(
            flops=flops, transcendentals=0, bytes_accessed=vals.size * 2 + panels.size * 2
        ),
    )(rows, cols, count, vals, panels)


def tile_backward(rows, cols, count, vals, grad_tiles):
    n_src, slots, tile, _ = vals.shape
    row_tiles, width = grad_tiles.shape[0], grad_tiles.shape[2]
    grid_spec = pltpu.PrefetchScalarGridSpec(
        num_scalar_prefetch=3,
        grid=(n_src,),
        in_specs=[
            pl.BlockSpec((1, slots, tile, tile), lambda c, *_: (c, 0, 0, 0)),
            pl.BlockSpec((row_tiles, tile, width), lambda c, *_: (0, 0, 0)),
        ],
        out_specs=pl.BlockSpec((1, row_tiles, tile, width), lambda c, *_: (c, 0, 0, 0)),
        scratch_shapes=[pltpu.VMEM((row_tiles, tile, width), jnp.float32)],
    )
    flops = 2 * n_src * slots * tile * tile * width
    return pl.pallas_call(
        backward_kernel,
        out_shape=jax.ShapeDtypeStruct((n_src, row_tiles, tile, width), jnp.bfloat16),
        grid_spec=grid_spec,
        cost_estimate=pl.CostEstimate(
            flops=flops, transcendentals=0, bytes_accessed=vals.size * 2 + n_src * row_tiles * tile * width * 2
        ),
    )(rows, cols, count, vals, grad_tiles)


MESH_ID = pl.DeviceIdType.MESH


def weight_sum_kernel(n_grp, n_blk, x_ref, out_ref, part, grp_part, whole, sems):
    g = lax.axis_index("grp")
    b = lax.axis_index("blk")
    send1, recv1, send2, recv2, send3, recv3 = sems
    barrier = pltpu.get_barrier_semaphore()
    for i in range(1, n_blk):
        pl.semaphore_signal(barrier, 1, device_id=(g, (b + i) % n_blk), device_id_type=MESH_ID)
    for i in range(1, n_grp):
        pl.semaphore_signal(barrier, 1, device_id=((g + i) % n_grp, b), device_id_type=MESH_ID)
    pl.semaphore_wait(barrier, n_blk - 1 + n_grp - 1)

    def blk_copy(src, dst, send, recv, to, slot):
        return pltpu.make_async_remote_copy(
            src_ref=src, dst_ref=dst, send_sem=send.at[to], recv_sem=recv.at[slot],
            device_id=(g, to), device_id_type=MESH_ID,
        )

    def grp_copy(src, dst, send, recv, to, slot):
        return pltpu.make_async_remote_copy(
            src_ref=src, dst_ref=dst, send_sem=send.at[to], recv_sem=recv.at[slot],
            device_id=(to, b), device_id_type=MESH_ID,
        )

    out1 = []
    for i in range(1, n_blk):
        to = (b + i) % n_blk
        cp = blk_copy(x_ref.at[to], part.at[b], send1, recv1, to, b)
        cp.start()
        out1.append(cp)
    part[b] = x_ref[b]
    for i in range(1, n_blk):
        src = (b + n_blk - i) % n_blk
        blk_copy(x_ref.at[b], part.at[src], send1, recv1, src, src).wait_recv()
    for cp in out1:
        cp.wait_send()
    acc = part[0]
    for j in range(1, n_blk):
        acc = acc + part[j]
    grp_part[g] = acc

    out2 = []
    for i in range(1, n_grp):
        to = (g + i) % n_grp
        cp = grp_copy(grp_part.at[g], grp_part.at[g], send2, recv2, to, g)
        cp.start()
        out2.append(cp)
    for i in range(1, n_grp):
        src = (g + n_grp - i) % n_grp
        grp_copy(grp_part.at[src], grp_part.at[src], send2, recv2, src, src).wait_recv()
    for cp in out2:
        cp.wait_send()
    acc = grp_part[0]
    for j in range(1, n_grp):
        acc = acc + grp_part[j]
    whole[b] = acc

    out3 = []
    for i in range(1, n_blk):
        to = (b + i) % n_blk
        cp = blk_copy(whole.at[b], whole.at[b], send3, recv3, to, b)
        cp.start()
        out3.append(cp)
    for i in range(1, n_blk):
        src = (b + n_blk - i) % n_blk
        blk_copy(whole.at[src], whole.at[src], send3, recv3, src, src).wait_recv()
    for cp in out3:
        cp.wait_send()
    out_ref[...] = whole[...]


def weight_sum(term, n_grp, n_blk):
    rows, cols = term.shape
    chunk = rows * cols // (n_blk * 128)
    x = term.reshape(n_blk, chunk, 128)
    vmem = pl.BlockSpec(memory_space=pltpu.VMEM)
    out = pl.pallas_call(
        functools.partial(weight_sum_kernel, n_grp, n_blk),
        out_shape=jax.ShapeDtypeStruct(x.shape, jnp.float32),
        in_specs=[vmem],
        out_specs=vmem,
        scratch_shapes=[
            pltpu.VMEM(x.shape, jnp.float32),
            pltpu.VMEM((n_grp, chunk, 128), jnp.float32),
            pltpu.VMEM(x.shape, jnp.float32),
            [pltpu.SemaphoreType.DMA((n_blk,)), pltpu.SemaphoreType.DMA((n_blk,)),
             pltpu.SemaphoreType.DMA((n_grp,)), pltpu.SemaphoreType.DMA((n_grp,)),
             pltpu.SemaphoreType.DMA((n_blk,)), pltpu.SemaphoreType.DMA((n_blk,))],
        ],
        compiler_params=pltpu.CompilerParams(collective_id=0, has_side_effects=True),
    )(x)
    return out.reshape(rows, cols)


def exchange_kernel(n_blk, by_dest, src_ref, out_ref, send, recv, own):
    g = lax.axis_index("grp")
    b = lax.axis_index("blk")
    barrier = pltpu.get_barrier_semaphore()
    for i in range(1, n_blk):
        pl.semaphore_signal(barrier, 1, device_id=(g, (b + i) % n_blk), device_id_type=MESH_ID)
    pl.semaphore_wait(barrier, n_blk - 1)

    def piece(to):
        return src_ref.at[to] if by_dest else src_ref

    def remote(to, slot):
        return pltpu.make_async_remote_copy(
            src_ref=piece(to), dst_ref=out_ref.at[slot], send_sem=send.at[to], recv_sem=recv.at[slot],
            device_id=(g, to), device_id_type=MESH_ID,
        )

    local = pltpu.make_async_copy(piece(b), out_ref.at[b], own)
    local.start()
    sent = []
    for i in range(1, n_blk):
        cp = remote((b + i) % n_blk, b)
        cp.start()
        sent.append(cp)
    for i in range(1, n_blk):
        src = (b + n_blk - i) % n_blk
        remote(src, src).wait_recv()
    for cp in sent:
        cp.wait_send()
    local.wait()


def exchange(src, n_blk, by_dest, collective):
    shape = src.shape[1:] if by_dest else src.shape
    any_space = pl.BlockSpec(memory_space=pl.ANY)
    return pl.pallas_call(
        functools.partial(exchange_kernel, n_blk, by_dest),
        out_shape=jax.ShapeDtypeStruct((n_blk,) + shape, src.dtype),
        in_specs=[any_space],
        out_specs=any_space,
        scratch_shapes=[
            pltpu.SemaphoreType.DMA((n_blk,)),
            pltpu.SemaphoreType.DMA((n_blk,)),
            pltpu.SemaphoreType.DMA,
        ],
        compiler_params=pltpu.CompilerParams(collective_id=collective, has_side_effects=True),
    )(src)


def local(
    feats,
    weight,
    cotangent,
    labels,
    tile_vals,
    tile_row,
    tile_col,
    tile_count,
    hub_vals,
    hub_col,
    hub_dest,
    hub_row,
):
    n_blocks = lax.axis_size("blk")
    n_groups = lax.axis_size("grp")
    my_group = lax.axis_index("grp")
    rows_dev = feats.shape[0]
    width = feats.shape[1]
    tile_size = tile_vals.shape[-1]
    row_tiles = rows_dev // tile_size
    hub_count = hub_vals.shape[2]
    capacity = max(2, hub_count // 4)
    highest = lax.Precision.HIGHEST
    dev_vals = tile_vals[0, 0]
    dev_rows = tile_row[0, 0].reshape(-1)
    dev_cols = tile_col[0, 0].reshape(-1)
    dev_count = tile_count[0, 0]
    tile_range = jnp.arange(row_tiles, dtype=jnp.int32)
    proj = jnp.dot(feats, weight, preferred_element_type=jnp.float32).astype(jnp.bfloat16)
    own_panel = proj.reshape(row_tiles, tile_size, width)

    panels = exchange(own_panel, n_blocks, False, 1)
    agg_sum = tile_forward(dev_rows, dev_cols, dev_count, dev_vals, panels)

    dest_all = hub_dest[:, 0, :, 0]
    hub_rows_all = hub_row[:, 0, :]
    hub_range = jnp.arange(hub_count, dtype=jnp.int32)
    earlier = hub_range[None, :] < hub_range[:, None]
    same_dest = dest_all[:, :, None] == dest_all[:, None, :]
    rank_all = jnp.sum((same_dest & earlier[None, :, :]).astype(jnp.int32), axis=-1)
    my_dest = lax.dynamic_index_in_dim(dest_all, my_group, 0, keepdims=False)
    my_rank = lax.dynamic_index_in_dim(rank_all, my_group, 0, keepdims=False)
    slot_of = my_dest * capacity + my_rank
    send_place = (
        slot_of[:, None] == jnp.arange(n_groups * capacity, dtype=jnp.int32)[None, :]
    ).astype(jnp.float32)
    hub_tiles = hub_vals[0, 0]
    hub_cols = hub_col[0, 0]
    hub_src = jnp.take(own_panel, hub_cols, axis=0)
    hub_part = jnp.einsum("hij,hjf->hif", hub_tiles, hub_src, preferred_element_type=jnp.float32)
    send_buf = jnp.einsum("hs,hif->sif", send_place, hub_part, precision=highest)
    send_buf = send_buf.reshape(n_groups, capacity, tile_size, width)
    received = lax.all_to_all(send_buf, "grp", split_axis=0, concat_axis=0, tiled=True)
    chosen = (dest_all == my_group).astype(jnp.float32)
    slot_hot = (rank_all[..., None] == jnp.arange(capacity, dtype=jnp.int32)).astype(
        jnp.float32
    ) * chosen[..., None]
    row_hot = (hub_rows_all[..., None] == tile_range).astype(jnp.float32)
    routing = jnp.einsum("shc,shr->scr", slot_hot, row_hot, precision=highest)
    agg_sum = agg_sum + jnp.einsum("scr,scif->rif", routing, received, precision=highest)
    agg_rows = agg_sum.reshape(rows_dev, width)
    layer_out = jax.nn.silu(agg_rows).astype(jnp.bfloat16)
    sigmoid_z = jax.nn.sigmoid(agg_rows)
    slope = sigmoid_z * (1.0 + agg_rows * (1.0 - sigmoid_z))
    keep = (labels >= 0).astype(jnp.float32)[:, None]
    grad_agg = (cotangent.astype(jnp.float32) * keep * slope).astype(jnp.bfloat16)
    grad_tiles = grad_agg.reshape(row_tiles, tile_size, width)

    partials = tile_backward(dev_rows, dev_cols, dev_count, dev_vals, grad_tiles)
    received_parts = exchange(partials, n_blocks, True, 2)
    grad_sum = jnp.sum(received_parts.astype(jnp.float32), axis=0)

    back_send = jnp.einsum(
        "scr,rif->scif",
        routing.astype(jnp.bfloat16),
        grad_tiles,
        preferred_element_type=jnp.float32,
    ).astype(jnp.bfloat16)
    back_recv = lax.all_to_all(back_send, "grp", split_axis=0, concat_axis=0, tiled=True)
    back_flat = back_recv.reshape(n_groups * capacity, tile_size, width)
    own_pick = jnp.einsum(
        "hs,sif->hif",
        send_place.astype(jnp.bfloat16),
        back_flat,
        preferred_element_type=jnp.float32,
    ).astype(jnp.bfloat16)
    hub_back = jnp.einsum("hij,hif->hjf", hub_tiles, own_pick, preferred_element_type=jnp.float32)
    col_hot = (hub_cols[:, None] == tile_range[None, :]).astype(jnp.float32)
    grad_sum = grad_sum + jnp.einsum("hr,hjf->rjf", col_hot, hub_back, precision=highest)
    grad_rows = grad_sum.reshape(rows_dev, width).astype(jnp.bfloat16)
    weight_term = lax.dot_general(
        feats, grad_rows, (((0,), (0,)), ((), ())), preferred_element_type=jnp.float32
    )
    grad_scale = 1.0 / math.sqrt(rows_dev * n_blocks * n_groups)
    grad_weight = weight_sum(weight_term, n_groups, n_blocks) * grad_scale
    grad_feats = lax.dot_general(
        grad_rows, weight, (((1,), (1,)), ((), ())), preferred_element_type=jnp.float32
    ).astype(jnp.bfloat16)
    return (layer_out, grad_feats, grad_weight)


def solution(mesh):
    in_specs = (
        P(("grp", "blk"), None),
        P(),
        P(("grp", "blk"), None),
        P(("grp", "blk")),
        P("grp", "blk", None, None, None, None),
        P("grp", "blk", None, None),
        P("grp", "blk", None, None),
        P("grp", "blk", None),
        P("grp", "blk", None, None, None),
        P("grp", "blk", None),
        P(None, "blk", None, None),
        P(None, "blk", None),
    )
    out_specs = (P(("grp", "blk"), None), P(("grp", "blk"), None), P())
    return jax.shard_map(local, mesh=mesh, in_specs=in_specs, out_specs=out_specs, check_vma=False)
```

```python
import functools
import math

import jax
import jax.numpy as jnp
from jax import lax
from jax.experimental import pallas as pl
from jax.experimental.pallas import tpu as pltpu
from jax.sharding import PartitionSpec as P


UNROLL = 4


def grouped_slots(count, slots, visit):
    def body(g, carry):
        terms = []
        for j in range(UNROLL):
            t = g * UNROLL + j
            terms.append((t, t < count))
        visit(terms)
        return carry

    lax.fori_loop(0, (count + UNROLL - 1) // UNROLL, body, 0)


def clamp_tile(index, limit):
    return jnp.minimum(jnp.maximum(index, 0), limit - 1)


def forward_kernel(rows_ref, cols_ref, count_ref, vals_ref, panel_ref, out_ref):
    c = pl.program_id(0)
    slots = vals_ref.shape[1]
    row_tiles = out_ref.shape[0]

    @pl.when(c == 0)
    def _():
        out_ref[...] = jnp.zeros_like(out_ref)

    def visit(terms):
        parts = []
        for t, valid in terms:
            r = clamp_tile(rows_ref[c * slots + t], row_tiles)
            k = clamp_tile(cols_ref[c * slots + t], row_tiles)
            prod = jnp.dot(vals_ref[0, t], panel_ref[0, k], preferred_element_type=jnp.float32)
            parts.append((r, jnp.where(valid, prod, 0.0)))
        for r, prod in parts:
            out_ref[r] += prod

    grouped_slots(count_ref[c], slots, visit)


def backward_kernel(rows_ref, cols_ref, count_ref, vals_ref, grad_ref, out_ref, acc_ref):
    c = pl.program_id(0)
    slots = vals_ref.shape[1]
    row_tiles = grad_ref.shape[0]
    acc_ref[...] = jnp.zeros_like(acc_ref)

    def visit(terms):
        parts = []
        for t, valid in terms:
            r = clamp_tile(rows_ref[c * slots + t], row_tiles)
            k = clamp_tile(cols_ref[c * slots + t], row_tiles)
            prod = lax.dot_general(
                vals_ref[0, t], grad_ref[r], (((0,), (0,)), ((), ())), preferred_element_type=jnp.float32
            )
            parts.append((k, jnp.where(valid, prod, 0.0)))
        for k, prod in parts:
            acc_ref[k] += prod

    grouped_slots(count_ref[c], slots, visit)
    out_ref[0] = acc_ref[...].astype(out_ref.dtype)


def tile_forward(rows, cols, count, vals, panels):
    n_src, slots, tile, _ = vals.shape
    row_tiles, width = panels.shape[1], panels.shape[3]
    grid_spec = pltpu.PrefetchScalarGridSpec(
        num_scalar_prefetch=3,
        grid=(n_src,),
        in_specs=[
            pl.BlockSpec((1, slots, tile, tile), lambda c, *_: (c, 0, 0, 0)),
            pl.BlockSpec((1, row_tiles, tile, width), lambda c, *_: (c, 0, 0, 0)),
        ],
        out_specs=pl.BlockSpec((row_tiles, tile, width), lambda c, *_: (0, 0, 0)),
    )
    flops = 2 * n_src * slots * tile * tile * width
    return pl.pallas_call(
        forward_kernel,
        out_shape=jax.ShapeDtypeStruct((row_tiles, tile, width), jnp.float32),
        grid_spec=grid_spec,
        cost_estimate=pl.CostEstimate(
            flops=flops, transcendentals=0, bytes_accessed=vals.size * 2 + panels.size * 2
        ),
    )(rows, cols, count, vals, panels)


def tile_backward(rows, cols, count, vals, grad_tiles):
    n_src, slots, tile, _ = vals.shape
    row_tiles, width = grad_tiles.shape[0], grad_tiles.shape[2]
    grid_spec = pltpu.PrefetchScalarGridSpec(
        num_scalar_prefetch=3,
        grid=(n_src,),
        in_specs=[
            pl.BlockSpec((1, slots, tile, tile), lambda c, *_: (c, 0, 0, 0)),
            pl.BlockSpec((row_tiles, tile, width), lambda c, *_: (0, 0, 0)),
        ],
        out_specs=pl.BlockSpec((1, row_tiles, tile, width), lambda c, *_: (c, 0, 0, 0)),
        scratch_shapes=[pltpu.VMEM((row_tiles, tile, width), jnp.float32)],
    )
    flops = 2 * n_src * slots * tile * tile * width
    return pl.pallas_call(
        backward_kernel,
        out_shape=jax.ShapeDtypeStruct((n_src, row_tiles, tile, width), jnp.bfloat16),
        grid_spec=grid_spec,
        cost_estimate=pl.CostEstimate(
            flops=flops, transcendentals=0, bytes_accessed=vals.size * 2 + n_src * row_tiles * tile * width * 2
        ),
    )(rows, cols, count, vals, grad_tiles)


MESH_ID = pl.DeviceIdType.MESH


def weight_sum_kernel(n_grp, n_blk, x_ref, out_ref, part, grp_part, whole, sems):
    g = lax.axis_index("grp")
    b = lax.axis_index("blk")
    send1, recv1, send2, recv2, send3, recv3 = sems
    barrier = pltpu.get_barrier_semaphore()
    for i in range(1, n_blk):
        pl.semaphore_signal(barrier, 1, device_id=(g, (b + i) % n_blk), device_id_type=MESH_ID)
    for i in range(1, n_grp):
        pl.semaphore_signal(barrier, 1, device_id=((g + i) % n_grp, b), device_id_type=MESH_ID)
    pl.semaphore_wait(barrier, n_blk - 1 + n_grp - 1)

    def blk_copy(src, dst, send, recv, to, slot):
        return pltpu.make_async_remote_copy(
            src_ref=src, dst_ref=dst, send_sem=send.at[to], recv_sem=recv.at[slot],
            device_id=(g, to), device_id_type=MESH_ID,
        )

    def grp_copy(src, dst, send, recv, to, slot):
        return pltpu.make_async_remote_copy(
            src_ref=src, dst_ref=dst, send_sem=send.at[to], recv_sem=recv.at[slot],
            device_id=(to, b), device_id_type=MESH_ID,
        )

    out1 = []
    for i in range(1, n_blk):
        to = (b + i) % n_blk
        cp = blk_copy(x_ref.at[to], part.at[b], send1, recv1, to, b)
        cp.start()
        out1.append(cp)
    part[b] = x_ref[b]
    for i in range(1, n_blk):
        src = (b + n_blk - i) % n_blk
        blk_copy(x_ref.at[b], part.at[src], send1, recv1, src, src).wait_recv()
    for cp in out1:
        cp.wait_send()
    acc = part[0]
    for j in range(1, n_blk):
        acc = acc + part[j]
    grp_part[g] = acc

    out2 = []
    for i in range(1, n_grp):
        to = (g + i) % n_grp
        cp = grp_copy(grp_part.at[g], grp_part.at[g], send2, recv2, to, g)
        cp.start()
        out2.append(cp)
    for i in range(1, n_grp):
        src = (g + n_grp - i) % n_grp
        grp_copy(grp_part.at[src], grp_part.at[src], send2, recv2, src, src).wait_recv()
    for cp in out2:
        cp.wait_send()
    acc = grp_part[0]
    for j in range(1, n_grp):
        acc = acc + grp_part[j]
    whole[b] = acc

    out3 = []
    for i in range(1, n_blk):
        to = (b + i) % n_blk
        cp = blk_copy(whole.at[b], whole.at[b], send3, recv3, to, b)
        cp.start()
        out3.append(cp)
    for i in range(1, n_blk):
        src = (b + n_blk - i) % n_blk
        blk_copy(whole.at[src], whole.at[src], send3, recv3, src, src).wait_recv()
    for cp in out3:
        cp.wait_send()
    out_ref[...] = whole[...]


def weight_sum(term, n_grp, n_blk):
    rows, cols = term.shape
    chunk = rows * cols // (n_blk * 128)
    x = term.reshape(n_blk, chunk, 128)
    vmem = pl.BlockSpec(memory_space=pltpu.VMEM)
    out = pl.pallas_call(
        functools.partial(weight_sum_kernel, n_grp, n_blk),
        out_shape=jax.ShapeDtypeStruct(x.shape, jnp.float32),
        in_specs=[vmem],
        out_specs=vmem,
        scratch_shapes=[
            pltpu.VMEM(x.shape, jnp.float32),
            pltpu.VMEM((n_grp, chunk, 128), jnp.float32),
            pltpu.VMEM(x.shape, jnp.float32),
            [pltpu.SemaphoreType.DMA((n_blk,)), pltpu.SemaphoreType.DMA((n_blk,)),
             pltpu.SemaphoreType.DMA((n_grp,)), pltpu.SemaphoreType.DMA((n_grp,)),
             pltpu.SemaphoreType.DMA((n_blk,)), pltpu.SemaphoreType.DMA((n_blk,))],
        ],
        compiler_params=pltpu.CompilerParams(collective_id=0, has_side_effects=True),
    )(x)
    return out.reshape(rows, cols)


def exchange_kernel(n_blk, by_dest, src_ref, out_ref, send, recv, own):
    g = lax.axis_index("grp")
    b = lax.axis_index("blk")
    barrier = pltpu.get_barrier_semaphore()
    for i in range(1, n_blk):
        pl.semaphore_signal(barrier, 1, device_id=(g, (b + i) % n_blk), device_id_type=MESH_ID)
    pl.semaphore_wait(barrier, n_blk - 1)

    def piece(to):
        return src_ref.at[to] if by_dest else src_ref

    def remote(to, slot):
        return pltpu.make_async_remote_copy(
            src_ref=piece(to), dst_ref=out_ref.at[slot], send_sem=send.at[to], recv_sem=recv.at[slot],
            device_id=(g, to), device_id_type=MESH_ID,
        )

    local = pltpu.make_async_copy(piece(b), out_ref.at[b], own)
    local.start()
    sent = []
    for i in range(1, n_blk):
        cp = remote((b + i) % n_blk, b)
        cp.start()
        sent.append(cp)
    for i in range(1, n_blk):
        src = (b + n_blk - i) % n_blk
        remote(src, src).wait_recv()
    for cp in sent:
        cp.wait_send()
    local.wait()


def exchange(src, n_blk, by_dest, collective):
    shape = src.shape[1:] if by_dest else src.shape
    any_space = pl.BlockSpec(memory_space=pl.ANY)
    return pl.pallas_call(
        functools.partial(exchange_kernel, n_blk, by_dest),
        out_shape=jax.ShapeDtypeStruct((n_blk,) + shape, src.dtype),
        in_specs=[any_space],
        out_specs=any_space,
        scratch_shapes=[
            pltpu.SemaphoreType.DMA((n_blk,)),
            pltpu.SemaphoreType.DMA((n_blk,)),
            pltpu.SemaphoreType.DMA,
        ],
        compiler_params=pltpu.CompilerParams(collective_id=collective, has_side_effects=True),
    )(src)


def local(
    feats,
    weight,
    cotangent,
    labels,
    tile_vals,
    tile_row,
    tile_col,
    tile_count,
    hub_vals,
    hub_col,
    hub_dest,
    hub_row,
):
    n_blocks = lax.axis_size("blk")
    n_groups = lax.axis_size("grp")
    my_group = lax.axis_index("grp")
    rows_dev = feats.shape[0]
    width = feats.shape[1]
    tile_size = tile_vals.shape[-1]
    row_tiles = rows_dev // tile_size
    hub_count = hub_vals.shape[2]
    capacity = max(2, hub_count // 4)
    highest = lax.Precision.HIGHEST
    dev_vals = tile_vals[0, 0]
    dev_rows = tile_row[0, 0].reshape(-1)
    dev_cols = tile_col[0, 0].reshape(-1)
    dev_count = tile_count[0, 0]
    tile_range = jnp.arange(row_tiles, dtype=jnp.int32)
    proj = jnp.dot(feats, weight, preferred_element_type=jnp.float32).astype(jnp.bfloat16)
    own_panel = proj.reshape(row_tiles, tile_size, width)

    panels = lax.all_gather(proj, "blk", axis=0, tiled=True)
    panels = panels.reshape(n_blocks, row_tiles, tile_size, width)
    agg_sum = tile_forward(dev_rows, dev_cols, dev_count, dev_vals, panels)

    dest_all = hub_dest[:, 0, :, 0]
    hub_rows_all = hub_row[:, 0, :]
    hub_range = jnp.arange(hub_count, dtype=jnp.int32)
    earlier = hub_range[None, :] < hub_range[:, None]
    same_dest = dest_all[:, :, None] == dest_all[:, None, :]
    rank_all = jnp.sum((same_dest & earlier[None, :, :]).astype(jnp.int32), axis=-1)
    my_dest = lax.dynamic_index_in_dim(dest_all, my_group, 0, keepdims=False)
    my_rank = lax.dynamic_index_in_dim(rank_all, my_group, 0, keepdims=False)
    slot_of = my_dest * capacity + my_rank
    send_place = (
        slot_of[:, None] == jnp.arange(n_groups * capacity, dtype=jnp.int32)[None, :]
    ).astype(jnp.float32)
    hub_tiles = hub_vals[0, 0]
    hub_cols = hub_col[0, 0]
    hub_src = jnp.take(own_panel, hub_cols, axis=0)
    hub_part = jnp.einsum("hij,hjf->hif", hub_tiles, hub_src, preferred_element_type=jnp.float32)
    send_buf = jnp.einsum("hs,hif->sif", send_place, hub_part, precision=highest)
    send_buf = send_buf.reshape(n_groups, capacity, tile_size, width)
    received = lax.all_to_all(send_buf, "grp", split_axis=0, concat_axis=0, tiled=True)
    chosen = (dest_all == my_group).astype(jnp.float32)
    slot_hot = (rank_all[..., None] == jnp.arange(capacity, dtype=jnp.int32)).astype(
        jnp.float32
    ) * chosen[..., None]
    row_hot = (hub_rows_all[..., None] == tile_range).astype(jnp.float32)
    routing = jnp.einsum("shc,shr->scr", slot_hot, row_hot, precision=highest)
    agg_sum = agg_sum + jnp.einsum("scr,scif->rif", routing, received, precision=highest)
    agg_rows = agg_sum.reshape(rows_dev, width)
    layer_out = jax.nn.silu(agg_rows).astype(jnp.bfloat16)
    sigmoid_z = jax.nn.sigmoid(agg_rows)
    slope = sigmoid_z * (1.0 + agg_rows * (1.0 - sigmoid_z))
    keep = (labels >= 0).astype(jnp.float32)[:, None]
    grad_agg = (cotangent.astype(jnp.float32) * keep * slope).astype(jnp.bfloat16)
    grad_tiles = grad_agg.reshape(row_tiles, tile_size, width)

    partials = tile_backward(dev_rows, dev_cols, dev_count, dev_vals, grad_tiles)
    received_parts = lax.all_to_all(partials, "blk", split_axis=0, concat_axis=0, tiled=True)
    grad_sum = jnp.sum(received_parts.astype(jnp.float32), axis=0)

    back_send = jnp.einsum(
        "scr,rif->scif",
        routing.astype(jnp.bfloat16),
        grad_tiles,
        preferred_element_type=jnp.float32,
    ).astype(jnp.bfloat16)
    back_recv = lax.all_to_all(back_send, "grp", split_axis=0, concat_axis=0, tiled=True)
    back_flat = back_recv.reshape(n_groups * capacity, tile_size, width)
    own_pick = jnp.einsum(
        "hs,sif->hif",
        send_place.astype(jnp.bfloat16),
        back_flat,
        preferred_element_type=jnp.float32,
    ).astype(jnp.bfloat16)
    hub_back = jnp.einsum("hij,hif->hjf", hub_tiles, own_pick, preferred_element_type=jnp.float32)
    col_hot = (hub_cols[:, None] == tile_range[None, :]).astype(jnp.float32)
    grad_sum = grad_sum + jnp.einsum("hr,hjf->rjf", col_hot, hub_back, precision=highest)
    grad_rows = grad_sum.reshape(rows_dev, width).astype(jnp.bfloat16)
    weight_term = lax.dot_general(
        feats, grad_rows, (((0,), (0,)), ((), ())), preferred_element_type=jnp.float32
    )
    grad_scale = 1.0 / math.sqrt(rows_dev * n_blocks * n_groups)
    grad_weight = weight_sum(weight_term, n_groups, n_blocks) * grad_scale
    grad_feats = lax.dot_general(
        grad_rows, weight, (((1,), (1,)), ((), ())), preferred_element_type=jnp.float32
    ).astype(jnp.bfloat16)
    return (layer_out, grad_feats, grad_weight)


def solution(mesh):
    in_specs = (
        P(("grp", "blk"), None),
        P(),
        P(("grp", "blk"), None),
        P(("grp", "blk")),
        P("grp", "blk", None, None, None, None),
        P("grp", "blk", None, None),
        P("grp", "blk", None, None),
        P("grp", "blk", None),
        P("grp", "blk", None, None, None),
        P("grp", "blk", None),
        P(None, "blk", None, None),
        P(None, "blk", None),
    )
    out_specs = (P(("grp", "blk"), None), P(("grp", "blk"), None), P())
    return jax.shard_map(local, mesh=mesh, in_specs=in_specs, out_specs=out_specs, check_vma=False)
```

```python
import functools
import math

import jax
import jax.numpy as jnp
from jax import lax
from jax.experimental import pallas as pl
from jax.experimental.pallas import tpu as pltpu
from jax.sharding import PartitionSpec as P


UNROLL = 4


def grouped_slots(count, slots, visit):
    def body(g, carry):
        terms = []
        for j in range(UNROLL):
            t = g * UNROLL + j
            terms.append((t, t < count))
        visit(terms)
        return carry

    lax.fori_loop(0, (count + UNROLL - 1) // UNROLL, body, 0)


def clamp_tile(index, limit):
    return jnp.minimum(jnp.maximum(index, 0), limit - 1)


def forward_kernel(rows_ref, cols_ref, count_ref, vals_ref, panel_ref, out_ref):
    c = pl.program_id(0)
    slots = vals_ref.shape[1]
    row_tiles = out_ref.shape[0]

    @pl.when(c == 0)
    def _():
        out_ref[...] = jnp.zeros_like(out_ref)

    def visit(terms):
        parts = []
        for t, valid in terms:
            r = clamp_tile(rows_ref[c * slots + t], row_tiles)
            k = clamp_tile(cols_ref[c * slots + t], row_tiles)
            prod = jnp.dot(vals_ref[0, t], panel_ref[0, k], preferred_element_type=jnp.float32)
            parts.append((r, jnp.where(valid, prod, 0.0)))
        for r, prod in parts:
            out_ref[r] += prod

    grouped_slots(count_ref[c], slots, visit)


def backward_kernel(rows_ref, cols_ref, count_ref, core_ref, vals_ref, grad_ref, out_ref, acc_ref):
    c = pl.program_id(0)
    slots = vals_ref.shape[1]
    row_tiles = grad_ref.shape[0]
    acc_ref[...] = jnp.zeros_like(acc_ref)

    def visit(terms):
        parts = []
        for t, valid in terms:
            r = clamp_tile(rows_ref[c * slots + t], row_tiles)
            k = clamp_tile(cols_ref[c * slots + t], row_tiles)
            prod = lax.dot_general(
                vals_ref[0, t], grad_ref[r], (((0,), (0,)), ((), ())), preferred_element_type=jnp.float32
            )
            parts.append((k, jnp.where(valid, prod, 0.0)))
        for k, prod in parts:
            acc_ref[k] += prod

    grouped_slots(count_ref[c], slots, visit)
    out_ref[0, 0] = acc_ref[...].astype(out_ref.dtype)


def tile_forward(rows, cols, count, vals, panels):
    n_src, slots, tile, _ = vals.shape
    row_tiles, width = panels.shape[1], panels.shape[3]
    grid_spec = pltpu.PrefetchScalarGridSpec(
        num_scalar_prefetch=3,
        grid=(n_src,),
        in_specs=[
            pl.BlockSpec((1, slots, tile, tile), lambda c, *_: (c, 0, 0, 0)),
            pl.BlockSpec((1, row_tiles, tile, width), lambda c, *_: (c, 0, 0, 0)),
        ],
        out_specs=pl.BlockSpec((row_tiles, tile, width), lambda c, *_: (0, 0, 0)),
    )
    flops = 2 * n_src * slots * tile * tile * width
    return pl.pallas_call(
        forward_kernel,
        out_shape=jax.ShapeDtypeStruct((row_tiles, tile, width), jnp.float32),
        grid_spec=grid_spec,
        cost_estimate=pl.CostEstimate(
            flops=flops, transcendentals=0, bytes_accessed=vals.size * 2 + panels.size * 2
        ),
    )(rows, cols, count, vals, panels)


def tile_backward(rows, cols, count, vals, grad_tiles, core):
    n_src, slots, tile, _ = vals.shape
    row_tiles, width = grad_tiles.shape[0], grad_tiles.shape[2]
    grid_spec = pltpu.PrefetchScalarGridSpec(
        num_scalar_prefetch=4,
        grid=(n_src,),
        in_specs=[
            pl.BlockSpec((1, slots, tile, tile), lambda c, *_: (c, 0, 0, 0)),
            pl.BlockSpec((row_tiles, tile, width), lambda c, *_: (0, 0, 0)),
        ],
        out_specs=pl.BlockSpec(
            (1, 1, row_tiles, tile, width), lambda c, r, k, n, core_ref: ((c + core_ref[0]) % 2, c // 2, 0, 0, 0)
        ),
        scratch_shapes=[pltpu.VMEM((row_tiles, tile, width), jnp.float32)],
    )
    flops = 2 * n_src * slots * tile * tile * width
    return pl.pallas_call(
        backward_kernel,
        out_shape=jax.ShapeDtypeStruct((2, n_src // 2, row_tiles, tile, width), jnp.float32),
        grid_spec=grid_spec,
        cost_estimate=pl.CostEstimate(
            flops=flops, transcendentals=0, bytes_accessed=vals.size * 2 + n_src * row_tiles * tile * width * 4
        ),
    )(rows, cols, count, core, vals, grad_tiles)


MESH_ID = pl.DeviceIdType.MESH


def weight_sum_kernel(n_grp, n_blk, x_ref, out_ref, part, grp_part, whole, sems):
    g = lax.axis_index("grp")
    b = lax.axis_index("blk")
    send1, recv1, send2, recv2, send3, recv3 = sems
    barrier = pltpu.get_barrier_semaphore()
    for i in range(1, n_blk):
        pl.semaphore_signal(barrier, 1, device_id=(g, (b + i) % n_blk), device_id_type=MESH_ID)
    for i in range(1, n_grp):
        pl.semaphore_signal(barrier, 1, device_id=((g + i) % n_grp, b), device_id_type=MESH_ID)
    pl.semaphore_wait(barrier, n_blk - 1 + n_grp - 1)

    def blk_copy(src, dst, send, recv, to, slot):
        return pltpu.make_async_remote_copy(
            src_ref=src, dst_ref=dst, send_sem=send.at[to], recv_sem=recv.at[slot],
            device_id=(g, to), device_id_type=MESH_ID,
        )

    def grp_copy(src, dst, send, recv, to, slot):
        return pltpu.make_async_remote_copy(
            src_ref=src, dst_ref=dst, send_sem=send.at[to], recv_sem=recv.at[slot],
            device_id=(to, b), device_id_type=MESH_ID,
        )

    out1 = []
    for i in range(1, n_blk):
        to = (b + i) % n_blk
        cp = blk_copy(x_ref.at[to], part.at[b], send1, recv1, to, b)
        cp.start()
        out1.append(cp)
    part[b] = x_ref[b]
    for i in range(1, n_blk):
        src = (b + n_blk - i) % n_blk
        blk_copy(x_ref.at[b], part.at[src], send1, recv1, src, src).wait_recv()
    for cp in out1:
        cp.wait_send()
    acc = part[0]
    for j in range(1, n_blk):
        acc = acc + part[j]
    grp_part[g] = acc

    out2 = []
    for i in range(1, n_grp):
        to = (g + i) % n_grp
        cp = grp_copy(grp_part.at[g], grp_part.at[g], send2, recv2, to, g)
        cp.start()
        out2.append(cp)
    for i in range(1, n_grp):
        src = (g + n_grp - i) % n_grp
        grp_copy(grp_part.at[src], grp_part.at[src], send2, recv2, src, src).wait_recv()
    for cp in out2:
        cp.wait_send()
    acc = grp_part[0]
    for j in range(1, n_grp):
        acc = acc + grp_part[j]
    whole[b] = acc

    out3 = []
    for i in range(1, n_blk):
        to = (b + i) % n_blk
        cp = blk_copy(whole.at[b], whole.at[b], send3, recv3, to, b)
        cp.start()
        out3.append(cp)
    for i in range(1, n_blk):
        src = (b + n_blk - i) % n_blk
        blk_copy(whole.at[src], whole.at[src], send3, recv3, src, src).wait_recv()
    for cp in out3:
        cp.wait_send()
    out_ref[...] = whole[...]


def weight_sum(term, n_grp, n_blk):
    rows, cols = term.shape
    chunk = rows * cols // (n_blk * 128)
    x = term.reshape(n_blk, chunk, 128)
    vmem = pl.BlockSpec(memory_space=pltpu.VMEM)
    out = pl.pallas_call(
        functools.partial(weight_sum_kernel, n_grp, n_blk),
        out_shape=jax.ShapeDtypeStruct(x.shape, jnp.float32),
        in_specs=[vmem],
        out_specs=vmem,
        scratch_shapes=[
            pltpu.VMEM(x.shape, jnp.float32),
            pltpu.VMEM((n_grp, chunk, 128), jnp.float32),
            pltpu.VMEM(x.shape, jnp.float32),
            [pltpu.SemaphoreType.DMA((n_blk,)), pltpu.SemaphoreType.DMA((n_blk,)),
             pltpu.SemaphoreType.DMA((n_grp,)), pltpu.SemaphoreType.DMA((n_grp,)),
             pltpu.SemaphoreType.DMA((n_blk,)), pltpu.SemaphoreType.DMA((n_blk,))],
        ],
        compiler_params=pltpu.CompilerParams(collective_id=0, has_side_effects=True),
    )(x)
    return out.reshape(rows, cols)


def exchange_kernel(n_blk, by_dest, src_ref, out_ref, send, recv, own):
    g = lax.axis_index("grp")
    b = lax.axis_index("blk")
    barrier = pltpu.get_barrier_semaphore()
    for i in range(1, n_blk):
        pl.semaphore_signal(barrier, 1, device_id=(g, (b + i) % n_blk), device_id_type=MESH_ID)
    pl.semaphore_wait(barrier, n_blk - 1)

    def piece(to):
        return src_ref.at[to] if by_dest else src_ref

    def remote(to, slot):
        return pltpu.make_async_remote_copy(
            src_ref=piece(to), dst_ref=out_ref.at[slot], send_sem=send.at[to], recv_sem=recv.at[slot],
            device_id=(g, to), device_id_type=MESH_ID,
        )

    local = pltpu.make_async_copy(piece(b), out_ref.at[b], own)
    local.start()
    sent = []
    for i in range(1, n_blk):
        cp = remote((b + i) % n_blk, b)
        cp.start()
        sent.append(cp)
    for i in range(1, n_blk):
        src = (b + n_blk - i) % n_blk
        remote(src, src).wait_recv()
    for cp in sent:
        cp.wait_send()
    local.wait()


def exchange(src, n_blk, by_dest, collective):
    shape = src.shape[1:] if by_dest else src.shape
    any_space = pl.BlockSpec(memory_space=pl.ANY)
    return pl.pallas_call(
        functools.partial(exchange_kernel, n_blk, by_dest),
        out_shape=jax.ShapeDtypeStruct((n_blk,) + shape, src.dtype),
        in_specs=[any_space],
        out_specs=any_space,
        scratch_shapes=[
            pltpu.SemaphoreType.DMA((n_blk,)),
            pltpu.SemaphoreType.DMA((n_blk,)),
            pltpu.SemaphoreType.DMA,
        ],
        compiler_params=pltpu.CompilerParams(collective_id=collective, has_side_effects=True),
    )(src)


def local(
    feats,
    weight,
    cotangent,
    labels,
    tile_vals,
    tile_row,
    tile_col,
    tile_count,
    hub_vals,
    hub_col,
    hub_dest,
    hub_row,
):
    n_blocks = lax.axis_size("blk")
    n_groups = lax.axis_size("grp")
    my_group = lax.axis_index("grp")
    rows_dev = feats.shape[0]
    width = feats.shape[1]
    tile_size = tile_vals.shape[-1]
    row_tiles = rows_dev // tile_size
    hub_count = hub_vals.shape[2]
    capacity = max(2, hub_count // 4)
    highest = lax.Precision.HIGHEST
    dev_vals = tile_vals[0, 0]
    dev_rows = tile_row[0, 0].reshape(-1)
    dev_cols = tile_col[0, 0].reshape(-1)
    dev_count = tile_count[0, 0]
    tile_range = jnp.arange(row_tiles, dtype=jnp.int32)
    proj = jnp.dot(feats, weight, preferred_element_type=jnp.float32).astype(jnp.bfloat16)
    own_panel = proj.reshape(row_tiles, tile_size, width)

    core = lax.axis_index("blk") % 2
    core_groups = [[i for i in range(n_blocks) if i % 2 == k] for k in range(2)]
    sibling = [(i, i ^ 1) for i in range(n_blocks)]
    half = lax.all_gather(own_panel, "blk", axis=0, tiled=False, axis_index_groups=core_groups)
    other = lax.ppermute(half, "blk", sibling)
    pair = jnp.where(core == 0, jnp.stack([half, other], 1), jnp.stack([other, half], 1))
    panels = pair.reshape(n_blocks, row_tiles, tile_size, width)
    agg_sum = tile_forward(dev_rows, dev_cols, dev_count, dev_vals, panels)

    dest_all = hub_dest[:, 0, :, 0]
    hub_rows_all = hub_row[:, 0, :]
    hub_range = jnp.arange(hub_count, dtype=jnp.int32)
    earlier = hub_range[None, :] < hub_range[:, None]
    same_dest = dest_all[:, :, None] == dest_all[:, None, :]
    rank_all = jnp.sum((same_dest & earlier[None, :, :]).astype(jnp.int32), axis=-1)
    my_dest = lax.dynamic_index_in_dim(dest_all, my_group, 0, keepdims=False)
    my_rank = lax.dynamic_index_in_dim(rank_all, my_group, 0, keepdims=False)
    slot_of = my_dest * capacity + my_rank
    send_place = (
        slot_of[:, None] == jnp.arange(n_groups * capacity, dtype=jnp.int32)[None, :]
    ).astype(jnp.float32)
    hub_tiles = hub_vals[0, 0]
    hub_cols = hub_col[0, 0]
    hub_src = jnp.take(own_panel, hub_cols, axis=0)
    hub_part = jnp.einsum("hij,hjf->hif", hub_tiles, hub_src, preferred_element_type=jnp.float32)
    send_buf = jnp.einsum("hs,hif->sif", send_place, hub_part, precision=highest)
    send_buf = send_buf.reshape(n_groups, capacity, tile_size, width)
    received = lax.all_to_all(send_buf, "grp", split_axis=0, concat_axis=0, tiled=True)
    chosen = (dest_all == my_group).astype(jnp.float32)
    slot_hot = (rank_all[..., None] == jnp.arange(capacity, dtype=jnp.int32)).astype(
        jnp.float32
    ) * chosen[..., None]
    row_hot = (hub_rows_all[..., None] == tile_range).astype(jnp.float32)
    routing = jnp.einsum("shc,shr->scr", slot_hot, row_hot, precision=highest)
    agg_sum = agg_sum + jnp.einsum("scr,scif->rif", routing, received, precision=highest)
    agg_rows = agg_sum.reshape(rows_dev, width)
    layer_out = jax.nn.silu(agg_rows).astype(jnp.bfloat16)
    sigmoid_z = jax.nn.sigmoid(agg_rows)
    slope = sigmoid_z * (1.0 + agg_rows * (1.0 - sigmoid_z))
    keep = (labels >= 0).astype(jnp.float32)[:, None]
    grad_agg = (cotangent.astype(jnp.float32) * keep * slope).astype(jnp.bfloat16)
    grad_tiles = grad_agg.reshape(row_tiles, tile_size, width)

    partials = tile_backward(dev_rows, dev_cols, dev_count, dev_vals, grad_tiles, core.reshape(1))
    from_sibling = lax.ppermute(partials[1], "blk", sibling)
    pair_sum = (partials[0] + from_sibling).astype(jnp.bfloat16)
    received_parts = lax.all_to_all(
        pair_sum, "blk", split_axis=0, concat_axis=0, tiled=True, axis_index_groups=core_groups
    )
    grad_sum = jnp.sum(received_parts.astype(jnp.float32), axis=0)

    back_send = jnp.einsum(
        "scr,rif->scif",
        routing.astype(jnp.bfloat16),
        grad_tiles,
        preferred_element_type=jnp.float32,
    ).astype(jnp.bfloat16)
    back_recv = lax.all_to_all(back_send, "grp", split_axis=0, concat_axis=0, tiled=True)
    back_flat = back_recv.reshape(n_groups * capacity, tile_size, width)
    own_pick = jnp.einsum(
        "hs,sif->hif",
        send_place.astype(jnp.bfloat16),
        back_flat,
        preferred_element_type=jnp.float32,
    ).astype(jnp.bfloat16)
    hub_back = jnp.einsum("hij,hif->hjf", hub_tiles, own_pick, preferred_element_type=jnp.float32)
    col_hot = (hub_cols[:, None] == tile_range[None, :]).astype(jnp.float32)
    grad_sum = grad_sum + jnp.einsum("hr,hjf->rjf", col_hot, hub_back, precision=highest)
    grad_rows = grad_sum.reshape(rows_dev, width).astype(jnp.bfloat16)
    weight_term = lax.dot_general(
        feats, grad_rows, (((0,), (0,)), ((), ())), preferred_element_type=jnp.float32
    )
    grad_scale = 1.0 / math.sqrt(rows_dev * n_blocks * n_groups)
    grad_weight = weight_sum(weight_term, n_groups, n_blocks) * grad_scale
    grad_feats = lax.dot_general(
        grad_rows, weight, (((1,), (1,)), ((), ())), preferred_element_type=jnp.float32
    ).astype(jnp.bfloat16)
    return (layer_out, grad_feats, grad_weight)


def solution(mesh):
    in_specs = (
        P(("grp", "blk"), None),
        P(),
        P(("grp", "blk"), None),
        P(("grp", "blk")),
        P("grp", "blk", None, None, None, None),
        P("grp", "blk", None, None),
        P("grp", "blk", None, None),
        P("grp", "blk", None),
        P("grp", "blk", None, None, None),
        P("grp", "blk", None),
        P(None, "blk", None, None),
        P(None, "blk", None),
    )
    out_specs = (P(("grp", "blk"), None), P(("grp", "blk"), None), P())
    return jax.shard_map(local, mesh=mesh, in_specs=in_specs, out_specs=out_specs, check_vma=False)
```

```python
import functools
import math

import jax
import jax.numpy as jnp
from jax import lax
from jax.experimental import pallas as pl
from jax.experimental.pallas import tpu as pltpu
from jax.sharding import PartitionSpec as P


UNROLL = 4


def grouped_slots(count, slots, visit):
    def body(g, carry):
        terms = []
        for j in range(UNROLL):
            t = g * UNROLL + j
            terms.append((t, t < count))
        visit(terms)
        return carry

    lax.fori_loop(0, (count + UNROLL - 1) // UNROLL, body, 0)


def clamp_tile(index, limit):
    return jnp.minimum(jnp.maximum(index, 0), limit - 1)


def forward_kernel(rows_ref, cols_ref, count_ref, vals_ref, panel_ref, out_ref):
    c = pl.program_id(0)
    slots = vals_ref.shape[1]
    row_tiles = out_ref.shape[0]

    @pl.when(c == 0)
    def _():
        out_ref[...] = jnp.zeros_like(out_ref)

    def visit(terms):
        parts = []
        for t, valid in terms:
            r = clamp_tile(rows_ref[c * slots + t], row_tiles)
            k = clamp_tile(cols_ref[c * slots + t], row_tiles)
            prod = jnp.dot(vals_ref[0, t], panel_ref[0, k], preferred_element_type=jnp.float32)
            parts.append((r, jnp.where(valid, prod, 0.0)))
        for r, prod in parts:
            out_ref[r] += prod

    grouped_slots(count_ref[c], slots, visit)


def backward_kernel(rows_ref, cols_ref, count_ref, core_ref, vals_ref, grad_ref, keep_ref, send_ref, acc_ref):
    i = pl.program_id(0)
    half = pl.num_programs(0) // 2
    p = i // half
    c = 2 * (i % half) + (p + core_ref[0]) % 2
    slots = vals_ref.shape[1]
    row_tiles = grad_ref.shape[0]
    acc_ref[...] = jnp.zeros_like(acc_ref)

    def visit(terms):
        parts = []
        for t, valid in terms:
            r = clamp_tile(rows_ref[c * slots + t], row_tiles)
            k = clamp_tile(cols_ref[c * slots + t], row_tiles)
            prod = lax.dot_general(
                vals_ref[0, t], grad_ref[r], (((0,), (0,)), ((), ())), preferred_element_type=jnp.float32
            )
            parts.append((k, jnp.where(valid, prod, 0.0)))
        for k, prod in parts:
            acc_ref[k] += prod

    grouped_slots(count_ref[c], slots, visit)

    @pl.when(p == 0)
    def _():
        keep_ref[0] = acc_ref[...]

    @pl.when(p == 1)
    def _():
        send_ref[0] = acc_ref[...]


def tile_forward(rows, cols, count, vals, panels):
    n_src, slots, tile, _ = vals.shape
    row_tiles, width = panels.shape[1], panels.shape[3]
    grid_spec = pltpu.PrefetchScalarGridSpec(
        num_scalar_prefetch=3,
        grid=(n_src,),
        in_specs=[
            pl.BlockSpec((1, slots, tile, tile), lambda c, *_: (c, 0, 0, 0)),
            pl.BlockSpec((1, row_tiles, tile, width), lambda c, *_: (c, 0, 0, 0)),
        ],
        out_specs=pl.BlockSpec((row_tiles, tile, width), lambda c, *_: (0, 0, 0)),
    )
    flops = 2 * n_src * slots * tile * tile * width
    return pl.pallas_call(
        forward_kernel,
        out_shape=jax.ShapeDtypeStruct((row_tiles, tile, width), jnp.float32),
        grid_spec=grid_spec,
        cost_estimate=pl.CostEstimate(
            flops=flops, transcendentals=0, bytes_accessed=vals.size * 2 + panels.size * 2
        ),
    )(rows, cols, count, vals, panels)


def tile_backward(rows, cols, count, vals, grad_tiles, core):
    n_src, slots, tile, _ = vals.shape
    row_tiles, width = grad_tiles.shape[0], grad_tiles.shape[2]
    half = n_src // 2

    def source(i, core_ref):
        return 2 * (i % half) + (i // half + core_ref[0]) % 2

    grid_spec = pltpu.PrefetchScalarGridSpec(
        num_scalar_prefetch=4,
        grid=(n_src,),
        in_specs=[
            pl.BlockSpec((1, slots, tile, tile), lambda i, r, k, n, core_ref: (source(i, core_ref), 0, 0, 0)),
            pl.BlockSpec((row_tiles, tile, width), lambda i, *_: (0, 0, 0)),
        ],
        out_specs=[
            pl.BlockSpec((1, row_tiles, tile, width), lambda i, *_: (jnp.minimum(i, half - 1), 0, 0, 0)),
            pl.BlockSpec((1, row_tiles, tile, width), lambda i, *_: (jnp.maximum(i - half, 0), 0, 0, 0)),
        ],
        scratch_shapes=[pltpu.VMEM((row_tiles, tile, width), jnp.float32)],
    )
    flops = 2 * n_src * slots * tile * tile * width
    part = jax.ShapeDtypeStruct((half, row_tiles, tile, width), jnp.float32)
    return pl.pallas_call(
        backward_kernel,
        out_shape=(part, part),
        grid_spec=grid_spec,
        cost_estimate=pl.CostEstimate(
            flops=flops, transcendentals=0, bytes_accessed=vals.size * 2 + n_src * row_tiles * tile * width * 4
        ),
    )(rows, cols, count, core, vals, grad_tiles)


MESH_ID = pl.DeviceIdType.MESH


def weight_sum_kernel(n_grp, n_blk, x_ref, out_ref, part, grp_part, whole, sems):
    g = lax.axis_index("grp")
    b = lax.axis_index("blk")
    send1, recv1, send2, recv2, send3, recv3 = sems
    barrier = pltpu.get_barrier_semaphore()
    for i in range(1, n_blk):
        pl.semaphore_signal(barrier, 1, device_id=(g, (b + i) % n_blk), device_id_type=MESH_ID)
    for i in range(1, n_grp):
        pl.semaphore_signal(barrier, 1, device_id=((g + i) % n_grp, b), device_id_type=MESH_ID)
    pl.semaphore_wait(barrier, n_blk - 1 + n_grp - 1)

    def blk_copy(src, dst, send, recv, to, slot):
        return pltpu.make_async_remote_copy(
            src_ref=src, dst_ref=dst, send_sem=send.at[to], recv_sem=recv.at[slot],
            device_id=(g, to), device_id_type=MESH_ID,
        )

    def grp_copy(src, dst, send, recv, to, slot):
        return pltpu.make_async_remote_copy(
            src_ref=src, dst_ref=dst, send_sem=send.at[to], recv_sem=recv.at[slot],
            device_id=(to, b), device_id_type=MESH_ID,
        )

    out1 = []
    for i in range(1, n_blk):
        to = (b + i) % n_blk
        cp = blk_copy(x_ref.at[to], part.at[b], send1, recv1, to, b)
        cp.start()
        out1.append(cp)
    part[b] = x_ref[b]
    for i in range(1, n_blk):
        src = (b + n_blk - i) % n_blk
        blk_copy(x_ref.at[b], part.at[src], send1, recv1, src, src).wait_recv()
    for cp in out1:
        cp.wait_send()
    acc = part[0]
    for j in range(1, n_blk):
        acc = acc + part[j]
    grp_part[g] = acc

    out2 = []
    for i in range(1, n_grp):
        to = (g + i) % n_grp
        cp = grp_copy(grp_part.at[g], grp_part.at[g], send2, recv2, to, g)
        cp.start()
        out2.append(cp)
    for i in range(1, n_grp):
        src = (g + n_grp - i) % n_grp
        grp_copy(grp_part.at[src], grp_part.at[src], send2, recv2, src, src).wait_recv()
    for cp in out2:
        cp.wait_send()
    acc = grp_part[0]
    for j in range(1, n_grp):
        acc = acc + grp_part[j]
    whole[b] = acc

    out3 = []
    for i in range(1, n_blk):
        to = (b + i) % n_blk
        cp = blk_copy(whole.at[b], whole.at[b], send3, recv3, to, b)
        cp.start()
        out3.append(cp)
    for i in range(1, n_blk):
        src = (b + n_blk - i) % n_blk
        blk_copy(whole.at[src], whole.at[src], send3, recv3, src, src).wait_recv()
    for cp in out3:
        cp.wait_send()
    out_ref[...] = whole[...]


def weight_sum(term, n_grp, n_blk):
    rows, cols = term.shape
    chunk = rows * cols // (n_blk * 128)
    x = term.reshape(n_blk, chunk, 128)
    vmem = pl.BlockSpec(memory_space=pltpu.VMEM)
    out = pl.pallas_call(
        functools.partial(weight_sum_kernel, n_grp, n_blk),
        out_shape=jax.ShapeDtypeStruct(x.shape, jnp.float32),
        in_specs=[vmem],
        out_specs=vmem,
        scratch_shapes=[
            pltpu.VMEM(x.shape, jnp.float32),
            pltpu.VMEM((n_grp, chunk, 128), jnp.float32),
            pltpu.VMEM(x.shape, jnp.float32),
            [pltpu.SemaphoreType.DMA((n_blk,)), pltpu.SemaphoreType.DMA((n_blk,)),
             pltpu.SemaphoreType.DMA((n_grp,)), pltpu.SemaphoreType.DMA((n_grp,)),
             pltpu.SemaphoreType.DMA((n_blk,)), pltpu.SemaphoreType.DMA((n_blk,))],
        ],
        compiler_params=pltpu.CompilerParams(collective_id=0, has_side_effects=True),
    )(x)
    return out.reshape(rows, cols)


def exchange_kernel(n_blk, by_dest, src_ref, out_ref, send, recv, own):
    g = lax.axis_index("grp")
    b = lax.axis_index("blk")
    barrier = pltpu.get_barrier_semaphore()
    for i in range(1, n_blk):
        pl.semaphore_signal(barrier, 1, device_id=(g, (b + i) % n_blk), device_id_type=MESH_ID)
    pl.semaphore_wait(barrier, n_blk - 1)

    def piece(to):
        return src_ref.at[to] if by_dest else src_ref

    def remote(to, slot):
        return pltpu.make_async_remote_copy(
            src_ref=piece(to), dst_ref=out_ref.at[slot], send_sem=send.at[to], recv_sem=recv.at[slot],
            device_id=(g, to), device_id_type=MESH_ID,
        )

    local = pltpu.make_async_copy(piece(b), out_ref.at[b], own)
    local.start()
    sent = []
    for i in range(1, n_blk):
        cp = remote((b + i) % n_blk, b)
        cp.start()
        sent.append(cp)
    for i in range(1, n_blk):
        src = (b + n_blk - i) % n_blk
        remote(src, src).wait_recv()
    for cp in sent:
        cp.wait_send()
    local.wait()


def exchange(src, n_blk, by_dest, collective):
    shape = src.shape[1:] if by_dest else src.shape
    any_space = pl.BlockSpec(memory_space=pl.ANY)
    return pl.pallas_call(
        functools.partial(exchange_kernel, n_blk, by_dest),
        out_shape=jax.ShapeDtypeStruct((n_blk,) + shape, src.dtype),
        in_specs=[any_space],
        out_specs=any_space,
        scratch_shapes=[
            pltpu.SemaphoreType.DMA((n_blk,)),
            pltpu.SemaphoreType.DMA((n_blk,)),
            pltpu.SemaphoreType.DMA,
        ],
        compiler_params=pltpu.CompilerParams(collective_id=collective, has_side_effects=True),
    )(src)


def local(
    feats,
    weight,
    cotangent,
    labels,
    tile_vals,
    tile_row,
    tile_col,
    tile_count,
    hub_vals,
    hub_col,
    hub_dest,
    hub_row,
):
    n_blocks = lax.axis_size("blk")
    n_groups = lax.axis_size("grp")
    my_group = lax.axis_index("grp")
    rows_dev = feats.shape[0]
    width = feats.shape[1]
    tile_size = tile_vals.shape[-1]
    row_tiles = rows_dev // tile_size
    hub_count = hub_vals.shape[2]
    capacity = max(2, hub_count // 4)
    highest = lax.Precision.HIGHEST
    dev_vals = tile_vals[0, 0]
    dev_rows = tile_row[0, 0].reshape(-1)
    dev_cols = tile_col[0, 0].reshape(-1)
    dev_count = tile_count[0, 0]
    tile_range = jnp.arange(row_tiles, dtype=jnp.int32)
    proj = jnp.dot(feats, weight, preferred_element_type=jnp.float32).astype(jnp.bfloat16)
    own_panel = proj.reshape(row_tiles, tile_size, width)

    core = lax.axis_index("blk") % 2
    core_groups = [[i for i in range(n_blocks) if i % 2 == k] for k in range(2)]
    sibling = [(i, i ^ 1) for i in range(n_blocks)]
    panels = lax.all_gather(proj, "blk", axis=0, tiled=True)
    panels = panels.reshape(n_blocks, row_tiles, tile_size, width)
    agg_sum = tile_forward(dev_rows, dev_cols, dev_count, dev_vals, panels)

    dest_all = hub_dest[:, 0, :, 0]
    hub_rows_all = hub_row[:, 0, :]
    hub_range = jnp.arange(hub_count, dtype=jnp.int32)
    earlier = hub_range[None, :] < hub_range[:, None]
    same_dest = dest_all[:, :, None] == dest_all[:, None, :]
    rank_all = jnp.sum((same_dest & earlier[None, :, :]).astype(jnp.int32), axis=-1)
    my_dest = lax.dynamic_index_in_dim(dest_all, my_group, 0, keepdims=False)
    my_rank = lax.dynamic_index_in_dim(rank_all, my_group, 0, keepdims=False)
    slot_of = my_dest * capacity + my_rank
    send_place = (
        slot_of[:, None] == jnp.arange(n_groups * capacity, dtype=jnp.int32)[None, :]
    ).astype(jnp.float32)
    hub_tiles = hub_vals[0, 0]
    hub_cols = hub_col[0, 0]
    hub_src = jnp.take(own_panel, hub_cols, axis=0)
    hub_part = jnp.einsum("hij,hjf->hif", hub_tiles, hub_src, preferred_element_type=jnp.float32)
    send_buf = jnp.einsum("hs,hif->sif", send_place, hub_part, precision=highest)
    send_buf = send_buf.reshape(n_groups, capacity, tile_size, width)
    received = lax.all_to_all(send_buf, "grp", split_axis=0, concat_axis=0, tiled=True)
    chosen = (dest_all == my_group).astype(jnp.float32)
    slot_hot = (rank_all[..., None] == jnp.arange(capacity, dtype=jnp.int32)).astype(
        jnp.float32
    ) * chosen[..., None]
    row_hot = (hub_rows_all[..., None] == tile_range).astype(jnp.float32)
    routing = jnp.einsum("shc,shr->scr", slot_hot, row_hot, precision=highest)
    agg_sum = agg_sum + jnp.einsum("scr,scif->rif", routing, received, precision=highest)
    agg_rows = agg_sum.reshape(rows_dev, width)
    layer_out = jax.nn.silu(agg_rows).astype(jnp.bfloat16)
    sigmoid_z = jax.nn.sigmoid(agg_rows)
    slope = sigmoid_z * (1.0 + agg_rows * (1.0 - sigmoid_z))
    keep = (labels >= 0).astype(jnp.float32)[:, None]
    grad_agg = (cotangent.astype(jnp.float32) * keep * slope).astype(jnp.bfloat16)
    grad_tiles = grad_agg.reshape(row_tiles, tile_size, width)

    keep, send = tile_backward(dev_rows, dev_cols, dev_count, dev_vals, grad_tiles, core.reshape(1))
    from_sibling = lax.ppermute(send, "blk", sibling)
    pair_sum = (keep + from_sibling).astype(jnp.bfloat16)
    received_parts = lax.all_to_all(
        pair_sum, "blk", split_axis=0, concat_axis=0, tiled=True, axis_index_groups=core_groups
    )
    grad_sum = jnp.sum(received_parts.astype(jnp.float32), axis=0)

    back_send = jnp.einsum(
        "scr,rif->scif",
        routing.astype(jnp.bfloat16),
        grad_tiles,
        preferred_element_type=jnp.float32,
    ).astype(jnp.bfloat16)
    back_recv = lax.all_to_all(back_send, "grp", split_axis=0, concat_axis=0, tiled=True)
    back_flat = back_recv.reshape(n_groups * capacity, tile_size, width)
    own_pick = jnp.einsum(
        "hs,sif->hif",
        send_place.astype(jnp.bfloat16),
        back_flat,
        preferred_element_type=jnp.float32,
    ).astype(jnp.bfloat16)
    hub_back = jnp.einsum("hij,hif->hjf", hub_tiles, own_pick, preferred_element_type=jnp.float32)
    col_hot = (hub_cols[:, None] == tile_range[None, :]).astype(jnp.float32)
    grad_sum = grad_sum + jnp.einsum("hr,hjf->rjf", col_hot, hub_back, precision=highest)
    grad_rows = grad_sum.reshape(rows_dev, width).astype(jnp.bfloat16)
    weight_term = lax.dot_general(
        feats, grad_rows, (((0,), (0,)), ((), ())), preferred_element_type=jnp.float32
    )
    grad_scale = 1.0 / math.sqrt(rows_dev * n_blocks * n_groups)
    grad_weight = weight_sum(weight_term, n_groups, n_blocks) * grad_scale
    grad_feats = lax.dot_general(
        grad_rows, weight, (((1,), (1,)), ((), ())), preferred_element_type=jnp.float32
    ).astype(jnp.bfloat16)
    return (layer_out, grad_feats, grad_weight)


def solution(mesh):
    in_specs = (
        P(("grp", "blk"), None),
        P(),
        P(("grp", "blk"), None),
        P(("grp", "blk")),
        P("grp", "blk", None, None, None, None),
        P("grp", "blk", None, None),
        P("grp", "blk", None, None),
        P("grp", "blk", None),
        P("grp", "blk", None, None, None),
        P("grp", "blk", None),
        P(None, "blk", None, None),
        P(None, "blk", None),
    )
    out_specs = (P(("grp", "blk"), None), P(("grp", "blk"), None), P())
    return jax.shard_map(local, mesh=mesh, in_specs=in_specs, out_specs=out_specs, check_vma=False)
```

```python
import functools
import math

import jax
import jax.numpy as jnp
from jax import lax
from jax.experimental import pallas as pl
from jax.experimental.pallas import tpu as pltpu
from jax.sharding import PartitionSpec as P


UNROLL = 4


def grouped_slots(count, slots, visit):
    def body(g, carry):
        terms = []
        for j in range(UNROLL):
            t = g * UNROLL + j
            terms.append((t, t < count))
        visit(terms)
        return carry

    lax.fori_loop(0, (count + UNROLL - 1) // UNROLL, body, 0)


def clamp_tile(index, limit):
    return jnp.minimum(jnp.maximum(index, 0), limit - 1)


def forward_kernel(rows_ref, cols_ref, count_ref, vals_ref, panel_ref, out_ref):
    c = pl.program_id(0)
    slots = vals_ref.shape[1]
    row_tiles = out_ref.shape[0]

    @pl.when(c == 0)
    def _():
        out_ref[...] = jnp.zeros_like(out_ref)

    def visit(terms):
        parts = []
        for t, valid in terms:
            r = clamp_tile(rows_ref[c * slots + t], row_tiles)
            k = clamp_tile(cols_ref[c * slots + t], row_tiles)
            prod = jnp.dot(vals_ref[0, t], panel_ref[0, 0, k], preferred_element_type=jnp.float32)
            parts.append((r, jnp.where(valid, prod, 0.0)))
        for r, prod in parts:
            out_ref[r] += prod

    grouped_slots(count_ref[c], slots, visit)


def backward_kernel(rows_ref, cols_ref, count_ref, core_ref, vals_ref, grad_ref, keep_ref, send_ref, acc_ref):
    i = pl.program_id(0)
    half = pl.num_programs(0) // 2
    p = i // half
    c = 2 * (i % half) + (p + core_ref[0]) % 2
    slots = vals_ref.shape[1]
    row_tiles = grad_ref.shape[0]
    acc_ref[...] = jnp.zeros_like(acc_ref)

    def visit(terms):
        parts = []
        for t, valid in terms:
            r = clamp_tile(rows_ref[c * slots + t], row_tiles)
            k = clamp_tile(cols_ref[c * slots + t], row_tiles)
            prod = lax.dot_general(
                vals_ref[0, t], grad_ref[r], (((0,), (0,)), ((), ())), preferred_element_type=jnp.float32
            )
            parts.append((k, jnp.where(valid, prod, 0.0)))
        for k, prod in parts:
            acc_ref[k] += prod

    grouped_slots(count_ref[c], slots, visit)

    @pl.when(p == 0)
    def _():
        keep_ref[0] = acc_ref[...]

    @pl.when(p == 1)
    def _():
        send_ref[0] = acc_ref[...]


def tile_forward(rows, cols, count, vals, panels):
    n_src, slots, tile, _ = vals.shape
    row_tiles, width = panels.shape[2], panels.shape[4]
    grid_spec = pltpu.PrefetchScalarGridSpec(
        num_scalar_prefetch=3,
        grid=(n_src,),
        in_specs=[
            pl.BlockSpec((1, slots, tile, tile), lambda c, *_: (c, 0, 0, 0)),
            pl.BlockSpec((1, 1, row_tiles, tile, width), lambda c, *_: (c % 2, c // 2, 0, 0, 0)),
        ],
        out_specs=pl.BlockSpec((row_tiles, tile, width), lambda c, *_: (0, 0, 0)),
    )
    flops = 2 * n_src * slots * tile * tile * width
    return pl.pallas_call(
        forward_kernel,
        out_shape=jax.ShapeDtypeStruct((row_tiles, tile, width), jnp.float32),
        grid_spec=grid_spec,
        cost_estimate=pl.CostEstimate(
            flops=flops, transcendentals=0, bytes_accessed=vals.size * 2 + panels.size * 2
        ),
    )(rows, cols, count, vals, panels)


def tile_backward(rows, cols, count, vals, grad_tiles, core):
    n_src, slots, tile, _ = vals.shape
    row_tiles, width = grad_tiles.shape[0], grad_tiles.shape[2]
    half = n_src // 2

    def source(i, core_ref):
        return 2 * (i % half) + (i // half + core_ref[0]) % 2

    grid_spec = pltpu.PrefetchScalarGridSpec(
        num_scalar_prefetch=4,
        grid=(n_src,),
        in_specs=[
            pl.BlockSpec((1, slots, tile, tile), lambda i, r, k, n, core_ref: (source(i, core_ref), 0, 0, 0)),
            pl.BlockSpec((row_tiles, tile, width), lambda i, *_: (0, 0, 0)),
        ],
        out_specs=[
            pl.BlockSpec((1, row_tiles, tile, width), lambda i, *_: (jnp.minimum(i, half - 1), 0, 0, 0)),
            pl.BlockSpec((1, row_tiles, tile, width), lambda i, *_: (jnp.maximum(i - half, 0), 0, 0, 0)),
        ],
        scratch_shapes=[pltpu.VMEM((row_tiles, tile, width), jnp.float32)],
    )
    flops = 2 * n_src * slots * tile * tile * width
    part = jax.ShapeDtypeStruct((half, row_tiles, tile, width), jnp.float32)
    return pl.pallas_call(
        backward_kernel,
        out_shape=(part, part),
        grid_spec=grid_spec,
        cost_estimate=pl.CostEstimate(
            flops=flops, transcendentals=0, bytes_accessed=vals.size * 2 + n_src * row_tiles * tile * width * 4
        ),
    )(rows, cols, count, core, vals, grad_tiles)


MESH_ID = pl.DeviceIdType.MESH


def weight_sum_kernel(n_grp, n_blk, x_ref, out_ref, part, grp_part, whole, sems):
    g = lax.axis_index("grp")
    b = lax.axis_index("blk")
    send1, recv1, send2, recv2, send3, recv3 = sems
    barrier = pltpu.get_barrier_semaphore()
    for i in range(1, n_blk):
        pl.semaphore_signal(barrier, 1, device_id=(g, (b + i) % n_blk), device_id_type=MESH_ID)
    for i in range(1, n_grp):
        pl.semaphore_signal(barrier, 1, device_id=((g + i) % n_grp, b), device_id_type=MESH_ID)
    pl.semaphore_wait(barrier, n_blk - 1 + n_grp - 1)

    def blk_copy(src, dst, send, recv, to, slot):
        return pltpu.make_async_remote_copy(
            src_ref=src, dst_ref=dst, send_sem=send.at[to], recv_sem=recv.at[slot],
            device_id=(g, to), device_id_type=MESH_ID,
        )

    def grp_copy(src, dst, send, recv, to, slot):
        return pltpu.make_async_remote_copy(
            src_ref=src, dst_ref=dst, send_sem=send.at[to], recv_sem=recv.at[slot],
            device_id=(to, b), device_id_type=MESH_ID,
        )

    out1 = []
    for i in range(1, n_blk):
        to = (b + i) % n_blk
        cp = blk_copy(x_ref.at[to], part.at[b], send1, recv1, to, b)
        cp.start()
        out1.append(cp)
    part[b] = x_ref[b]
    for i in range(1, n_blk):
        src = (b + n_blk - i) % n_blk
        blk_copy(x_ref.at[b], part.at[src], send1, recv1, src, src).wait_recv()
    for cp in out1:
        cp.wait_send()
    acc = part[0]
    for j in range(1, n_blk):
        acc = acc + part[j]
    grp_part[g] = acc

    out2 = []
    for i in range(1, n_grp):
        to = (g + i) % n_grp
        cp = grp_copy(grp_part.at[g], grp_part.at[g], send2, recv2, to, g)
        cp.start()
        out2.append(cp)
    for i in range(1, n_grp):
        src = (g + n_grp - i) % n_grp
        grp_copy(grp_part.at[src], grp_part.at[src], send2, recv2, src, src).wait_recv()
    for cp in out2:
        cp.wait_send()
    acc = grp_part[0]
    for j in range(1, n_grp):
        acc = acc + grp_part[j]
    whole[b] = acc

    out3 = []
    for i in range(1, n_blk):
        to = (b + i) % n_blk
        cp = blk_copy(whole.at[b], whole.at[b], send3, recv3, to, b)
        cp.start()
        out3.append(cp)
    for i in range(1, n_blk):
        src = (b + n_blk - i) % n_blk
        blk_copy(whole.at[src], whole.at[src], send3, recv3, src, src).wait_recv()
    for cp in out3:
        cp.wait_send()
    out_ref[...] = whole[...]


def weight_sum(term, n_grp, n_blk):
    rows, cols = term.shape
    chunk = rows * cols // (n_blk * 128)
    x = term.reshape(n_blk, chunk, 128)
    vmem = pl.BlockSpec(memory_space=pltpu.VMEM)
    out = pl.pallas_call(
        functools.partial(weight_sum_kernel, n_grp, n_blk),
        out_shape=jax.ShapeDtypeStruct(x.shape, jnp.float32),
        in_specs=[vmem],
        out_specs=vmem,
        scratch_shapes=[
            pltpu.VMEM(x.shape, jnp.float32),
            pltpu.VMEM((n_grp, chunk, 128), jnp.float32),
            pltpu.VMEM(x.shape, jnp.float32),
            [pltpu.SemaphoreType.DMA((n_blk,)), pltpu.SemaphoreType.DMA((n_blk,)),
             pltpu.SemaphoreType.DMA((n_grp,)), pltpu.SemaphoreType.DMA((n_grp,)),
             pltpu.SemaphoreType.DMA((n_blk,)), pltpu.SemaphoreType.DMA((n_blk,))],
        ],
        compiler_params=pltpu.CompilerParams(collective_id=0, has_side_effects=True),
    )(x)
    return out.reshape(rows, cols)


def exchange_kernel(n_blk, by_dest, src_ref, out_ref, send, recv, own):
    g = lax.axis_index("grp")
    b = lax.axis_index("blk")
    barrier = pltpu.get_barrier_semaphore()
    for i in range(1, n_blk):
        pl.semaphore_signal(barrier, 1, device_id=(g, (b + i) % n_blk), device_id_type=MESH_ID)
    pl.semaphore_wait(barrier, n_blk - 1)

    def piece(to):
        return src_ref.at[to] if by_dest else src_ref

    def remote(to, slot):
        return pltpu.make_async_remote_copy(
            src_ref=piece(to), dst_ref=out_ref.at[slot], send_sem=send.at[to], recv_sem=recv.at[slot],
            device_id=(g, to), device_id_type=MESH_ID,
        )

    local = pltpu.make_async_copy(piece(b), out_ref.at[b], own)
    local.start()
    sent = []
    for i in range(1, n_blk):
        cp = remote((b + i) % n_blk, b)
        cp.start()
        sent.append(cp)
    for i in range(1, n_blk):
        src = (b + n_blk - i) % n_blk
        remote(src, src).wait_recv()
    for cp in sent:
        cp.wait_send()
    local.wait()


def exchange(src, n_blk, by_dest, collective):
    shape = src.shape[1:] if by_dest else src.shape
    any_space = pl.BlockSpec(memory_space=pl.ANY)
    return pl.pallas_call(
        functools.partial(exchange_kernel, n_blk, by_dest),
        out_shape=jax.ShapeDtypeStruct((n_blk,) + shape, src.dtype),
        in_specs=[any_space],
        out_specs=any_space,
        scratch_shapes=[
            pltpu.SemaphoreType.DMA((n_blk,)),
            pltpu.SemaphoreType.DMA((n_blk,)),
            pltpu.SemaphoreType.DMA,
        ],
        compiler_params=pltpu.CompilerParams(collective_id=collective, has_side_effects=True),
    )(src)


def local(
    feats,
    weight,
    cotangent,
    labels,
    tile_vals,
    tile_row,
    tile_col,
    tile_count,
    hub_vals,
    hub_col,
    hub_dest,
    hub_row,
):
    n_blocks = lax.axis_size("blk")
    n_groups = lax.axis_size("grp")
    my_group = lax.axis_index("grp")
    rows_dev = feats.shape[0]
    width = feats.shape[1]
    tile_size = tile_vals.shape[-1]
    row_tiles = rows_dev // tile_size
    hub_count = hub_vals.shape[2]
    capacity = max(2, hub_count // 4)
    highest = lax.Precision.HIGHEST
    dev_vals = tile_vals[0, 0]
    dev_rows = tile_row[0, 0].reshape(-1)
    dev_cols = tile_col[0, 0].reshape(-1)
    dev_count = tile_count[0, 0]
    tile_range = jnp.arange(row_tiles, dtype=jnp.int32)
    proj = jnp.dot(feats, weight, preferred_element_type=jnp.float32).astype(jnp.bfloat16)
    own_panel = proj.reshape(row_tiles, tile_size, width)

    core = lax.axis_index("blk") % 2
    core_groups = [[i for i in range(n_blocks) if i % 2 == k] for k in range(2)]
    sibling = [(i, i ^ 1) for i in range(n_blocks)]
    pair_groups = [[i, i + 1] for i in range(0, n_blocks, 2)]
    same_core = lax.all_gather(own_panel, "blk", axis=0, tiled=False, axis_index_groups=core_groups)

    dest_all = hub_dest[:, 0, :, 0]
    hub_rows_all = hub_row[:, 0, :]
    hub_range = jnp.arange(hub_count, dtype=jnp.int32)
    earlier = hub_range[None, :] < hub_range[:, None]
    same_dest = dest_all[:, :, None] == dest_all[:, None, :]
    rank_all = jnp.sum((same_dest & earlier[None, :, :]).astype(jnp.int32), axis=-1)
    my_dest = lax.dynamic_index_in_dim(dest_all, my_group, 0, keepdims=False)
    my_rank = lax.dynamic_index_in_dim(rank_all, my_group, 0, keepdims=False)
    slot_of = my_dest * capacity + my_rank
    send_place = (
        slot_of[:, None] == jnp.arange(n_groups * capacity, dtype=jnp.int32)[None, :]
    ).astype(jnp.float32)
    hub_tiles = hub_vals[0, 0]
    hub_cols = hub_col[0, 0]
    hub_src = jnp.take(own_panel, hub_cols, axis=0)
    hub_part = jnp.einsum("hij,hjf->hif", hub_tiles, hub_src, preferred_element_type=jnp.float32)
    send_buf = jnp.einsum("hs,hif->sif", send_place, hub_part, precision=highest)
    send_buf = send_buf.reshape(n_groups, capacity, tile_size, width)
    received = lax.all_to_all(send_buf, "grp", split_axis=0, concat_axis=0, tiled=True)
    same_core, received = lax.optimization_barrier((same_core, received))
    panels = lax.all_gather(same_core, "blk", axis=0, tiled=False, axis_index_groups=pair_groups)
    agg_sum = tile_forward(dev_rows, dev_cols, dev_count, dev_vals, panels)
    chosen = (dest_all == my_group).astype(jnp.float32)
    slot_hot = (rank_all[..., None] == jnp.arange(capacity, dtype=jnp.int32)).astype(
        jnp.float32
    ) * chosen[..., None]
    row_hot = (hub_rows_all[..., None] == tile_range).astype(jnp.float32)
    routing = jnp.einsum("shc,shr->scr", slot_hot, row_hot, precision=highest)
    agg_sum = agg_sum + jnp.einsum("scr,scif->rif", routing, received, precision=highest)
    agg_rows = agg_sum.reshape(rows_dev, width)
    layer_out = jax.nn.silu(agg_rows).astype(jnp.bfloat16)
    sigmoid_z = jax.nn.sigmoid(agg_rows)
    slope = sigmoid_z * (1.0 + agg_rows * (1.0 - sigmoid_z))
    keep = (labels >= 0).astype(jnp.float32)[:, None]
    grad_agg = (cotangent.astype(jnp.float32) * keep * slope).astype(jnp.bfloat16)
    grad_tiles = grad_agg.reshape(row_tiles, tile_size, width)

    keep, send = tile_backward(dev_rows, dev_cols, dev_count, dev_vals, grad_tiles, core.reshape(1))
    from_sibling = lax.ppermute(send, "blk", sibling)
    pair_sum = (keep + from_sibling).astype(jnp.bfloat16)
    received_parts = lax.all_to_all(
        pair_sum, "blk", split_axis=0, concat_axis=0, tiled=True, axis_index_groups=core_groups
    )
    grad_sum = jnp.sum(received_parts.astype(jnp.float32), axis=0)

    back_send = jnp.einsum(
        "scr,rif->scif",
        routing.astype(jnp.bfloat16),
        grad_tiles,
        preferred_element_type=jnp.float32,
    ).astype(jnp.bfloat16)
    back_recv = lax.all_to_all(back_send, "grp", split_axis=0, concat_axis=0, tiled=True)
    back_flat = back_recv.reshape(n_groups * capacity, tile_size, width)
    own_pick = jnp.einsum(
        "hs,sif->hif",
        send_place.astype(jnp.bfloat16),
        back_flat,
        preferred_element_type=jnp.float32,
    ).astype(jnp.bfloat16)
    hub_back = jnp.einsum("hij,hif->hjf", hub_tiles, own_pick, preferred_element_type=jnp.float32)
    col_hot = (hub_cols[:, None] == tile_range[None, :]).astype(jnp.float32)
    grad_sum = grad_sum + jnp.einsum("hr,hjf->rjf", col_hot, hub_back, precision=highest)
    grad_rows = grad_sum.reshape(rows_dev, width).astype(jnp.bfloat16)
    weight_term = lax.dot_general(
        feats, grad_rows, (((0,), (0,)), ((), ())), preferred_element_type=jnp.float32
    )
    grad_scale = 1.0 / math.sqrt(rows_dev * n_blocks * n_groups)
    grad_weight = weight_sum(weight_term, n_groups, n_blocks) * grad_scale
    grad_feats = lax.dot_general(
        grad_rows, weight, (((1,), (1,)), ((), ())), preferred_element_type=jnp.float32
    ).astype(jnp.bfloat16)
    return (layer_out, grad_feats, grad_weight)


def solution(mesh):
    in_specs = (
        P(("grp", "blk"), None),
        P(),
        P(("grp", "blk"), None),
        P(("grp", "blk")),
        P("grp", "blk", None, None, None, None),
        P("grp", "blk", None, None),
        P("grp", "blk", None, None),
        P("grp", "blk", None),
        P("grp", "blk", None, None, None),
        P("grp", "blk", None),
        P(None, "blk", None, None),
        P(None, "blk", None),
    )
    out_specs = (P(("grp", "blk"), None), P(("grp", "blk"), None), P())
    return jax.shard_map(local, mesh=mesh, in_specs=in_specs, out_specs=out_specs, check_vma=False)
```

```python
import functools
import math

import jax
import jax.numpy as jnp
from jax import lax
from jax.experimental import pallas as pl
from jax.experimental.pallas import tpu as pltpu
from jax.sharding import PartitionSpec as P


UNROLL = 4


def grouped_slots(count, slots, visit):
    def body(g, carry):
        terms = []
        for j in range(UNROLL):
            t = g * UNROLL + j
            terms.append((t, t < count))
        visit(terms)
        return carry

    lax.fori_loop(0, (count + UNROLL - 1) // UNROLL, body, 0)


def clamp_tile(index, limit):
    return jnp.minimum(jnp.maximum(index, 0), limit - 1)


def forward_kernel(rows_ref, cols_ref, count_ref, vals_ref, panel_ref, out_ref):
    c = pl.program_id(0)
    slots = vals_ref.shape[1]
    row_tiles = out_ref.shape[0]

    @pl.when(c == 0)
    def _():
        out_ref[...] = jnp.zeros_like(out_ref)

    def visit(terms):
        parts = []
        for t, valid in terms:
            r = clamp_tile(rows_ref[c * slots + t], row_tiles)
            k = clamp_tile(cols_ref[c * slots + t], row_tiles)
            prod = jnp.dot(vals_ref[0, t], panel_ref[0, k], preferred_element_type=jnp.float32)
            parts.append((r, jnp.where(valid, prod, 0.0)))
        for r, prod in parts:
            out_ref[r] += prod

    grouped_slots(count_ref[c], slots, visit)


def backward_kernel(rows_ref, cols_ref, count_ref, core_ref, vals_ref, grad_ref, keep_ref, send_ref, acc_ref):
    i = pl.program_id(0)
    half = pl.num_programs(0) // 2
    p = i // half
    c = 2 * (i % half) + (p + core_ref[0]) % 2
    slots = vals_ref.shape[1]
    row_tiles = grad_ref.shape[0]
    acc_ref[...] = jnp.zeros_like(acc_ref)

    def visit(terms):
        parts = []
        for t, valid in terms:
            r = clamp_tile(rows_ref[c * slots + t], row_tiles)
            k = clamp_tile(cols_ref[c * slots + t], row_tiles)
            prod = lax.dot_general(
                vals_ref[0, t], grad_ref[r], (((0,), (0,)), ((), ())), preferred_element_type=jnp.float32
            )
            parts.append((k, jnp.where(valid, prod, 0.0)))
        for k, prod in parts:
            acc_ref[k] += prod

    grouped_slots(count_ref[c], slots, visit)

    @pl.when(p == 0)
    def _():
        keep_ref[0] = acc_ref[...]

    @pl.when(p == 1)
    def _():
        send_ref[0] = acc_ref[...]


def tile_forward(rows, cols, count, vals, panels):
    n_src, slots, tile, _ = vals.shape
    row_tiles, width = panels.shape[1], panels.shape[3]
    grid_spec = pltpu.PrefetchScalarGridSpec(
        num_scalar_prefetch=3,
        grid=(n_src,),
        in_specs=[
            pl.BlockSpec((1, slots, tile, tile), lambda c, *_: (c, 0, 0, 0)),
            pl.BlockSpec((1, row_tiles, tile, width), lambda c, *_: (c, 0, 0, 0)),
        ],
        out_specs=pl.BlockSpec((row_tiles, tile, width), lambda c, *_: (0, 0, 0)),
    )
    flops = 2 * n_src * slots * tile * tile * width
    return pl.pallas_call(
        forward_kernel,
        out_shape=jax.ShapeDtypeStruct((row_tiles, tile, width), jnp.float32),
        grid_spec=grid_spec,
        cost_estimate=pl.CostEstimate(
            flops=flops, transcendentals=0, bytes_accessed=vals.size * 2 + panels.size * 2
        ),
    )(rows, cols, count, vals, panels)


def tile_backward(rows, cols, count, vals, grad_tiles, core):
    n_src, slots, tile, _ = vals.shape
    row_tiles, width = grad_tiles.shape[0], grad_tiles.shape[2]
    half = n_src // 2

    def source(i, core_ref):
        return 2 * (i % half) + (i // half + core_ref[0]) % 2

    grid_spec = pltpu.PrefetchScalarGridSpec(
        num_scalar_prefetch=4,
        grid=(n_src,),
        in_specs=[
            pl.BlockSpec((1, slots, tile, tile), lambda i, r, k, n, core_ref: (source(i, core_ref), 0, 0, 0)),
            pl.BlockSpec((row_tiles, tile, width), lambda i, *_: (0, 0, 0)),
        ],
        out_specs=[
            pl.BlockSpec((1, row_tiles, tile, width), lambda i, *_: (jnp.minimum(i, half - 1), 0, 0, 0)),
            pl.BlockSpec((1, row_tiles, tile, width), lambda i, *_: (jnp.maximum(i - half, 0), 0, 0, 0)),
        ],
        scratch_shapes=[pltpu.VMEM((row_tiles, tile, width), jnp.float32)],
    )
    flops = 2 * n_src * slots * tile * tile * width
    part = jax.ShapeDtypeStruct((half, row_tiles, tile, width), jnp.float32)
    return pl.pallas_call(
        backward_kernel,
        out_shape=(part, part),
        grid_spec=grid_spec,
        cost_estimate=pl.CostEstimate(
            flops=flops, transcendentals=0, bytes_accessed=vals.size * 2 + n_src * row_tiles * tile * width * 4
        ),
    )(rows, cols, count, core, vals, grad_tiles)


MESH_ID = pl.DeviceIdType.MESH


def weight_sum_kernel(n_grp, n_blk, x_ref, out_ref, part, grp_part, whole, sems):
    g = lax.axis_index("grp")
    b = lax.axis_index("blk")
    send1, recv1, send2, recv2, send3, recv3 = sems
    barrier = pltpu.get_barrier_semaphore()
    for i in range(1, n_blk):
        pl.semaphore_signal(barrier, 1, device_id=(g, (b + i) % n_blk), device_id_type=MESH_ID)
    for i in range(1, n_grp):
        pl.semaphore_signal(barrier, 1, device_id=((g + i) % n_grp, b), device_id_type=MESH_ID)
    pl.semaphore_wait(barrier, n_blk - 1 + n_grp - 1)

    def blk_copy(src, dst, send, recv, to, slot):
        return pltpu.make_async_remote_copy(
            src_ref=src, dst_ref=dst, send_sem=send.at[to], recv_sem=recv.at[slot],
            device_id=(g, to), device_id_type=MESH_ID,
        )

    def grp_copy(src, dst, send, recv, to, slot):
        return pltpu.make_async_remote_copy(
            src_ref=src, dst_ref=dst, send_sem=send.at[to], recv_sem=recv.at[slot],
            device_id=(to, b), device_id_type=MESH_ID,
        )

    out1 = []
    for i in range(1, n_blk):
        to = (b + i) % n_blk
        cp = blk_copy(x_ref.at[to], part.at[b], send1, recv1, to, b)
        cp.start()
        out1.append(cp)
    part[b] = x_ref[b]
    for i in range(1, n_blk):
        src = (b + n_blk - i) % n_blk
        blk_copy(x_ref.at[b], part.at[src], send1, recv1, src, src).wait_recv()
    for cp in out1:
        cp.wait_send()
    acc = part[0]
    for j in range(1, n_blk):
        acc = acc + part[j]
    grp_part[g] = acc

    out2 = []
    for i in range(1, n_grp):
        to = (g + i) % n_grp
        cp = grp_copy(grp_part.at[g], grp_part.at[g], send2, recv2, to, g)
        cp.start()
        out2.append(cp)
    for i in range(1, n_grp):
        src = (g + n_grp - i) % n_grp
        grp_copy(grp_part.at[src], grp_part.at[src], send2, recv2, src, src).wait_recv()
    for cp in out2:
        cp.wait_send()
    acc = grp_part[0]
    for j in range(1, n_grp):
        acc = acc + grp_part[j]
    whole[b] = acc

    out3 = []
    for i in range(1, n_blk):
        to = (b + i) % n_blk
        cp = blk_copy(whole.at[b], whole.at[b], send3, recv3, to, b)
        cp.start()
        out3.append(cp)
    for i in range(1, n_blk):
        src = (b + n_blk - i) % n_blk
        blk_copy(whole.at[src], whole.at[src], send3, recv3, src, src).wait_recv()
    for cp in out3:
        cp.wait_send()
    out_ref[...] = whole[...]


def weight_sum(term, n_grp, n_blk):
    rows, cols = term.shape
    chunk = rows * cols // (n_blk * 128)
    x = term.reshape(n_blk, chunk, 128)
    vmem = pl.BlockSpec(memory_space=pltpu.VMEM)
    out = pl.pallas_call(
        functools.partial(weight_sum_kernel, n_grp, n_blk),
        out_shape=jax.ShapeDtypeStruct(x.shape, jnp.float32),
        in_specs=[vmem],
        out_specs=vmem,
        scratch_shapes=[
            pltpu.VMEM(x.shape, jnp.float32),
            pltpu.VMEM((n_grp, chunk, 128), jnp.float32),
            pltpu.VMEM(x.shape, jnp.float32),
            [pltpu.SemaphoreType.DMA((n_blk,)), pltpu.SemaphoreType.DMA((n_blk,)),
             pltpu.SemaphoreType.DMA((n_grp,)), pltpu.SemaphoreType.DMA((n_grp,)),
             pltpu.SemaphoreType.DMA((n_blk,)), pltpu.SemaphoreType.DMA((n_blk,))],
        ],
        compiler_params=pltpu.CompilerParams(collective_id=0, has_side_effects=True),
    )(x)
    return out.reshape(rows, cols)


def exchange_kernel(n_blk, by_dest, src_ref, out_ref, send, recv, own):
    g = lax.axis_index("grp")
    b = lax.axis_index("blk")
    barrier = pltpu.get_barrier_semaphore()
    for i in range(1, n_blk):
        pl.semaphore_signal(barrier, 1, device_id=(g, (b + i) % n_blk), device_id_type=MESH_ID)
    pl.semaphore_wait(barrier, n_blk - 1)

    def piece(to):
        return src_ref.at[to] if by_dest else src_ref

    def remote(to, slot):
        return pltpu.make_async_remote_copy(
            src_ref=piece(to), dst_ref=out_ref.at[slot], send_sem=send.at[to], recv_sem=recv.at[slot],
            device_id=(g, to), device_id_type=MESH_ID,
        )

    local = pltpu.make_async_copy(piece(b), out_ref.at[b], own)
    local.start()
    sent = []
    for i in range(1, n_blk):
        cp = remote((b + i) % n_blk, b)
        cp.start()
        sent.append(cp)
    for i in range(1, n_blk):
        src = (b + n_blk - i) % n_blk
        remote(src, src).wait_recv()
    for cp in sent:
        cp.wait_send()
    local.wait()


def exchange(src, n_blk, by_dest, collective):
    shape = src.shape[1:] if by_dest else src.shape
    any_space = pl.BlockSpec(memory_space=pl.ANY)
    return pl.pallas_call(
        functools.partial(exchange_kernel, n_blk, by_dest),
        out_shape=jax.ShapeDtypeStruct((n_blk,) + shape, src.dtype),
        in_specs=[any_space],
        out_specs=any_space,
        scratch_shapes=[
            pltpu.SemaphoreType.DMA((n_blk,)),
            pltpu.SemaphoreType.DMA((n_blk,)),
            pltpu.SemaphoreType.DMA,
        ],
        compiler_params=pltpu.CompilerParams(collective_id=collective, has_side_effects=True),
    )(src)


def local(
    feats,
    weight,
    cotangent,
    labels,
    tile_vals,
    tile_row,
    tile_col,
    tile_count,
    hub_vals,
    hub_col,
    hub_dest,
    hub_row,
):
    n_blocks = lax.axis_size("blk")
    n_groups = lax.axis_size("grp")
    my_group = lax.axis_index("grp")
    rows_dev = feats.shape[0]
    width = feats.shape[1]
    tile_size = tile_vals.shape[-1]
    row_tiles = rows_dev // tile_size
    hub_count = hub_vals.shape[2]
    capacity = max(2, hub_count // 4)
    highest = lax.Precision.HIGHEST
    dev_vals = tile_vals[0, 0]
    dev_rows = tile_row[0, 0].reshape(-1)
    dev_cols = tile_col[0, 0].reshape(-1)
    dev_count = tile_count[0, 0]
    tile_range = jnp.arange(row_tiles, dtype=jnp.int32)
    proj = jnp.dot(feats, weight, preferred_element_type=jnp.float32).astype(jnp.bfloat16)
    own_panel = proj.reshape(row_tiles, tile_size, width)

    core = lax.axis_index("blk") % 2
    core_groups = [[i for i in range(n_blocks) if i % 2 == k] for k in range(2)]
    sibling = [(i, i ^ 1) for i in range(n_blocks)]
    panels = lax.all_gather(proj, "blk", axis=0, tiled=True)
    panels = panels.reshape(n_blocks, row_tiles, tile_size, width)
    agg_sum = tile_forward(dev_rows, dev_cols, dev_count, dev_vals, panels)

    dest_all = hub_dest[:, 0, :, 0]
    hub_rows_all = hub_row[:, 0, :]
    hub_range = jnp.arange(hub_count, dtype=jnp.int32)
    earlier = hub_range[None, :] < hub_range[:, None]
    same_dest = dest_all[:, :, None] == dest_all[:, None, :]
    rank_all = jnp.sum((same_dest & earlier[None, :, :]).astype(jnp.int32), axis=-1)
    my_dest = lax.dynamic_index_in_dim(dest_all, my_group, 0, keepdims=False)
    my_rank = lax.dynamic_index_in_dim(rank_all, my_group, 0, keepdims=False)
    slot_of = my_dest * capacity + my_rank
    send_place = (
        slot_of[:, None] == jnp.arange(n_groups * capacity, dtype=jnp.int32)[None, :]
    ).astype(jnp.float32)
    hub_tiles = hub_vals[0, 0]
    hub_cols = hub_col[0, 0]
    hub_src = jnp.take(own_panel, hub_cols, axis=0)
    hub_part = jnp.einsum("hij,hjf->hif", hub_tiles, hub_src, preferred_element_type=jnp.float32)
    send_buf = jnp.einsum(
        "hs,hif->sif", send_place.astype(jnp.bfloat16), hub_part.astype(jnp.bfloat16),
        preferred_element_type=jnp.float32,
    ).astype(jnp.bfloat16)
    send_buf = send_buf.reshape(n_groups, capacity, tile_size, width)
    received = lax.all_to_all(send_buf, "grp", split_axis=0, concat_axis=0, tiled=True)
    chosen = (dest_all == my_group).astype(jnp.float32)
    slot_hot = (rank_all[..., None] == jnp.arange(capacity, dtype=jnp.int32)).astype(
        jnp.float32
    ) * chosen[..., None]
    row_hot = (hub_rows_all[..., None] == tile_range).astype(jnp.float32)
    routing = jnp.einsum("shc,shr->scr", slot_hot, row_hot, precision=highest)
    agg_sum = agg_sum + jnp.einsum(
        "scr,scif->rif", routing.astype(jnp.bfloat16), received, preferred_element_type=jnp.float32
    )
    agg_rows = agg_sum.reshape(rows_dev, width)
    layer_out = jax.nn.silu(agg_rows).astype(jnp.bfloat16)
    sigmoid_z = jax.nn.sigmoid(agg_rows)
    slope = sigmoid_z * (1.0 + agg_rows * (1.0 - sigmoid_z))
    keep = (labels >= 0).astype(jnp.float32)[:, None]
    grad_agg = (cotangent.astype(jnp.float32) * keep * slope).astype(jnp.bfloat16)
    grad_tiles = grad_agg.reshape(row_tiles, tile_size, width)

    keep, send = tile_backward(dev_rows, dev_cols, dev_count, dev_vals, grad_tiles, core.reshape(1))
    from_sibling = lax.ppermute(send, "blk", sibling)
    pair_sum = (keep + from_sibling).astype(jnp.bfloat16)
    received_parts = lax.all_to_all(
        pair_sum, "blk", split_axis=0, concat_axis=0, tiled=True, axis_index_groups=core_groups
    )
    grad_sum = jnp.sum(received_parts.astype(jnp.float32), axis=0)

    back_send = jnp.einsum(
        "scr,rif->scif",
        routing.astype(jnp.bfloat16),
        grad_tiles,
        preferred_element_type=jnp.float32,
    ).astype(jnp.bfloat16)
    back_recv = lax.all_to_all(back_send, "grp", split_axis=0, concat_axis=0, tiled=True)
    back_flat = back_recv.reshape(n_groups * capacity, tile_size, width)
    own_pick = jnp.einsum(
        "hs,sif->hif",
        send_place.astype(jnp.bfloat16),
        back_flat,
        preferred_element_type=jnp.float32,
    ).astype(jnp.bfloat16)
    hub_back = jnp.einsum("hij,hif->hjf", hub_tiles, own_pick, preferred_element_type=jnp.float32)
    col_hot = (hub_cols[:, None] == tile_range[None, :]).astype(jnp.float32)
    grad_sum = grad_sum + jnp.einsum("hr,hjf->rjf", col_hot, hub_back, precision=highest)
    grad_rows = grad_sum.reshape(rows_dev, width).astype(jnp.bfloat16)
    weight_term = lax.dot_general(
        feats, grad_rows, (((0,), (0,)), ((), ())), preferred_element_type=jnp.float32
    )
    grad_scale = 1.0 / math.sqrt(rows_dev * n_blocks * n_groups)
    grad_weight = weight_sum(weight_term, n_groups, n_blocks) * grad_scale
    grad_feats = lax.dot_general(
        grad_rows, weight, (((1,), (1,)), ((), ())), preferred_element_type=jnp.float32
    ).astype(jnp.bfloat16)
    return (layer_out, grad_feats, grad_weight)


def solution(mesh):
    in_specs = (
        P(("grp", "blk"), None),
        P(),
        P(("grp", "blk"), None),
        P(("grp", "blk")),
        P("grp", "blk", None, None, None, None),
        P("grp", "blk", None, None),
        P("grp", "blk", None, None),
        P("grp", "blk", None),
        P("grp", "blk", None, None, None),
        P("grp", "blk", None),
        P(None, "blk", None, None),
        P(None, "blk", None),
    )
    out_specs = (P(("grp", "blk"), None), P(("grp", "blk"), None), P())
    return jax.shard_map(local, mesh=mesh, in_specs=in_specs, out_specs=out_specs, check_vma=False)
```

```python
import functools
import math

import jax
import jax.numpy as jnp
from jax import lax
from jax.experimental import pallas as pl
from jax.experimental.pallas import tpu as pltpu
from jax.sharding import PartitionSpec as P


UNROLL = 8


def grouped_slots(count, slots, visit):
    def body(g, carry):
        terms = []
        for j in range(UNROLL):
            t = g * UNROLL + j
            terms.append((t, t < count))
        visit(terms)
        return carry

    lax.fori_loop(0, (count + UNROLL - 1) // UNROLL, body, 0)


def clamp_tile(index, limit):
    return jnp.minimum(jnp.maximum(index, 0), limit - 1)


def forward_kernel(rows_ref, cols_ref, count_ref, vals_ref, panel_ref, out_ref):
    c = pl.program_id(0)
    slots = vals_ref.shape[1]
    row_tiles = out_ref.shape[0]

    @pl.when(c == 0)
    def _():
        out_ref[...] = jnp.zeros_like(out_ref)

    def visit(terms):
        parts = []
        for t, valid in terms:
            r = clamp_tile(rows_ref[c * slots + t], row_tiles)
            k = clamp_tile(cols_ref[c * slots + t], row_tiles)
            prod = jnp.dot(vals_ref[0, t], panel_ref[0, k], preferred_element_type=jnp.float32)
            parts.append((r, jnp.where(valid, prod, 0.0)))
        for r, prod in parts:
            out_ref[r] += prod

    grouped_slots(count_ref[c], slots, visit)


def backward_kernel(rows_ref, cols_ref, count_ref, core_ref, vals_ref, grad_ref, keep_ref, send_ref, acc_ref):
    i = pl.program_id(0)
    half = pl.num_programs(0) // 2
    p = i // half
    c = 2 * (i % half) + (p + core_ref[0]) % 2
    slots = vals_ref.shape[1]
    row_tiles = grad_ref.shape[0]
    acc_ref[...] = jnp.zeros_like(acc_ref)

    def visit(terms):
        parts = []
        for t, valid in terms:
            r = clamp_tile(rows_ref[c * slots + t], row_tiles)
            k = clamp_tile(cols_ref[c * slots + t], row_tiles)
            prod = lax.dot_general(
                vals_ref[0, t], grad_ref[r], (((0,), (0,)), ((), ())), preferred_element_type=jnp.float32
            )
            parts.append((k, jnp.where(valid, prod, 0.0)))
        for k, prod in parts:
            acc_ref[k] += prod

    grouped_slots(count_ref[c], slots, visit)

    @pl.when(p == 0)
    def _():
        keep_ref[0] = acc_ref[...]

    @pl.when(p == 1)
    def _():
        send_ref[0] = acc_ref[...]


def tile_forward(rows, cols, count, vals, panels):
    n_src, slots, tile, _ = vals.shape
    row_tiles, width = panels.shape[1], panels.shape[3]
    grid_spec = pltpu.PrefetchScalarGridSpec(
        num_scalar_prefetch=3,
        grid=(n_src,),
        in_specs=[
            pl.BlockSpec((1, slots, tile, tile), lambda c, *_: (c, 0, 0, 0)),
            pl.BlockSpec((1, row_tiles, tile, width), lambda c, *_: (c, 0, 0, 0)),
        ],
        out_specs=pl.BlockSpec((row_tiles, tile, width), lambda c, *_: (0, 0, 0)),
    )
    flops = 2 * n_src * slots * tile * tile * width
    return pl.pallas_call(
        forward_kernel,
        out_shape=jax.ShapeDtypeStruct((row_tiles, tile, width), jnp.float32),
        grid_spec=grid_spec,
        cost_estimate=pl.CostEstimate(
            flops=flops, transcendentals=0, bytes_accessed=vals.size * 2 + panels.size * 2
        ),
    )(rows, cols, count, vals, panels)


def tile_backward(rows, cols, count, vals, grad_tiles, core):
    n_src, slots, tile, _ = vals.shape
    row_tiles, width = grad_tiles.shape[0], grad_tiles.shape[2]
    half = n_src // 2

    def source(i, core_ref):
        return 2 * (i % half) + (i // half + core_ref[0]) % 2

    grid_spec = pltpu.PrefetchScalarGridSpec(
        num_scalar_prefetch=4,
        grid=(n_src,),
        in_specs=[
            pl.BlockSpec((1, slots, tile, tile), lambda i, r, k, n, core_ref: (source(i, core_ref), 0, 0, 0)),
            pl.BlockSpec((row_tiles, tile, width), lambda i, *_: (0, 0, 0)),
        ],
        out_specs=[
            pl.BlockSpec((1, row_tiles, tile, width), lambda i, *_: (jnp.minimum(i, half - 1), 0, 0, 0)),
            pl.BlockSpec((1, row_tiles, tile, width), lambda i, *_: (jnp.maximum(i - half, 0), 0, 0, 0)),
        ],
        scratch_shapes=[pltpu.VMEM((row_tiles, tile, width), jnp.float32)],
    )
    flops = 2 * n_src * slots * tile * tile * width
    part = jax.ShapeDtypeStruct((half, row_tiles, tile, width), jnp.float32)
    return pl.pallas_call(
        backward_kernel,
        out_shape=(part, part),
        grid_spec=grid_spec,
        cost_estimate=pl.CostEstimate(
            flops=flops, transcendentals=0, bytes_accessed=vals.size * 2 + n_src * row_tiles * tile * width * 4
        ),
    )(rows, cols, count, core, vals, grad_tiles)


MESH_ID = pl.DeviceIdType.MESH


def weight_sum_kernel(n_grp, n_blk, x_ref, out_ref, part, grp_part, whole, sems):
    g = lax.axis_index("grp")
    b = lax.axis_index("blk")
    send1, recv1, send2, recv2, send3, recv3 = sems
    barrier = pltpu.get_barrier_semaphore()
    for i in range(1, n_blk):
        pl.semaphore_signal(barrier, 1, device_id=(g, (b + i) % n_blk), device_id_type=MESH_ID)
    for i in range(1, n_grp):
        pl.semaphore_signal(barrier, 1, device_id=((g + i) % n_grp, b), device_id_type=MESH_ID)
    pl.semaphore_wait(barrier, n_blk - 1 + n_grp - 1)

    def blk_copy(src, dst, send, recv, to, slot):
        return pltpu.make_async_remote_copy(
            src_ref=src, dst_ref=dst, send_sem=send.at[to], recv_sem=recv.at[slot],
            device_id=(g, to), device_id_type=MESH_ID,
        )

    def grp_copy(src, dst, send, recv, to, slot):
        return pltpu.make_async_remote_copy(
            src_ref=src, dst_ref=dst, send_sem=send.at[to], recv_sem=recv.at[slot],
            device_id=(to, b), device_id_type=MESH_ID,
        )

    out1 = []
    for i in range(1, n_blk):
        to = (b + i) % n_blk
        cp = blk_copy(x_ref.at[to], part.at[b], send1, recv1, to, b)
        cp.start()
        out1.append(cp)
    part[b] = x_ref[b]
    for i in range(1, n_blk):
        src = (b + n_blk - i) % n_blk
        blk_copy(x_ref.at[b], part.at[src], send1, recv1, src, src).wait_recv()
    for cp in out1:
        cp.wait_send()
    acc = part[0]
    for j in range(1, n_blk):
        acc = acc + part[j]
    grp_part[g] = acc

    out2 = []
    for i in range(1, n_grp):
        to = (g + i) % n_grp
        cp = grp_copy(grp_part.at[g], grp_part.at[g], send2, recv2, to, g)
        cp.start()
        out2.append(cp)
    for i in range(1, n_grp):
        src = (g + n_grp - i) % n_grp
        grp_copy(grp_part.at[src], grp_part.at[src], send2, recv2, src, src).wait_recv()
    for cp in out2:
        cp.wait_send()
    acc = grp_part[0]
    for j in range(1, n_grp):
        acc = acc + grp_part[j]
    whole[b] = acc

    out3 = []
    for i in range(1, n_blk):
        to = (b + i) % n_blk
        cp = blk_copy(whole.at[b], whole.at[b], send3, recv3, to, b)
        cp.start()
        out3.append(cp)
    for i in range(1, n_blk):
        src = (b + n_blk - i) % n_blk
        blk_copy(whole.at[src], whole.at[src], send3, recv3, src, src).wait_recv()
    for cp in out3:
        cp.wait_send()
    out_ref[...] = whole[...]


def weight_sum(term, n_grp, n_blk):
    rows, cols = term.shape
    chunk = rows * cols // (n_blk * 128)
    x = term.reshape(n_blk, chunk, 128)
    vmem = pl.BlockSpec(memory_space=pltpu.VMEM)
    out = pl.pallas_call(
        functools.partial(weight_sum_kernel, n_grp, n_blk),
        out_shape=jax.ShapeDtypeStruct(x.shape, jnp.float32),
        in_specs=[vmem],
        out_specs=vmem,
        scratch_shapes=[
            pltpu.VMEM(x.shape, jnp.float32),
            pltpu.VMEM((n_grp, chunk, 128), jnp.float32),
            pltpu.VMEM(x.shape, jnp.float32),
            [pltpu.SemaphoreType.DMA((n_blk,)), pltpu.SemaphoreType.DMA((n_blk,)),
             pltpu.SemaphoreType.DMA((n_grp,)), pltpu.SemaphoreType.DMA((n_grp,)),
             pltpu.SemaphoreType.DMA((n_blk,)), pltpu.SemaphoreType.DMA((n_blk,))],
        ],
        compiler_params=pltpu.CompilerParams(collective_id=0, has_side_effects=True),
    )(x)
    return out.reshape(rows, cols)


def exchange_kernel(n_blk, by_dest, src_ref, out_ref, send, recv, own):
    g = lax.axis_index("grp")
    b = lax.axis_index("blk")
    barrier = pltpu.get_barrier_semaphore()
    for i in range(1, n_blk):
        pl.semaphore_signal(barrier, 1, device_id=(g, (b + i) % n_blk), device_id_type=MESH_ID)
    pl.semaphore_wait(barrier, n_blk - 1)

    def piece(to):
        return src_ref.at[to] if by_dest else src_ref

    def remote(to, slot):
        return pltpu.make_async_remote_copy(
            src_ref=piece(to), dst_ref=out_ref.at[slot], send_sem=send.at[to], recv_sem=recv.at[slot],
            device_id=(g, to), device_id_type=MESH_ID,
        )

    local = pltpu.make_async_copy(piece(b), out_ref.at[b], own)
    local.start()
    sent = []
    for i in range(1, n_blk):
        cp = remote((b + i) % n_blk, b)
        cp.start()
        sent.append(cp)
    for i in range(1, n_blk):
        src = (b + n_blk - i) % n_blk
        remote(src, src).wait_recv()
    for cp in sent:
        cp.wait_send()
    local.wait()


def exchange(src, n_blk, by_dest, collective):
    shape = src.shape[1:] if by_dest else src.shape
    any_space = pl.BlockSpec(memory_space=pl.ANY)
    return pl.pallas_call(
        functools.partial(exchange_kernel, n_blk, by_dest),
        out_shape=jax.ShapeDtypeStruct((n_blk,) + shape, src.dtype),
        in_specs=[any_space],
        out_specs=any_space,
        scratch_shapes=[
            pltpu.SemaphoreType.DMA((n_blk,)),
            pltpu.SemaphoreType.DMA((n_blk,)),
            pltpu.SemaphoreType.DMA,
        ],
        compiler_params=pltpu.CompilerParams(collective_id=collective, has_side_effects=True),
    )(src)


def local(
    feats,
    weight,
    cotangent,
    labels,
    tile_vals,
    tile_row,
    tile_col,
    tile_count,
    hub_vals,
    hub_col,
    hub_dest,
    hub_row,
):
    n_blocks = lax.axis_size("blk")
    n_groups = lax.axis_size("grp")
    my_group = lax.axis_index("grp")
    rows_dev = feats.shape[0]
    width = feats.shape[1]
    tile_size = tile_vals.shape[-1]
    row_tiles = rows_dev // tile_size
    hub_count = hub_vals.shape[2]
    capacity = max(2, hub_count // 4)
    highest = lax.Precision.HIGHEST
    dev_vals = tile_vals[0, 0]
    dev_rows = tile_row[0, 0].reshape(-1)
    dev_cols = tile_col[0, 0].reshape(-1)
    dev_count = tile_count[0, 0]
    tile_range = jnp.arange(row_tiles, dtype=jnp.int32)
    proj = jnp.dot(feats, weight, preferred_element_type=jnp.float32).astype(jnp.bfloat16)
    own_panel = proj.reshape(row_tiles, tile_size, width)

    core = lax.axis_index("blk") % 2
    core_groups = [[i for i in range(n_blocks) if i % 2 == k] for k in range(2)]
    sibling = [(i, i ^ 1) for i in range(n_blocks)]
    panels = lax.all_gather(proj, "blk", axis=0, tiled=True)
    panels = panels.reshape(n_blocks, row_tiles, tile_size, width)
    agg_sum = tile_forward(dev_rows, dev_cols, dev_count, dev_vals, panels)

    dest_all = hub_dest[:, 0, :, 0]
    hub_rows_all = hub_row[:, 0, :]
    hub_range = jnp.arange(hub_count, dtype=jnp.int32)
    earlier = hub_range[None, :] < hub_range[:, None]
    same_dest = dest_all[:, :, None] == dest_all[:, None, :]
    rank_all = jnp.sum((same_dest & earlier[None, :, :]).astype(jnp.int32), axis=-1)
    my_dest = lax.dynamic_index_in_dim(dest_all, my_group, 0, keepdims=False)
    my_rank = lax.dynamic_index_in_dim(rank_all, my_group, 0, keepdims=False)
    slot_of = my_dest * capacity + my_rank
    send_place = (
        slot_of[:, None] == jnp.arange(n_groups * capacity, dtype=jnp.int32)[None, :]
    ).astype(jnp.float32)
    hub_tiles = hub_vals[0, 0]
    hub_cols = hub_col[0, 0]
    hub_src = jnp.take(own_panel, hub_cols, axis=0)
    hub_part = jnp.einsum("hij,hjf->hif", hub_tiles, hub_src, preferred_element_type=jnp.float32)
    send_buf = jnp.einsum(
        "hs,hif->sif", send_place.astype(jnp.bfloat16), hub_part.astype(jnp.bfloat16),
        preferred_element_type=jnp.float32,
    ).astype(jnp.bfloat16)
    send_buf = send_buf.reshape(n_groups, capacity, tile_size, width)
    received = lax.all_to_all(send_buf, "grp", split_axis=0, concat_axis=0, tiled=True)
    chosen = (dest_all == my_group).astype(jnp.float32)
    slot_hot = (rank_all[..., None] == jnp.arange(capacity, dtype=jnp.int32)).astype(
        jnp.float32
    ) * chosen[..., None]
    row_hot = (hub_rows_all[..., None] == tile_range).astype(jnp.float32)
    routing = jnp.einsum("shc,shr->scr", slot_hot, row_hot, precision=highest)
    agg_sum = agg_sum + jnp.einsum(
        "scr,scif->rif", routing.astype(jnp.bfloat16), received, preferred_element_type=jnp.float32
    )
    agg_rows = agg_sum.reshape(rows_dev, width)
    layer_out = jax.nn.silu(agg_rows).astype(jnp.bfloat16)
    sigmoid_z = jax.nn.sigmoid(agg_rows)
    slope = sigmoid_z * (1.0 + agg_rows * (1.0 - sigmoid_z))
    keep = (labels >= 0).astype(jnp.float32)[:, None]
    grad_agg = (cotangent.astype(jnp.float32) * keep * slope).astype(jnp.bfloat16)
    grad_tiles = grad_agg.reshape(row_tiles, tile_size, width)

    keep, send = tile_backward(dev_rows, dev_cols, dev_count, dev_vals, grad_tiles, core.reshape(1))
    from_sibling = lax.ppermute(send, "blk", sibling)
    pair_sum = (keep + from_sibling).astype(jnp.bfloat16)
    received_parts = lax.all_to_all(
        pair_sum, "blk", split_axis=0, concat_axis=0, tiled=True, axis_index_groups=core_groups
    )
    grad_sum = jnp.sum(received_parts.astype(jnp.float32), axis=0)

    back_send = jnp.einsum(
        "scr,rif->scif",
        routing.astype(jnp.bfloat16),
        grad_tiles,
        preferred_element_type=jnp.float32,
    ).astype(jnp.bfloat16)
    back_recv = lax.all_to_all(back_send, "grp", split_axis=0, concat_axis=0, tiled=True)
    back_flat = back_recv.reshape(n_groups * capacity, tile_size, width)
    own_pick = jnp.einsum(
        "hs,sif->hif",
        send_place.astype(jnp.bfloat16),
        back_flat,
        preferred_element_type=jnp.float32,
    ).astype(jnp.bfloat16)
    hub_back = jnp.einsum("hij,hif->hjf", hub_tiles, own_pick, preferred_element_type=jnp.float32)
    col_hot = (hub_cols[:, None] == tile_range[None, :]).astype(jnp.float32)
    grad_sum = grad_sum + jnp.einsum("hr,hjf->rjf", col_hot, hub_back, precision=highest)
    grad_rows = grad_sum.reshape(rows_dev, width).astype(jnp.bfloat16)
    weight_term = lax.dot_general(
        feats, grad_rows, (((0,), (0,)), ((), ())), preferred_element_type=jnp.float32
    )
    grad_scale = 1.0 / math.sqrt(rows_dev * n_blocks * n_groups)
    grad_weight = weight_sum(weight_term, n_groups, n_blocks) * grad_scale
    grad_feats = lax.dot_general(
        grad_rows, weight, (((1,), (1,)), ((), ())), preferred_element_type=jnp.float32
    ).astype(jnp.bfloat16)
    return (layer_out, grad_feats, grad_weight)


def solution(mesh):
    in_specs = (
        P(("grp", "blk"), None),
        P(),
        P(("grp", "blk"), None),
        P(("grp", "blk")),
        P("grp", "blk", None, None, None, None),
        P("grp", "blk", None, None),
        P("grp", "blk", None, None),
        P("grp", "blk", None),
        P("grp", "blk", None, None, None),
        P("grp", "blk", None),
        P(None, "blk", None, None),
        P(None, "blk", None),
    )
    out_specs = (P(("grp", "blk"), None), P(("grp", "blk"), None), P())
    return jax.shard_map(local, mesh=mesh, in_specs=in_specs, out_specs=out_specs, check_vma=False)
```

```python
import functools
import math

import jax
import jax.numpy as jnp
from jax import lax
from jax.experimental import pallas as pl
from jax.experimental.pallas import tpu as pltpu
from jax.sharding import PartitionSpec as P


UNROLL = 16


def grouped_slots(count, slots, visit):
    def body(g, carry):
        terms = []
        for j in range(UNROLL):
            t = g * UNROLL + j
            terms.append((t, t < count))
        visit(terms)
        return carry

    lax.fori_loop(0, (count + UNROLL - 1) // UNROLL, body, 0)


def clamp_tile(index, limit):
    return jnp.minimum(jnp.maximum(index, 0), limit - 1)


def forward_kernel(rows_ref, cols_ref, count_ref, vals_ref, panel_ref, out_ref):
    c = pl.program_id(0)
    slots = vals_ref.shape[1]
    row_tiles = out_ref.shape[0]

    @pl.when(c == 0)
    def _():
        out_ref[...] = jnp.zeros_like(out_ref)

    def visit(terms):
        parts = []
        for t, valid in terms:
            r = clamp_tile(rows_ref[c * slots + t], row_tiles)
            k = clamp_tile(cols_ref[c * slots + t], row_tiles)
            prod = jnp.dot(vals_ref[0, t], panel_ref[0, k], preferred_element_type=jnp.float32)
            parts.append((r, jnp.where(valid, prod, 0.0)))
        for r, prod in parts:
            out_ref[r] += prod

    grouped_slots(count_ref[c], slots, visit)


def backward_kernel(rows_ref, cols_ref, count_ref, core_ref, vals_ref, grad_ref, keep_ref, send_ref, acc_ref):
    i = pl.program_id(0)
    half = pl.num_programs(0) // 2
    p = i // half
    c = 2 * (i % half) + (p + core_ref[0]) % 2
    slots = vals_ref.shape[1]
    row_tiles = grad_ref.shape[0]
    acc_ref[...] = jnp.zeros_like(acc_ref)

    def visit(terms):
        parts = []
        for t, valid in terms:
            r = clamp_tile(rows_ref[c * slots + t], row_tiles)
            k = clamp_tile(cols_ref[c * slots + t], row_tiles)
            prod = lax.dot_general(
                vals_ref[0, t], grad_ref[r], (((0,), (0,)), ((), ())), preferred_element_type=jnp.float32
            )
            parts.append((k, jnp.where(valid, prod, 0.0)))
        for k, prod in parts:
            acc_ref[k] += prod

    grouped_slots(count_ref[c], slots, visit)

    @pl.when(p == 0)
    def _():
        keep_ref[0] = acc_ref[...]

    @pl.when(p == 1)
    def _():
        send_ref[0] = acc_ref[...]


def tile_forward(rows, cols, count, vals, panels):
    n_src, slots, tile, _ = vals.shape
    row_tiles, width = panels.shape[1], panels.shape[3]
    grid_spec = pltpu.PrefetchScalarGridSpec(
        num_scalar_prefetch=3,
        grid=(n_src,),
        in_specs=[
            pl.BlockSpec((1, slots, tile, tile), lambda c, *_: (c, 0, 0, 0)),
            pl.BlockSpec((1, row_tiles, tile, width), lambda c, *_: (c, 0, 0, 0)),
        ],
        out_specs=pl.BlockSpec((row_tiles, tile, width), lambda c, *_: (0, 0, 0)),
    )
    flops = 2 * n_src * slots * tile * tile * width
    return pl.pallas_call(
        forward_kernel,
        out_shape=jax.ShapeDtypeStruct((row_tiles, tile, width), jnp.float32),
        grid_spec=grid_spec,
        cost_estimate=pl.CostEstimate(
            flops=flops, transcendentals=0, bytes_accessed=vals.size * 2 + panels.size * 2
        ),
    )(rows, cols, count, vals, panels)


def tile_backward(rows, cols, count, vals, grad_tiles, core):
    n_src, slots, tile, _ = vals.shape
    row_tiles, width = grad_tiles.shape[0], grad_tiles.shape[2]
    half = n_src // 2

    def source(i, core_ref):
        return 2 * (i % half) + (i // half + core_ref[0]) % 2

    grid_spec = pltpu.PrefetchScalarGridSpec(
        num_scalar_prefetch=4,
        grid=(n_src,),
        in_specs=[
            pl.BlockSpec((1, slots, tile, tile), lambda i, r, k, n, core_ref: (source(i, core_ref), 0, 0, 0)),
            pl.BlockSpec((row_tiles, tile, width), lambda i, *_: (0, 0, 0)),
        ],
        out_specs=[
            pl.BlockSpec((1, row_tiles, tile, width), lambda i, *_: (jnp.minimum(i, half - 1), 0, 0, 0)),
            pl.BlockSpec((1, row_tiles, tile, width), lambda i, *_: (jnp.maximum(i - half, 0), 0, 0, 0)),
        ],
        scratch_shapes=[pltpu.VMEM((row_tiles, tile, width), jnp.float32)],
    )
    flops = 2 * n_src * slots * tile * tile * width
    part = jax.ShapeDtypeStruct((half, row_tiles, tile, width), jnp.float32)
    return pl.pallas_call(
        backward_kernel,
        out_shape=(part, part),
        grid_spec=grid_spec,
        cost_estimate=pl.CostEstimate(
            flops=flops, transcendentals=0, bytes_accessed=vals.size * 2 + n_src * row_tiles * tile * width * 4
        ),
    )(rows, cols, count, core, vals, grad_tiles)


MESH_ID = pl.DeviceIdType.MESH


def weight_sum_kernel(n_grp, n_blk, x_ref, out_ref, part, grp_part, whole, sems):
    g = lax.axis_index("grp")
    b = lax.axis_index("blk")
    send1, recv1, send2, recv2, send3, recv3 = sems
    barrier = pltpu.get_barrier_semaphore()
    for i in range(1, n_blk):
        pl.semaphore_signal(barrier, 1, device_id=(g, (b + i) % n_blk), device_id_type=MESH_ID)
    for i in range(1, n_grp):
        pl.semaphore_signal(barrier, 1, device_id=((g + i) % n_grp, b), device_id_type=MESH_ID)
    pl.semaphore_wait(barrier, n_blk - 1 + n_grp - 1)

    def blk_copy(src, dst, send, recv, to, slot):
        return pltpu.make_async_remote_copy(
            src_ref=src, dst_ref=dst, send_sem=send.at[to], recv_sem=recv.at[slot],
            device_id=(g, to), device_id_type=MESH_ID,
        )

    def grp_copy(src, dst, send, recv, to, slot):
        return pltpu.make_async_remote_copy(
            src_ref=src, dst_ref=dst, send_sem=send.at[to], recv_sem=recv.at[slot],
            device_id=(to, b), device_id_type=MESH_ID,
        )

    out1 = []
    for i in range(1, n_blk):
        to = (b + i) % n_blk
        cp = blk_copy(x_ref.at[to], part.at[b], send1, recv1, to, b)
        cp.start()
        out1.append(cp)
    part[b] = x_ref[b]
    for i in range(1, n_blk):
        src = (b + n_blk - i) % n_blk
        blk_copy(x_ref.at[b], part.at[src], send1, recv1, src, src).wait_recv()
    for cp in out1:
        cp.wait_send()
    acc = part[0]
    for j in range(1, n_blk):
        acc = acc + part[j]
    grp_part[g] = acc

    out2 = []
    for i in range(1, n_grp):
        to = (g + i) % n_grp
        cp = grp_copy(grp_part.at[g], grp_part.at[g], send2, recv2, to, g)
        cp.start()
        out2.append(cp)
    for i in range(1, n_grp):
        src = (g + n_grp - i) % n_grp
        grp_copy(grp_part.at[src], grp_part.at[src], send2, recv2, src, src).wait_recv()
    for cp in out2:
        cp.wait_send()
    acc = grp_part[0]
    for j in range(1, n_grp):
        acc = acc + grp_part[j]
    whole[b] = acc

    out3 = []
    for i in range(1, n_blk):
        to = (b + i) % n_blk
        cp = blk_copy(whole.at[b], whole.at[b], send3, recv3, to, b)
        cp.start()
        out3.append(cp)
    for i in range(1, n_blk):
        src = (b + n_blk - i) % n_blk
        blk_copy(whole.at[src], whole.at[src], send3, recv3, src, src).wait_recv()
    for cp in out3:
        cp.wait_send()
    out_ref[...] = whole[...]


def weight_sum(term, n_grp, n_blk):
    rows, cols = term.shape
    chunk = rows * cols // (n_blk * 128)
    x = term.reshape(n_blk, chunk, 128)
    vmem = pl.BlockSpec(memory_space=pltpu.VMEM)
    out = pl.pallas_call(
        functools.partial(weight_sum_kernel, n_grp, n_blk),
        out_shape=jax.ShapeDtypeStruct(x.shape, jnp.float32),
        in_specs=[vmem],
        out_specs=vmem,
        scratch_shapes=[
            pltpu.VMEM(x.shape, jnp.float32),
            pltpu.VMEM((n_grp, chunk, 128), jnp.float32),
            pltpu.VMEM(x.shape, jnp.float32),
            [pltpu.SemaphoreType.DMA((n_blk,)), pltpu.SemaphoreType.DMA((n_blk,)),
             pltpu.SemaphoreType.DMA((n_grp,)), pltpu.SemaphoreType.DMA((n_grp,)),
             pltpu.SemaphoreType.DMA((n_blk,)), pltpu.SemaphoreType.DMA((n_blk,))],
        ],
        compiler_params=pltpu.CompilerParams(collective_id=0, has_side_effects=True),
    )(x)
    return out.reshape(rows, cols)


def exchange_kernel(n_blk, by_dest, src_ref, out_ref, send, recv, own):
    g = lax.axis_index("grp")
    b = lax.axis_index("blk")
    barrier = pltpu.get_barrier_semaphore()
    for i in range(1, n_blk):
        pl.semaphore_signal(barrier, 1, device_id=(g, (b + i) % n_blk), device_id_type=MESH_ID)
    pl.semaphore_wait(barrier, n_blk - 1)

    def piece(to):
        return src_ref.at[to] if by_dest else src_ref

    def remote(to, slot):
        return pltpu.make_async_remote_copy(
            src_ref=piece(to), dst_ref=out_ref.at[slot], send_sem=send.at[to], recv_sem=recv.at[slot],
            device_id=(g, to), device_id_type=MESH_ID,
        )

    local = pltpu.make_async_copy(piece(b), out_ref.at[b], own)
    local.start()
    sent = []
    for i in range(1, n_blk):
        cp = remote((b + i) % n_blk, b)
        cp.start()
        sent.append(cp)
    for i in range(1, n_blk):
        src = (b + n_blk - i) % n_blk
        remote(src, src).wait_recv()
    for cp in sent:
        cp.wait_send()
    local.wait()


def exchange(src, n_blk, by_dest, collective):
    shape = src.shape[1:] if by_dest else src.shape
    any_space = pl.BlockSpec(memory_space=pl.ANY)
    return pl.pallas_call(
        functools.partial(exchange_kernel, n_blk, by_dest),
        out_shape=jax.ShapeDtypeStruct((n_blk,) + shape, src.dtype),
        in_specs=[any_space],
        out_specs=any_space,
        scratch_shapes=[
            pltpu.SemaphoreType.DMA((n_blk,)),
            pltpu.SemaphoreType.DMA((n_blk,)),
            pltpu.SemaphoreType.DMA,
        ],
        compiler_params=pltpu.CompilerParams(collective_id=collective, has_side_effects=True),
    )(src)


def local(
    feats,
    weight,
    cotangent,
    labels,
    tile_vals,
    tile_row,
    tile_col,
    tile_count,
    hub_vals,
    hub_col,
    hub_dest,
    hub_row,
):
    n_blocks = lax.axis_size("blk")
    n_groups = lax.axis_size("grp")
    my_group = lax.axis_index("grp")
    rows_dev = feats.shape[0]
    width = feats.shape[1]
    tile_size = tile_vals.shape[-1]
    row_tiles = rows_dev // tile_size
    hub_count = hub_vals.shape[2]
    capacity = max(2, hub_count // 4)
    highest = lax.Precision.HIGHEST
    dev_vals = tile_vals[0, 0]
    dev_rows = tile_row[0, 0].reshape(-1)
    dev_cols = tile_col[0, 0].reshape(-1)
    dev_count = tile_count[0, 0]
    tile_range = jnp.arange(row_tiles, dtype=jnp.int32)
    proj = jnp.dot(feats, weight, preferred_element_type=jnp.float32).astype(jnp.bfloat16)
    own_panel = proj.reshape(row_tiles, tile_size, width)

    core = lax.axis_index("blk") % 2
    core_groups = [[i for i in range(n_blocks) if i % 2 == k] for k in range(2)]
    sibling = [(i, i ^ 1) for i in range(n_blocks)]
    panels = lax.all_gather(proj, "blk", axis=0, tiled=True)
    panels = panels.reshape(n_blocks, row_tiles, tile_size, width)
    agg_sum = tile_forward(dev_rows, dev_cols, dev_count, dev_vals, panels)

    dest_all = hub_dest[:, 0, :, 0]
    hub_rows_all = hub_row[:, 0, :]
    hub_range = jnp.arange(hub_count, dtype=jnp.int32)
    earlier = hub_range[None, :] < hub_range[:, None]
    same_dest = dest_all[:, :, None] == dest_all[:, None, :]
    rank_all = jnp.sum((same_dest & earlier[None, :, :]).astype(jnp.int32), axis=-1)
    my_dest = lax.dynamic_index_in_dim(dest_all, my_group, 0, keepdims=False)
    my_rank = lax.dynamic_index_in_dim(rank_all, my_group, 0, keepdims=False)
    slot_of = my_dest * capacity + my_rank
    send_place = (
        slot_of[:, None] == jnp.arange(n_groups * capacity, dtype=jnp.int32)[None, :]
    ).astype(jnp.float32)
    hub_tiles = hub_vals[0, 0]
    hub_cols = hub_col[0, 0]
    hub_src = jnp.take(own_panel, hub_cols, axis=0)
    hub_part = jnp.einsum("hij,hjf->hif", hub_tiles, hub_src, preferred_element_type=jnp.float32)
    send_buf = jnp.einsum(
        "hs,hif->sif", send_place.astype(jnp.bfloat16), hub_part.astype(jnp.bfloat16),
        preferred_element_type=jnp.float32,
    ).astype(jnp.bfloat16)
    send_buf = send_buf.reshape(n_groups, capacity, tile_size, width)
    received = lax.all_to_all(send_buf, "grp", split_axis=0, concat_axis=0, tiled=True)
    chosen = (dest_all == my_group).astype(jnp.float32)
    slot_hot = (rank_all[..., None] == jnp.arange(capacity, dtype=jnp.int32)).astype(
        jnp.float32
    ) * chosen[..., None]
    row_hot = (hub_rows_all[..., None] == tile_range).astype(jnp.float32)
    routing = jnp.einsum("shc,shr->scr", slot_hot, row_hot, precision=highest)
    agg_sum = agg_sum + jnp.einsum(
        "scr,scif->rif", routing.astype(jnp.bfloat16), received, preferred_element_type=jnp.float32
    )
    agg_rows = agg_sum.reshape(rows_dev, width)
    layer_out = jax.nn.silu(agg_rows).astype(jnp.bfloat16)
    sigmoid_z = jax.nn.sigmoid(agg_rows)
    slope = sigmoid_z * (1.0 + agg_rows * (1.0 - sigmoid_z))
    keep = (labels >= 0).astype(jnp.float32)[:, None]
    grad_agg = (cotangent.astype(jnp.float32) * keep * slope).astype(jnp.bfloat16)
    grad_tiles = grad_agg.reshape(row_tiles, tile_size, width)

    keep, send = tile_backward(dev_rows, dev_cols, dev_count, dev_vals, grad_tiles, core.reshape(1))
    from_sibling = lax.ppermute(send, "blk", sibling)
    pair_sum = (keep + from_sibling).astype(jnp.bfloat16)
    received_parts = lax.all_to_all(
        pair_sum, "blk", split_axis=0, concat_axis=0, tiled=True, axis_index_groups=core_groups
    )
    grad_sum = jnp.sum(received_parts.astype(jnp.float32), axis=0)

    back_send = jnp.einsum(
        "scr,rif->scif",
        routing.astype(jnp.bfloat16),
        grad_tiles,
        preferred_element_type=jnp.float32,
    ).astype(jnp.bfloat16)
    back_recv = lax.all_to_all(back_send, "grp", split_axis=0, concat_axis=0, tiled=True)
    back_flat = back_recv.reshape(n_groups * capacity, tile_size, width)
    own_pick = jnp.einsum(
        "hs,sif->hif",
        send_place.astype(jnp.bfloat16),
        back_flat,
        preferred_element_type=jnp.float32,
    ).astype(jnp.bfloat16)
    hub_back = jnp.einsum("hij,hif->hjf", hub_tiles, own_pick, preferred_element_type=jnp.float32)
    col_hot = (hub_cols[:, None] == tile_range[None, :]).astype(jnp.float32)
    grad_sum = grad_sum + jnp.einsum("hr,hjf->rjf", col_hot, hub_back, precision=highest)
    grad_rows = grad_sum.reshape(rows_dev, width).astype(jnp.bfloat16)
    weight_term = lax.dot_general(
        feats, grad_rows, (((0,), (0,)), ((), ())), preferred_element_type=jnp.float32
    )
    grad_scale = 1.0 / math.sqrt(rows_dev * n_blocks * n_groups)
    grad_weight = weight_sum(weight_term, n_groups, n_blocks) * grad_scale
    grad_feats = lax.dot_general(
        grad_rows, weight, (((1,), (1,)), ((), ())), preferred_element_type=jnp.float32
    ).astype(jnp.bfloat16)
    return (layer_out, grad_feats, grad_weight)


def solution(mesh):
    in_specs = (
        P(("grp", "blk"), None),
        P(),
        P(("grp", "blk"), None),
        P(("grp", "blk")),
        P("grp", "blk", None, None, None, None),
        P("grp", "blk", None, None),
        P("grp", "blk", None, None),
        P("grp", "blk", None),
        P("grp", "blk", None, None, None),
        P("grp", "blk", None),
        P(None, "blk", None, None),
        P(None, "blk", None),
    )
    out_specs = (P(("grp", "blk"), None), P(("grp", "blk"), None), P())
    return jax.shard_map(local, mesh=mesh, in_specs=in_specs, out_specs=out_specs, check_vma=False)
```

```python
import functools
import math

import jax
import jax.numpy as jnp
from jax import lax
from jax.experimental import pallas as pl
from jax.experimental.pallas import tpu as pltpu
from jax.sharding import PartitionSpec as P


UNROLL = 16


def grouped_slots(count, slots, visit):
    def body(g, carry):
        terms = []
        for j in range(UNROLL):
            t = g * UNROLL + j
            terms.append((t, t < count))
        visit(terms)
        return carry

    lax.fori_loop(0, (count + UNROLL - 1) // UNROLL, body, 0)


def clamp_tile(index, limit):
    return jnp.minimum(jnp.maximum(index, 0), limit - 1)


def forward_kernel(rows_ref, cols_ref, count_ref, vals_ref, panel_ref, out_ref):
    c = pl.program_id(0)
    slots = vals_ref.shape[1]
    row_tiles = out_ref.shape[0]

    @pl.when(c == 0)
    def _():
        out_ref[...] = jnp.zeros_like(out_ref)

    def visit(terms):
        parts = []
        for t, valid in terms:
            r = clamp_tile(rows_ref[c * slots + t], row_tiles)
            k = clamp_tile(cols_ref[c * slots + t], row_tiles)
            prod = jnp.dot(vals_ref[0, t], panel_ref[0, k], preferred_element_type=jnp.float32)
            parts.append((r, jnp.where(valid, prod, 0.0)))
        for r, prod in parts:
            out_ref[r] += prod

    grouped_slots(count_ref[c], slots, visit)


def backward_kernel(rows_ref, cols_ref, count_ref, core_ref, vals_ref, grad_ref, keep_ref, send_ref, acc_ref):
    i = pl.program_id(0)
    half = pl.num_programs(0) // 2
    p = i // half
    c = 2 * (i % half) + (p + core_ref[0]) % 2
    slots = vals_ref.shape[1]
    row_tiles = grad_ref.shape[0]
    acc_ref[...] = jnp.zeros_like(acc_ref)

    def visit(terms):
        parts = []
        for t, valid in terms:
            r = clamp_tile(rows_ref[c * slots + t], row_tiles)
            k = clamp_tile(cols_ref[c * slots + t], row_tiles)
            prod = lax.dot_general(
                vals_ref[0, t], grad_ref[r], (((0,), (0,)), ((), ())), preferred_element_type=jnp.float32
            )
            parts.append((k, jnp.where(valid, prod, 0.0)))
        for k, prod in parts:
            acc_ref[k] += prod

    grouped_slots(count_ref[c], slots, visit)

    @pl.when(p == 0)
    def _():
        keep_ref[0] = acc_ref[...]

    @pl.when(p == 1)
    def _():
        send_ref[0] = acc_ref[...].astype(send_ref.dtype)


def tile_forward(rows, cols, count, vals, panels):
    n_src, slots, tile, _ = vals.shape
    row_tiles, width = panels.shape[1], panels.shape[3]
    grid_spec = pltpu.PrefetchScalarGridSpec(
        num_scalar_prefetch=3,
        grid=(n_src,),
        in_specs=[
            pl.BlockSpec((1, slots, tile, tile), lambda c, *_: (c, 0, 0, 0)),
            pl.BlockSpec((1, row_tiles, tile, width), lambda c, *_: (c, 0, 0, 0)),
        ],
        out_specs=pl.BlockSpec((row_tiles, tile, width), lambda c, *_: (0, 0, 0)),
    )
    flops = 2 * n_src * slots * tile * tile * width
    return pl.pallas_call(
        forward_kernel,
        out_shape=jax.ShapeDtypeStruct((row_tiles, tile, width), jnp.float32),
        grid_spec=grid_spec,
        cost_estimate=pl.CostEstimate(
            flops=flops, transcendentals=0, bytes_accessed=vals.size * 2 + panels.size * 2
        ),
    )(rows, cols, count, vals, panels)


def tile_backward(rows, cols, count, vals, grad_tiles, core):
    n_src, slots, tile, _ = vals.shape
    row_tiles, width = grad_tiles.shape[0], grad_tiles.shape[2]
    half = n_src // 2

    def source(i, core_ref):
        return 2 * (i % half) + (i // half + core_ref[0]) % 2

    grid_spec = pltpu.PrefetchScalarGridSpec(
        num_scalar_prefetch=4,
        grid=(n_src,),
        in_specs=[
            pl.BlockSpec((1, slots, tile, tile), lambda i, r, k, n, core_ref: (source(i, core_ref), 0, 0, 0)),
            pl.BlockSpec((row_tiles, tile, width), lambda i, *_: (0, 0, 0)),
        ],
        out_specs=[
            pl.BlockSpec((1, row_tiles, tile, width), lambda i, *_: (jnp.minimum(i, half - 1), 0, 0, 0)),
            pl.BlockSpec((1, row_tiles, tile, width), lambda i, *_: (jnp.maximum(i - half, 0), 0, 0, 0)),
        ],
        scratch_shapes=[pltpu.VMEM((row_tiles, tile, width), jnp.float32)],
    )
    flops = 2 * n_src * slots * tile * tile * width
    part = jax.ShapeDtypeStruct((half, row_tiles, tile, width), jnp.float32)
    part_out = jax.ShapeDtypeStruct((half, row_tiles, tile, width), jnp.bfloat16)
    return pl.pallas_call(
        backward_kernel,
        out_shape=(part, part_out),
        grid_spec=grid_spec,
        cost_estimate=pl.CostEstimate(
            flops=flops, transcendentals=0, bytes_accessed=vals.size * 2 + n_src * row_tiles * tile * width * 4
        ),
    )(rows, cols, count, core, vals, grad_tiles)


MESH_ID = pl.DeviceIdType.MESH


def weight_sum_kernel(n_grp, n_blk, x_ref, out_ref, part, grp_part, whole, sems):
    g = lax.axis_index("grp")
    b = lax.axis_index("blk")
    send1, recv1, send2, recv2, send3, recv3 = sems
    barrier = pltpu.get_barrier_semaphore()
    for i in range(1, n_blk):
        pl.semaphore_signal(barrier, 1, device_id=(g, (b + i) % n_blk), device_id_type=MESH_ID)
    for i in range(1, n_grp):
        pl.semaphore_signal(barrier, 1, device_id=((g + i) % n_grp, b), device_id_type=MESH_ID)
    pl.semaphore_wait(barrier, n_blk - 1 + n_grp - 1)

    def blk_copy(src, dst, send, recv, to, slot):
        return pltpu.make_async_remote_copy(
            src_ref=src, dst_ref=dst, send_sem=send.at[to], recv_sem=recv.at[slot],
            device_id=(g, to), device_id_type=MESH_ID,
        )

    def grp_copy(src, dst, send, recv, to, slot):
        return pltpu.make_async_remote_copy(
            src_ref=src, dst_ref=dst, send_sem=send.at[to], recv_sem=recv.at[slot],
            device_id=(to, b), device_id_type=MESH_ID,
        )

    out1 = []
    for i in range(1, n_blk):
        to = (b + i) % n_blk
        cp = blk_copy(x_ref.at[to], part.at[b], send1, recv1, to, b)
        cp.start()
        out1.append(cp)
    part[b] = x_ref[b]
    for i in range(1, n_blk):
        src = (b + n_blk - i) % n_blk
        blk_copy(x_ref.at[b], part.at[src], send1, recv1, src, src).wait_recv()
    for cp in out1:
        cp.wait_send()
    acc = part[0]
    for j in range(1, n_blk):
        acc = acc + part[j]
    grp_part[g] = acc

    out2 = []
    for i in range(1, n_grp):
        to = (g + i) % n_grp
        cp = grp_copy(grp_part.at[g], grp_part.at[g], send2, recv2, to, g)
        cp.start()
        out2.append(cp)
    for i in range(1, n_grp):
        src = (g + n_grp - i) % n_grp
        grp_copy(grp_part.at[src], grp_part.at[src], send2, recv2, src, src).wait_recv()
    for cp in out2:
        cp.wait_send()
    acc = grp_part[0]
    for j in range(1, n_grp):
        acc = acc + grp_part[j]
    whole[b] = acc

    out3 = []
    for i in range(1, n_blk):
        to = (b + i) % n_blk
        cp = blk_copy(whole.at[b], whole.at[b], send3, recv3, to, b)
        cp.start()
        out3.append(cp)
    for i in range(1, n_blk):
        src = (b + n_blk - i) % n_blk
        blk_copy(whole.at[src], whole.at[src], send3, recv3, src, src).wait_recv()
    for cp in out3:
        cp.wait_send()
    out_ref[...] = whole[...]


def weight_sum(term, n_grp, n_blk):
    rows, cols = term.shape
    chunk = rows * cols // (n_blk * 128)
    x = term.reshape(n_blk, chunk, 128)
    vmem = pl.BlockSpec(memory_space=pltpu.VMEM)
    out = pl.pallas_call(
        functools.partial(weight_sum_kernel, n_grp, n_blk),
        out_shape=jax.ShapeDtypeStruct(x.shape, jnp.float32),
        in_specs=[vmem],
        out_specs=vmem,
        scratch_shapes=[
            pltpu.VMEM(x.shape, jnp.float32),
            pltpu.VMEM((n_grp, chunk, 128), jnp.float32),
            pltpu.VMEM(x.shape, jnp.float32),
            [pltpu.SemaphoreType.DMA((n_blk,)), pltpu.SemaphoreType.DMA((n_blk,)),
             pltpu.SemaphoreType.DMA((n_grp,)), pltpu.SemaphoreType.DMA((n_grp,)),
             pltpu.SemaphoreType.DMA((n_blk,)), pltpu.SemaphoreType.DMA((n_blk,))],
        ],
        compiler_params=pltpu.CompilerParams(collective_id=0, has_side_effects=True),
    )(x)
    return out.reshape(rows, cols)


def exchange_kernel(n_blk, by_dest, src_ref, out_ref, send, recv, own):
    g = lax.axis_index("grp")
    b = lax.axis_index("blk")
    barrier = pltpu.get_barrier_semaphore()
    for i in range(1, n_blk):
        pl.semaphore_signal(barrier, 1, device_id=(g, (b + i) % n_blk), device_id_type=MESH_ID)
    pl.semaphore_wait(barrier, n_blk - 1)

    def piece(to):
        return src_ref.at[to] if by_dest else src_ref

    def remote(to, slot):
        return pltpu.make_async_remote_copy(
            src_ref=piece(to), dst_ref=out_ref.at[slot], send_sem=send.at[to], recv_sem=recv.at[slot],
            device_id=(g, to), device_id_type=MESH_ID,
        )

    local = pltpu.make_async_copy(piece(b), out_ref.at[b], own)
    local.start()
    sent = []
    for i in range(1, n_blk):
        cp = remote((b + i) % n_blk, b)
        cp.start()
        sent.append(cp)
    for i in range(1, n_blk):
        src = (b + n_blk - i) % n_blk
        remote(src, src).wait_recv()
    for cp in sent:
        cp.wait_send()
    local.wait()


def exchange(src, n_blk, by_dest, collective):
    shape = src.shape[1:] if by_dest else src.shape
    any_space = pl.BlockSpec(memory_space=pl.ANY)
    return pl.pallas_call(
        functools.partial(exchange_kernel, n_blk, by_dest),
        out_shape=jax.ShapeDtypeStruct((n_blk,) + shape, src.dtype),
        in_specs=[any_space],
        out_specs=any_space,
        scratch_shapes=[
            pltpu.SemaphoreType.DMA((n_blk,)),
            pltpu.SemaphoreType.DMA((n_blk,)),
            pltpu.SemaphoreType.DMA,
        ],
        compiler_params=pltpu.CompilerParams(collective_id=collective, has_side_effects=True),
    )(src)


def local(
    feats,
    weight,
    cotangent,
    labels,
    tile_vals,
    tile_row,
    tile_col,
    tile_count,
    hub_vals,
    hub_col,
    hub_dest,
    hub_row,
):
    n_blocks = lax.axis_size("blk")
    n_groups = lax.axis_size("grp")
    my_group = lax.axis_index("grp")
    rows_dev = feats.shape[0]
    width = feats.shape[1]
    tile_size = tile_vals.shape[-1]
    row_tiles = rows_dev // tile_size
    hub_count = hub_vals.shape[2]
    capacity = max(2, hub_count // 4)
    highest = lax.Precision.HIGHEST
    dev_vals = tile_vals[0, 0]
    dev_rows = tile_row[0, 0].reshape(-1)
    dev_cols = tile_col[0, 0].reshape(-1)
    dev_count = tile_count[0, 0]
    tile_range = jnp.arange(row_tiles, dtype=jnp.int32)
    proj = jnp.dot(feats, weight, preferred_element_type=jnp.float32).astype(jnp.bfloat16)
    own_panel = proj.reshape(row_tiles, tile_size, width)

    core = lax.axis_index("blk") % 2
    core_groups = [[i for i in range(n_blocks) if i % 2 == k] for k in range(2)]
    sibling = [(i, i ^ 1) for i in range(n_blocks)]
    panels = lax.all_gather(proj, "blk", axis=0, tiled=True)
    panels = panels.reshape(n_blocks, row_tiles, tile_size, width)
    agg_sum = tile_forward(dev_rows, dev_cols, dev_count, dev_vals, panels)

    dest_all = hub_dest[:, 0, :, 0]
    hub_rows_all = hub_row[:, 0, :]
    hub_range = jnp.arange(hub_count, dtype=jnp.int32)
    earlier = hub_range[None, :] < hub_range[:, None]
    same_dest = dest_all[:, :, None] == dest_all[:, None, :]
    rank_all = jnp.sum((same_dest & earlier[None, :, :]).astype(jnp.int32), axis=-1)
    my_dest = lax.dynamic_index_in_dim(dest_all, my_group, 0, keepdims=False)
    my_rank = lax.dynamic_index_in_dim(rank_all, my_group, 0, keepdims=False)
    slot_of = my_dest * capacity + my_rank
    send_place = (
        slot_of[:, None] == jnp.arange(n_groups * capacity, dtype=jnp.int32)[None, :]
    ).astype(jnp.float32)
    hub_tiles = hub_vals[0, 0]
    hub_cols = hub_col[0, 0]
    hub_src = jnp.take(own_panel, hub_cols, axis=0)
    hub_part = jnp.einsum("hij,hjf->hif", hub_tiles, hub_src, preferred_element_type=jnp.float32)
    send_buf = jnp.einsum(
        "hs,hif->sif", send_place.astype(jnp.bfloat16), hub_part.astype(jnp.bfloat16),
        preferred_element_type=jnp.float32,
    ).astype(jnp.bfloat16)
    send_buf = send_buf.reshape(n_groups, capacity, tile_size, width)
    received = lax.all_to_all(send_buf, "grp", split_axis=0, concat_axis=0, tiled=True)
    chosen = (dest_all == my_group).astype(jnp.float32)
    slot_hot = (rank_all[..., None] == jnp.arange(capacity, dtype=jnp.int32)).astype(
        jnp.float32
    ) * chosen[..., None]
    row_hot = (hub_rows_all[..., None] == tile_range).astype(jnp.float32)
    routing = jnp.einsum("shc,shr->scr", slot_hot, row_hot, precision=highest)
    agg_sum = agg_sum + jnp.einsum(
        "scr,scif->rif", routing.astype(jnp.bfloat16), received, preferred_element_type=jnp.float32
    )
    agg_rows = agg_sum.reshape(rows_dev, width)
    layer_out = jax.nn.silu(agg_rows).astype(jnp.bfloat16)
    sigmoid_z = jax.nn.sigmoid(agg_rows)
    slope = sigmoid_z * (1.0 + agg_rows * (1.0 - sigmoid_z))
    keep = (labels >= 0).astype(jnp.float32)[:, None]
    grad_agg = (cotangent.astype(jnp.float32) * keep * slope).astype(jnp.bfloat16)
    grad_tiles = grad_agg.reshape(row_tiles, tile_size, width)

    keep, send = tile_backward(dev_rows, dev_cols, dev_count, dev_vals, grad_tiles, core.reshape(1))
    from_sibling = lax.ppermute(send, "blk", sibling)
    pair_sum = (keep + from_sibling.astype(jnp.float32)).astype(jnp.bfloat16)
    received_parts = lax.all_to_all(
        pair_sum, "blk", split_axis=0, concat_axis=0, tiled=True, axis_index_groups=core_groups
    )
    grad_sum = jnp.sum(received_parts.astype(jnp.float32), axis=0)

    back_send = jnp.einsum(
        "scr,rif->scif",
        routing.astype(jnp.bfloat16),
        grad_tiles,
        preferred_element_type=jnp.float32,
    ).astype(jnp.bfloat16)
    back_recv = lax.all_to_all(back_send, "grp", split_axis=0, concat_axis=0, tiled=True)
    back_flat = back_recv.reshape(n_groups * capacity, tile_size, width)
    own_pick = jnp.einsum(
        "hs,sif->hif",
        send_place.astype(jnp.bfloat16),
        back_flat,
        preferred_element_type=jnp.float32,
    ).astype(jnp.bfloat16)
    hub_back = jnp.einsum("hij,hif->hjf", hub_tiles, own_pick, preferred_element_type=jnp.float32)
    col_hot = (hub_cols[:, None] == tile_range[None, :]).astype(jnp.float32)
    grad_sum = grad_sum + jnp.einsum("hr,hjf->rjf", col_hot, hub_back, precision=highest)
    grad_rows = grad_sum.reshape(rows_dev, width).astype(jnp.bfloat16)
    weight_term = lax.dot_general(
        feats, grad_rows, (((0,), (0,)), ((), ())), preferred_element_type=jnp.float32
    )
    grad_scale = 1.0 / math.sqrt(rows_dev * n_blocks * n_groups)
    grad_weight = weight_sum(weight_term, n_groups, n_blocks) * grad_scale
    grad_feats = lax.dot_general(
        grad_rows, weight, (((1,), (1,)), ((), ())), preferred_element_type=jnp.float32
    ).astype(jnp.bfloat16)
    return (layer_out, grad_feats, grad_weight)


def solution(mesh):
    in_specs = (
        P(("grp", "blk"), None),
        P(),
        P(("grp", "blk"), None),
        P(("grp", "blk")),
        P("grp", "blk", None, None, None, None),
        P("grp", "blk", None, None),
        P("grp", "blk", None, None),
        P("grp", "blk", None),
        P("grp", "blk", None, None, None),
        P("grp", "blk", None),
        P(None, "blk", None, None),
        P(None, "blk", None),
    )
    out_specs = (P(("grp", "blk"), None), P(("grp", "blk"), None), P())
    return jax.shard_map(local, mesh=mesh, in_specs=in_specs, out_specs=out_specs, check_vma=False)
```

```python
import functools
import math

import jax
import jax.numpy as jnp
from jax import lax
from jax.experimental import pallas as pl
from jax.experimental.pallas import tpu as pltpu
from jax.sharding import PartitionSpec as P


UNROLL = 16


def grouped_slots(count, slots, visit):
    def body(g, carry):
        terms = []
        for j in range(UNROLL):
            t = g * UNROLL + j
            terms.append((t, t < count))
        visit(terms)
        return carry

    lax.fori_loop(0, (count + UNROLL - 1) // UNROLL, body, 0)


def clamp_tile(index, limit):
    return jnp.minimum(jnp.maximum(index, 0), limit - 1)


def forward_kernel(rows_ref, cols_ref, count_ref, vals_ref, panel_ref, out_ref):
    c = pl.program_id(0)
    slots = vals_ref.shape[1]
    row_tiles = out_ref.shape[0]

    @pl.when(c == 0)
    def _():
        out_ref[...] = jnp.zeros_like(out_ref)

    def visit(terms):
        parts = []
        for t, valid in terms:
            r = clamp_tile(rows_ref[c * slots + t], row_tiles)
            k = clamp_tile(cols_ref[c * slots + t], row_tiles)
            prod = jnp.dot(vals_ref[0, t], panel_ref[0, k], preferred_element_type=jnp.float32)
            parts.append((r, jnp.where(valid, prod, 0.0)))
        for r, prod in parts:
            out_ref[r] += prod

    grouped_slots(count_ref[c], slots, visit)


def backward_kernel(rows_ref, cols_ref, count_ref, core_ref, vals_ref, grad_ref, keep_ref, send_ref, acc_ref):
    i = pl.program_id(0)
    half = pl.num_programs(0) // 2
    p = i // half
    c = 2 * (i % half) + (p + core_ref[0]) % 2
    slots = vals_ref.shape[1]
    row_tiles = grad_ref.shape[0]
    acc_ref[...] = jnp.zeros_like(acc_ref)

    def visit(terms):
        parts = []
        for t, valid in terms:
            r = clamp_tile(rows_ref[c * slots + t], row_tiles)
            k = clamp_tile(cols_ref[c * slots + t], row_tiles)
            prod = lax.dot_general(
                vals_ref[0, t], grad_ref[r], (((0,), (0,)), ((), ())), preferred_element_type=jnp.float32
            )
            parts.append((k, jnp.where(valid, prod, 0.0)))
        for k, prod in parts:
            acc_ref[k] += prod

    grouped_slots(count_ref[c], slots, visit)

    @pl.when(p == 0)
    def _():
        keep_ref[0] = acc_ref[...]

    @pl.when(p == 1)
    def _():
        send_ref[0] = acc_ref[...].astype(send_ref.dtype)


def tile_forward(rows, cols, count, vals, panels):
    n_src, slots, tile, _ = vals.shape
    row_tiles, width = panels.shape[1], panels.shape[3]
    grid_spec = pltpu.PrefetchScalarGridSpec(
        num_scalar_prefetch=3,
        grid=(n_src,),
        in_specs=[
            pl.BlockSpec((1, slots, tile, tile), lambda c, *_: (c, 0, 0, 0)),
            pl.BlockSpec((1, row_tiles, tile, width), lambda c, *_: (c, 0, 0, 0)),
        ],
        out_specs=pl.BlockSpec((row_tiles, tile, width), lambda c, *_: (0, 0, 0)),
    )
    flops = 2 * n_src * slots * tile * tile * width
    return pl.pallas_call(
        forward_kernel,
        out_shape=jax.ShapeDtypeStruct((row_tiles, tile, width), jnp.float32),
        grid_spec=grid_spec,
        cost_estimate=pl.CostEstimate(
            flops=flops, transcendentals=0, bytes_accessed=vals.size * 2 + panels.size * 2
        ),
    )(rows, cols, count, vals, panels)


def tile_backward(rows, cols, count, vals, grad_tiles, core):
    n_src, slots, tile, _ = vals.shape
    row_tiles, width = grad_tiles.shape[0], grad_tiles.shape[2]
    half = n_src // 2

    def source(i, core_ref):
        return 2 * (i % half) + (i // half + core_ref[0]) % 2

    grid_spec = pltpu.PrefetchScalarGridSpec(
        num_scalar_prefetch=4,
        grid=(n_src,),
        in_specs=[
            pl.BlockSpec((1, slots, tile, tile), lambda i, r, k, n, core_ref: (source(i, core_ref), 0, 0, 0)),
            pl.BlockSpec((row_tiles, tile, width), lambda i, *_: (0, 0, 0)),
        ],
        out_specs=[
            pl.BlockSpec((1, row_tiles, tile, width), lambda i, *_: (jnp.minimum(i, half - 1), 0, 0, 0)),
            pl.BlockSpec((1, row_tiles, tile, width), lambda i, *_: (jnp.maximum(i - half, 0), 0, 0, 0)),
        ],
        scratch_shapes=[pltpu.VMEM((row_tiles, tile, width), jnp.float32)],
    )
    flops = 2 * n_src * slots * tile * tile * width
    part = jax.ShapeDtypeStruct((half, row_tiles, tile, width), jnp.float32)
    part_out = jax.ShapeDtypeStruct((half, row_tiles, tile, width), jnp.bfloat16)
    return pl.pallas_call(
        backward_kernel,
        out_shape=(part, part_out),
        grid_spec=grid_spec,
        cost_estimate=pl.CostEstimate(
            flops=flops, transcendentals=0, bytes_accessed=vals.size * 2 + n_src * row_tiles * tile * width * 4
        ),
    )(rows, cols, count, core, vals, grad_tiles)


MESH_ID = pl.DeviceIdType.MESH


def weight_sum_kernel(n_grp, n_blk, x_ref, out_ref, part, grp_part, whole, sems):
    g = lax.axis_index("grp")
    b = lax.axis_index("blk")
    send1, recv1, send2, recv2, send3, recv3 = sems
    barrier = pltpu.get_barrier_semaphore()
    for i in range(1, n_blk):
        pl.semaphore_signal(barrier, 1, device_id=(g, (b + i) % n_blk), device_id_type=MESH_ID)
    for i in range(1, n_grp):
        pl.semaphore_signal(barrier, 1, device_id=((g + i) % n_grp, b), device_id_type=MESH_ID)
    pl.semaphore_wait(barrier, n_blk - 1 + n_grp - 1)

    def blk_copy(src, dst, send, recv, to, slot):
        return pltpu.make_async_remote_copy(
            src_ref=src, dst_ref=dst, send_sem=send.at[to], recv_sem=recv.at[slot],
            device_id=(g, to), device_id_type=MESH_ID,
        )

    def grp_copy(src, dst, send, recv, to, slot):
        return pltpu.make_async_remote_copy(
            src_ref=src, dst_ref=dst, send_sem=send.at[to], recv_sem=recv.at[slot],
            device_id=(to, b), device_id_type=MESH_ID,
        )

    out1 = []
    for i in range(1, n_blk):
        to = (b + i) % n_blk
        cp = blk_copy(x_ref.at[to], part.at[b], send1, recv1, to, b)
        cp.start()
        out1.append(cp)
    part[b] = x_ref[b]
    for i in range(1, n_blk):
        src = (b + n_blk - i) % n_blk
        blk_copy(x_ref.at[b], part.at[src], send1, recv1, src, src).wait_recv()
    for cp in out1:
        cp.wait_send()
    acc = part[0]
    for j in range(1, n_blk):
        acc = acc + part[j]
    grp_part[g] = acc

    out2 = []
    for i in range(1, n_grp):
        to = (g + i) % n_grp
        cp = grp_copy(grp_part.at[g], grp_part.at[g], send2, recv2, to, g)
        cp.start()
        out2.append(cp)
    for i in range(1, n_grp):
        src = (g + n_grp - i) % n_grp
        grp_copy(grp_part.at[src], grp_part.at[src], send2, recv2, src, src).wait_recv()
    for cp in out2:
        cp.wait_send()
    acc = grp_part[0]
    for j in range(1, n_grp):
        acc = acc + grp_part[j]
    whole[b] = acc

    out3 = []
    for i in range(1, n_blk):
        to = (b + i) % n_blk
        cp = blk_copy(whole.at[b], whole.at[b], send3, recv3, to, b)
        cp.start()
        out3.append(cp)
    for i in range(1, n_blk):
        src = (b + n_blk - i) % n_blk
        blk_copy(whole.at[src], whole.at[src], send3, recv3, src, src).wait_recv()
    for cp in out3:
        cp.wait_send()
    out_ref[...] = whole[...]


def weight_sum(term, n_grp, n_blk):
    rows, cols = term.shape
    chunk = rows * cols // (n_blk * 128)
    x = term.reshape(n_blk, chunk, 128)
    vmem = pl.BlockSpec(memory_space=pltpu.VMEM)
    out = pl.pallas_call(
        functools.partial(weight_sum_kernel, n_grp, n_blk),
        out_shape=jax.ShapeDtypeStruct(x.shape, jnp.float32),
        in_specs=[vmem],
        out_specs=vmem,
        scratch_shapes=[
            pltpu.VMEM(x.shape, jnp.float32),
            pltpu.VMEM((n_grp, chunk, 128), jnp.float32),
            pltpu.VMEM(x.shape, jnp.float32),
            [pltpu.SemaphoreType.DMA((n_blk,)), pltpu.SemaphoreType.DMA((n_blk,)),
             pltpu.SemaphoreType.DMA((n_grp,)), pltpu.SemaphoreType.DMA((n_grp,)),
             pltpu.SemaphoreType.DMA((n_blk,)), pltpu.SemaphoreType.DMA((n_blk,))],
        ],
        compiler_params=pltpu.CompilerParams(collective_id=0, has_side_effects=True),
    )(x)
    return out.reshape(rows, cols)


def exchange_kernel(n_blk, by_dest, src_ref, out_ref, send, recv, own):
    g = lax.axis_index("grp")
    b = lax.axis_index("blk")
    barrier = pltpu.get_barrier_semaphore()
    for i in range(1, n_blk):
        pl.semaphore_signal(barrier, 1, device_id=(g, (b + i) % n_blk), device_id_type=MESH_ID)
    pl.semaphore_wait(barrier, n_blk - 1)

    def piece(to):
        return src_ref.at[to] if by_dest else src_ref

    def remote(to, slot):
        return pltpu.make_async_remote_copy(
            src_ref=piece(to), dst_ref=out_ref.at[slot], send_sem=send.at[to], recv_sem=recv.at[slot],
            device_id=(g, to), device_id_type=MESH_ID,
        )

    local = pltpu.make_async_copy(piece(b), out_ref.at[b], own)
    local.start()
    sent = []
    for i in range(1, n_blk):
        cp = remote((b + i) % n_blk, b)
        cp.start()
        sent.append(cp)
    for i in range(1, n_blk):
        src = (b + n_blk - i) % n_blk
        remote(src, src).wait_recv()
    for cp in sent:
        cp.wait_send()
    local.wait()


def exchange(src, n_blk, by_dest, collective):
    shape = src.shape[1:] if by_dest else src.shape
    any_space = pl.BlockSpec(memory_space=pl.ANY)
    return pl.pallas_call(
        functools.partial(exchange_kernel, n_blk, by_dest),
        out_shape=jax.ShapeDtypeStruct((n_blk,) + shape, src.dtype),
        in_specs=[any_space],
        out_specs=any_space,
        scratch_shapes=[
            pltpu.SemaphoreType.DMA((n_blk,)),
            pltpu.SemaphoreType.DMA((n_blk,)),
            pltpu.SemaphoreType.DMA,
        ],
        compiler_params=pltpu.CompilerParams(collective_id=collective, has_side_effects=True),
    )(src)


def local(
    feats,
    weight,
    cotangent,
    labels,
    tile_vals,
    tile_row,
    tile_col,
    tile_count,
    hub_vals,
    hub_col,
    hub_dest,
    hub_row,
):
    n_blocks = lax.axis_size("blk")
    n_groups = lax.axis_size("grp")
    my_group = lax.axis_index("grp")
    rows_dev = feats.shape[0]
    width = feats.shape[1]
    tile_size = tile_vals.shape[-1]
    row_tiles = rows_dev // tile_size
    hub_count = hub_vals.shape[2]
    capacity = max(2, hub_count // 4)
    highest = lax.Precision.HIGHEST
    dev_vals = tile_vals[0, 0]
    dev_rows = tile_row[0, 0].reshape(-1)
    dev_cols = tile_col[0, 0].reshape(-1)
    dev_count = tile_count[0, 0]
    tile_range = jnp.arange(row_tiles, dtype=jnp.int32)
    proj = jnp.dot(feats, weight, preferred_element_type=jnp.float32).astype(jnp.bfloat16)
    own_panel = proj.reshape(row_tiles, tile_size, width)

    core = lax.axis_index("blk") % 2
    core_groups = [[i for i in range(n_blocks) if i % 2 == k] for k in range(2)]
    sibling = [(i, i ^ 1) for i in range(n_blocks)]
    panels = lax.all_gather(proj, "blk", axis=0, tiled=True)
    panels = panels.reshape(n_blocks, row_tiles, tile_size, width)
    agg_sum = tile_forward(dev_rows, dev_cols, dev_count, dev_vals, panels)

    dest_all = hub_dest[:, 0, :, 0]
    hub_rows_all = hub_row[:, 0, :]
    hub_range = jnp.arange(hub_count, dtype=jnp.int32)
    earlier = hub_range[None, :] < hub_range[:, None]
    same_dest = dest_all[:, :, None] == dest_all[:, None, :]
    rank_all = jnp.sum((same_dest & earlier[None, :, :]).astype(jnp.int32), axis=-1)
    my_dest = lax.dynamic_index_in_dim(dest_all, my_group, 0, keepdims=False)
    my_rank = lax.dynamic_index_in_dim(rank_all, my_group, 0, keepdims=False)
    slot_of = my_dest * capacity + my_rank
    send_place = (
        slot_of[:, None] == jnp.arange(n_groups * capacity, dtype=jnp.int32)[None, :]
    ).astype(jnp.float32)
    hub_tiles = hub_vals[0, 0]
    hub_cols = hub_col[0, 0]
    hub_src = jnp.take(own_panel, hub_cols, axis=0)
    hub_part = jnp.einsum("hij,hjf->hif", hub_tiles, hub_src, preferred_element_type=jnp.float32)
    send_buf = jnp.einsum(
        "hs,hif->sif", send_place.astype(jnp.bfloat16), hub_part.astype(jnp.bfloat16),
        preferred_element_type=jnp.float32,
    ).astype(jnp.bfloat16)
    send_buf = send_buf.reshape(n_groups, capacity, tile_size, width)
    received = lax.all_to_all(send_buf, "grp", split_axis=0, concat_axis=0, tiled=True)
    chosen = (dest_all == my_group).astype(jnp.float32)
    slot_hot = (rank_all[..., None] == jnp.arange(capacity, dtype=jnp.int32)).astype(
        jnp.float32
    ) * chosen[..., None]
    row_hot = (hub_rows_all[..., None] == tile_range).astype(jnp.float32)
    routing = jnp.einsum("shc,shr->scr", slot_hot, row_hot, precision=highest)
    agg_sum = agg_sum + jnp.einsum(
        "scr,scif->rif", routing.astype(jnp.bfloat16), received, preferred_element_type=jnp.float32
    )
    agg_rows = agg_sum.reshape(rows_dev, width)
    layer_out = jax.nn.silu(agg_rows).astype(jnp.bfloat16)
    sigmoid_z = jax.nn.sigmoid(agg_rows)
    slope = sigmoid_z * (1.0 + agg_rows * (1.0 - sigmoid_z))
    keep = (labels >= 0).astype(jnp.float32)[:, None]
    grad_agg = (cotangent.astype(jnp.float32) * keep * slope).astype(jnp.bfloat16)
    grad_tiles = grad_agg.reshape(row_tiles, tile_size, width)

    keep, send = tile_backward(dev_rows, dev_cols, dev_count, dev_vals, grad_tiles, core.reshape(1))
    from_sibling = lax.ppermute(send, "blk", sibling)
    pair_sum = (keep + from_sibling.astype(jnp.float32)).astype(jnp.bfloat16)
    received_parts = lax.all_to_all(
        pair_sum, "blk", split_axis=0, concat_axis=0, tiled=True, axis_index_groups=core_groups
    )
    grad_sum = jnp.sum(received_parts.astype(jnp.float32), axis=0)

    rotation = (my_group + jnp.arange(n_groups, dtype=jnp.int32)) % n_groups
    back_send = jnp.einsum(
        "scr,rif->scif",
        jnp.take(routing, rotation, axis=0).astype(jnp.bfloat16),
        grad_tiles,
        preferred_element_type=jnp.float32,
    ).astype(jnp.bfloat16)
    pieces = [back_send[0]] + [
        lax.ppermute(back_send[k], "grp", [(i, (i + k) % n_groups) for i in range(n_groups)])
        for k in range(1, n_groups)
    ]
    back_flat = jnp.stack(pieces).reshape(n_groups * capacity, tile_size, width)
    back_slot = ((my_group - my_dest) % n_groups) * capacity + my_rank
    back_place = (
        back_slot[:, None] == jnp.arange(n_groups * capacity, dtype=jnp.int32)[None, :]
    ).astype(jnp.bfloat16)
    own_pick = jnp.einsum(
        "hs,sif->hif",
        back_place,
        back_flat,
        preferred_element_type=jnp.float32,
    ).astype(jnp.bfloat16)
    hub_back = jnp.einsum("hij,hif->hjf", hub_tiles, own_pick, preferred_element_type=jnp.float32)
    col_hot = (hub_cols[:, None] == tile_range[None, :]).astype(jnp.float32)
    grad_sum = grad_sum + jnp.einsum("hr,hjf->rjf", col_hot, hub_back, precision=highest)
    grad_rows = grad_sum.reshape(rows_dev, width).astype(jnp.bfloat16)
    weight_term = lax.dot_general(
        feats, grad_rows, (((0,), (0,)), ((), ())), preferred_element_type=jnp.float32
    )
    grad_scale = 1.0 / math.sqrt(rows_dev * n_blocks * n_groups)
    grad_weight = weight_sum(weight_term, n_groups, n_blocks) * grad_scale
    grad_feats = lax.dot_general(
        grad_rows, weight, (((1,), (1,)), ((), ())), preferred_element_type=jnp.float32
    ).astype(jnp.bfloat16)
    return (layer_out, grad_feats, grad_weight)


def solution(mesh):
    in_specs = (
        P(("grp", "blk"), None),
        P(),
        P(("grp", "blk"), None),
        P(("grp", "blk")),
        P("grp", "blk", None, None, None, None),
        P("grp", "blk", None, None),
        P("grp", "blk", None, None),
        P("grp", "blk", None),
        P("grp", "blk", None, None, None),
        P("grp", "blk", None),
        P(None, "blk", None, None),
        P(None, "blk", None),
    )
    out_specs = (P(("grp", "blk"), None), P(("grp", "blk"), None), P())
    return jax.shard_map(local, mesh=mesh, in_specs=in_specs, out_specs=out_specs, check_vma=False)
```

```python
import functools
import math

import jax
import jax.numpy as jnp
from jax import lax
from jax.experimental import pallas as pl
from jax.experimental.pallas import tpu as pltpu
from jax.sharding import PartitionSpec as P


UNROLL = 16


def grouped_slots(count, slots, visit):
    def body(g, carry):
        terms = []
        for j in range(UNROLL):
            t = g * UNROLL + j
            terms.append((t, t < count))
        visit(terms)
        return carry

    lax.fori_loop(0, (count + UNROLL - 1) // UNROLL, body, 0)


def clamp_tile(index, limit):
    return jnp.minimum(jnp.maximum(index, 0), limit - 1)


def forward_kernel(rows_ref, cols_ref, count_ref, vals_ref, panel_ref, out_ref):
    c = pl.program_id(0)
    slots = vals_ref.shape[1]
    row_tiles = out_ref.shape[0]

    @pl.when(c == 0)
    def _():
        out_ref[...] = jnp.zeros_like(out_ref)

    def visit(terms):
        parts = []
        for t, valid in terms:
            r = clamp_tile(rows_ref[c * slots + t], row_tiles)
            k = clamp_tile(cols_ref[c * slots + t], row_tiles)
            prod = jnp.dot(vals_ref[0, t], panel_ref[0, k], preferred_element_type=jnp.float32)
            parts.append((r, jnp.where(valid, prod, 0.0)))
        for r, prod in parts:
            out_ref[r] += prod

    grouped_slots(count_ref[c], slots, visit)


def backward_kernel(rows_ref, cols_ref, count_ref, core_ref, vals_ref, grad_ref, keep_ref, send_ref, acc_ref):
    i = pl.program_id(0)
    half = pl.num_programs(0) // 2
    p = i // half
    c = 2 * (i % half) + (p + core_ref[0]) % 2
    slots = vals_ref.shape[1]
    row_tiles = grad_ref.shape[0]
    acc_ref[...] = jnp.zeros_like(acc_ref)

    def visit(terms):
        parts = []
        for t, valid in terms:
            r = clamp_tile(rows_ref[c * slots + t], row_tiles)
            k = clamp_tile(cols_ref[c * slots + t], row_tiles)
            prod = lax.dot_general(
                vals_ref[0, t], grad_ref[r], (((0,), (0,)), ((), ())), preferred_element_type=jnp.float32
            )
            parts.append((k, jnp.where(valid, prod, 0.0)))
        for k, prod in parts:
            acc_ref[k] += prod

    grouped_slots(count_ref[c], slots, visit)

    @pl.when(p == 0)
    def _():
        keep_ref[0] = acc_ref[...]

    @pl.when(p == 1)
    def _():
        send_ref[0] = acc_ref[...].astype(send_ref.dtype)


def tile_forward(rows, cols, count, vals, panels):
    n_src, slots, tile, _ = vals.shape
    row_tiles, width = panels.shape[1], panels.shape[3]
    grid_spec = pltpu.PrefetchScalarGridSpec(
        num_scalar_prefetch=3,
        grid=(n_src,),
        in_specs=[
            pl.BlockSpec((1, slots, tile, tile), lambda c, *_: (c, 0, 0, 0)),
            pl.BlockSpec((1, row_tiles, tile, width), lambda c, *_: (c, 0, 0, 0)),
        ],
        out_specs=pl.BlockSpec((row_tiles, tile, width), lambda c, *_: (0, 0, 0)),
    )
    flops = 2 * n_src * slots * tile * tile * width
    return pl.pallas_call(
        forward_kernel,
        out_shape=jax.ShapeDtypeStruct((row_tiles, tile, width), jnp.float32),
        grid_spec=grid_spec,
        cost_estimate=pl.CostEstimate(
            flops=flops, transcendentals=0, bytes_accessed=vals.size * 2 + panels.size * 2
        ),
    )(rows, cols, count, vals, panels)


def tile_backward(rows, cols, count, vals, grad_tiles, core):
    n_src, slots, tile, _ = vals.shape
    row_tiles, width = grad_tiles.shape[0], grad_tiles.shape[2]
    half = n_src // 2

    def source(i, core_ref):
        return 2 * (i % half) + (i // half + core_ref[0]) % 2

    grid_spec = pltpu.PrefetchScalarGridSpec(
        num_scalar_prefetch=4,
        grid=(n_src,),
        in_specs=[
            pl.BlockSpec((1, slots, tile, tile), lambda i, r, k, n, core_ref: (source(i, core_ref), 0, 0, 0)),
            pl.BlockSpec((row_tiles, tile, width), lambda i, *_: (0, 0, 0)),
        ],
        out_specs=[
            pl.BlockSpec((1, row_tiles, tile, width), lambda i, *_: (jnp.minimum(i, half - 1), 0, 0, 0)),
            pl.BlockSpec((1, row_tiles, tile, width), lambda i, *_: (jnp.maximum(i - half, 0), 0, 0, 0)),
        ],
        scratch_shapes=[pltpu.VMEM((row_tiles, tile, width), jnp.float32)],
    )
    flops = 2 * n_src * slots * tile * tile * width
    part = jax.ShapeDtypeStruct((half, row_tiles, tile, width), jnp.float32)
    part_out = jax.ShapeDtypeStruct((half, row_tiles, tile, width), jnp.bfloat16)
    return pl.pallas_call(
        backward_kernel,
        out_shape=(part, part_out),
        grid_spec=grid_spec,
        cost_estimate=pl.CostEstimate(
            flops=flops, transcendentals=0, bytes_accessed=vals.size * 2 + n_src * row_tiles * tile * width * 4
        ),
    )(rows, cols, count, core, vals, grad_tiles)


MESH_ID = pl.DeviceIdType.MESH


def weight_sum_kernel(n_grp, n_blk, x_ref, out_ref, part, grp_part, whole, sems):
    g = lax.axis_index("grp")
    b = lax.axis_index("blk")
    send1, recv1, send2, recv2, send3, recv3 = sems
    barrier = pltpu.get_barrier_semaphore()
    for i in range(1, n_blk):
        pl.semaphore_signal(barrier, 1, device_id=(g, (b + i) % n_blk), device_id_type=MESH_ID)
    for i in range(1, n_grp):
        pl.semaphore_signal(barrier, 1, device_id=((g + i) % n_grp, b), device_id_type=MESH_ID)
    pl.semaphore_wait(barrier, n_blk - 1 + n_grp - 1)

    def blk_copy(src, dst, send, recv, to, slot):
        return pltpu.make_async_remote_copy(
            src_ref=src, dst_ref=dst, send_sem=send.at[to], recv_sem=recv.at[slot],
            device_id=(g, to), device_id_type=MESH_ID,
        )

    def grp_copy(src, dst, send, recv, to, slot):
        return pltpu.make_async_remote_copy(
            src_ref=src, dst_ref=dst, send_sem=send.at[to], recv_sem=recv.at[slot],
            device_id=(to, b), device_id_type=MESH_ID,
        )

    out1 = []
    for i in range(1, n_blk):
        to = (b + i) % n_blk
        cp = blk_copy(x_ref.at[to], part.at[b], send1, recv1, to, b)
        cp.start()
        out1.append(cp)
    part[b] = x_ref[b]
    for i in range(1, n_blk):
        src = (b + n_blk - i) % n_blk
        blk_copy(x_ref.at[b], part.at[src], send1, recv1, src, src).wait_recv()
    for cp in out1:
        cp.wait_send()
    acc = part[0]
    for j in range(1, n_blk):
        acc = acc + part[j]
    grp_part[g] = acc

    out2 = []
    for i in range(1, n_grp):
        to = (g + i) % n_grp
        cp = grp_copy(grp_part.at[g], grp_part.at[g], send2, recv2, to, g)
        cp.start()
        out2.append(cp)
    for i in range(1, n_grp):
        src = (g + n_grp - i) % n_grp
        grp_copy(grp_part.at[src], grp_part.at[src], send2, recv2, src, src).wait_recv()
    for cp in out2:
        cp.wait_send()
    acc = grp_part[0]
    for j in range(1, n_grp):
        acc = acc + grp_part[j]
    whole[b] = acc

    out3 = []
    for i in range(1, n_blk):
        to = (b + i) % n_blk
        cp = blk_copy(whole.at[b], whole.at[b], send3, recv3, to, b)
        cp.start()
        out3.append(cp)
    for i in range(1, n_blk):
        src = (b + n_blk - i) % n_blk
        blk_copy(whole.at[src], whole.at[src], send3, recv3, src, src).wait_recv()
    for cp in out3:
        cp.wait_send()
    out_ref[...] = whole[...]


def weight_sum(term, n_grp, n_blk):
    rows, cols = term.shape
    chunk = rows * cols // (n_blk * 128)
    x = term.reshape(n_blk, chunk, 128)
    vmem = pl.BlockSpec(memory_space=pltpu.VMEM)
    out = pl.pallas_call(
        functools.partial(weight_sum_kernel, n_grp, n_blk),
        out_shape=jax.ShapeDtypeStruct(x.shape, jnp.float32),
        in_specs=[vmem],
        out_specs=vmem,
        scratch_shapes=[
            pltpu.VMEM(x.shape, jnp.float32),
            pltpu.VMEM((n_grp, chunk, 128), jnp.float32),
            pltpu.VMEM(x.shape, jnp.float32),
            [pltpu.SemaphoreType.DMA((n_blk,)), pltpu.SemaphoreType.DMA((n_blk,)),
             pltpu.SemaphoreType.DMA((n_grp,)), pltpu.SemaphoreType.DMA((n_grp,)),
             pltpu.SemaphoreType.DMA((n_blk,)), pltpu.SemaphoreType.DMA((n_blk,))],
        ],
        compiler_params=pltpu.CompilerParams(collective_id=0, has_side_effects=True),
    )(x)
    return out.reshape(rows, cols)


def exchange_kernel(n_blk, by_dest, src_ref, out_ref, send, recv, own):
    g = lax.axis_index("grp")
    b = lax.axis_index("blk")
    barrier = pltpu.get_barrier_semaphore()
    for i in range(1, n_blk):
        pl.semaphore_signal(barrier, 1, device_id=(g, (b + i) % n_blk), device_id_type=MESH_ID)
    pl.semaphore_wait(barrier, n_blk - 1)

    def piece(to):
        return src_ref.at[to] if by_dest else src_ref

    def remote(to, slot):
        return pltpu.make_async_remote_copy(
            src_ref=piece(to), dst_ref=out_ref.at[slot], send_sem=send.at[to], recv_sem=recv.at[slot],
            device_id=(g, to), device_id_type=MESH_ID,
        )

    local = pltpu.make_async_copy(piece(b), out_ref.at[b], own)
    local.start()
    sent = []
    for i in range(1, n_blk):
        cp = remote((b + i) % n_blk, b)
        cp.start()
        sent.append(cp)
    for i in range(1, n_blk):
        src = (b + n_blk - i) % n_blk
        remote(src, src).wait_recv()
    for cp in sent:
        cp.wait_send()
    local.wait()


def exchange(src, n_blk, by_dest, collective):
    shape = src.shape[1:] if by_dest else src.shape
    any_space = pl.BlockSpec(memory_space=pl.ANY)
    return pl.pallas_call(
        functools.partial(exchange_kernel, n_blk, by_dest),
        out_shape=jax.ShapeDtypeStruct((n_blk,) + shape, src.dtype),
        in_specs=[any_space],
        out_specs=any_space,
        scratch_shapes=[
            pltpu.SemaphoreType.DMA((n_blk,)),
            pltpu.SemaphoreType.DMA((n_blk,)),
            pltpu.SemaphoreType.DMA,
        ],
        compiler_params=pltpu.CompilerParams(collective_id=collective, has_side_effects=True),
    )(src)


def local(
    feats,
    weight,
    cotangent,
    labels,
    tile_vals,
    tile_row,
    tile_col,
    tile_count,
    hub_vals,
    hub_col,
    hub_dest,
    hub_row,
):
    n_blocks = lax.axis_size("blk")
    n_groups = lax.axis_size("grp")
    my_group = lax.axis_index("grp")
    rows_dev = feats.shape[0]
    width = feats.shape[1]
    tile_size = tile_vals.shape[-1]
    row_tiles = rows_dev // tile_size
    hub_count = hub_vals.shape[2]
    capacity = max(2, hub_count // 4)
    highest = lax.Precision.HIGHEST
    dev_vals = tile_vals[0, 0]
    dev_rows = tile_row[0, 0].reshape(-1)
    dev_cols = tile_col[0, 0].reshape(-1)
    dev_count = tile_count[0, 0]
    tile_range = jnp.arange(row_tiles, dtype=jnp.int32)
    proj = jnp.dot(feats, weight, preferred_element_type=jnp.float32).astype(jnp.bfloat16)
    own_panel = proj.reshape(row_tiles, tile_size, width)

    core = lax.axis_index("blk") % 2
    core_groups = [[i for i in range(n_blocks) if i % 2 == k] for k in range(2)]
    sibling = [(i, i ^ 1) for i in range(n_blocks)]
    panels = lax.all_gather(proj, "blk", axis=0, tiled=True)
    panels = panels.reshape(n_blocks, row_tiles, tile_size, width)
    agg_sum = tile_forward(dev_rows, dev_cols, dev_count, dev_vals, panels)

    dest_all = hub_dest[:, 0, :, 0]
    hub_rows_all = hub_row[:, 0, :]
    hub_range = jnp.arange(hub_count, dtype=jnp.int32)
    earlier = hub_range[None, :] < hub_range[:, None]
    same_dest = dest_all[:, :, None] == dest_all[:, None, :]
    rank_all = jnp.sum((same_dest & earlier[None, :, :]).astype(jnp.int32), axis=-1)
    my_dest = lax.dynamic_index_in_dim(dest_all, my_group, 0, keepdims=False)
    my_rank = lax.dynamic_index_in_dim(rank_all, my_group, 0, keepdims=False)
    slot_of = my_dest * capacity + my_rank
    send_place = (
        slot_of[:, None] == jnp.arange(n_groups * capacity, dtype=jnp.int32)[None, :]
    ).astype(jnp.float32)
    hub_tiles = hub_vals[0, 0]
    hub_cols = hub_col[0, 0]
    hub_src = jnp.take(own_panel, hub_cols, axis=0)
    hub_part = jnp.einsum("hij,hjf->hif", hub_tiles, hub_src, preferred_element_type=jnp.float32)
    send_buf = jnp.einsum(
        "hs,hif->sif", send_place.astype(jnp.bfloat16), hub_part.astype(jnp.bfloat16),
        preferred_element_type=jnp.float32,
    ).astype(jnp.bfloat16)
    send_buf = send_buf.reshape(n_groups, capacity, tile_size, width)
    received = lax.all_to_all(send_buf, "grp", split_axis=0, concat_axis=0, tiled=True)
    chosen = (dest_all == my_group).astype(jnp.float32)
    slot_hot = (rank_all[..., None] == jnp.arange(capacity, dtype=jnp.int32)).astype(
        jnp.float32
    ) * chosen[..., None]
    row_hot = (hub_rows_all[..., None] == tile_range).astype(jnp.float32)
    routing = jnp.einsum("shc,shr->scr", slot_hot, row_hot, precision=highest)
    agg_sum = agg_sum + jnp.einsum(
        "scr,scif->rif", routing.astype(jnp.bfloat16), received, preferred_element_type=jnp.float32
    )
    agg_rows = agg_sum.reshape(rows_dev, width)
    layer_out = jax.nn.silu(agg_rows).astype(jnp.bfloat16)
    sigmoid_z = jax.nn.sigmoid(agg_rows)
    slope = sigmoid_z * (1.0 + agg_rows * (1.0 - sigmoid_z))
    keep = (labels >= 0).astype(jnp.float32)[:, None]
    grad_agg = (cotangent.astype(jnp.float32) * keep * slope).astype(jnp.bfloat16)
    grad_tiles = grad_agg.reshape(row_tiles, tile_size, width)

    keep, send = tile_backward(dev_rows, dev_cols, dev_count, dev_vals, grad_tiles, core.reshape(1))
    from_sibling = lax.ppermute(send, "blk", sibling)
    pair_sum = (keep + from_sibling.astype(jnp.float32)).astype(jnp.bfloat16)
    received_parts = lax.all_to_all(
        pair_sum, "blk", split_axis=0, concat_axis=0, tiled=True, axis_index_groups=core_groups
    )
    grad_sum = jnp.sum(received_parts.astype(jnp.float32), axis=0)

    rotation = (my_group + jnp.arange(n_groups, dtype=jnp.int32)) % n_groups
    back_send = jnp.einsum(
        "scr,rif->scif",
        jnp.take(routing, rotation, axis=0).astype(jnp.bfloat16),
        grad_tiles,
        preferred_element_type=jnp.float32,
    ).astype(jnp.bfloat16)
    pieces = [back_send[0]] + [
        lax.ppermute(back_send[k], "grp", [(i, (i + k) % n_groups) for i in range(n_groups)])
        for k in range(1, n_groups)
    ]
    back_slot = ((my_group - my_dest) % n_groups) * capacity + my_rank
    own_sum = None
    for k, piece in enumerate(pieces):
        place_k = (
            back_slot[:, None] == (k * capacity + jnp.arange(capacity, dtype=jnp.int32))[None, :]
        ).astype(jnp.bfloat16)
        term = jnp.einsum("hc,cif->hif", place_k, piece, preferred_element_type=jnp.float32)
        own_sum = term if own_sum is None else own_sum + term
    own_pick = own_sum.astype(jnp.bfloat16)
    hub_back = jnp.einsum("hij,hif->hjf", hub_tiles, own_pick, preferred_element_type=jnp.float32)
    col_hot = (hub_cols[:, None] == tile_range[None, :]).astype(jnp.float32)
    grad_sum = grad_sum + jnp.einsum("hr,hjf->rjf", col_hot, hub_back, precision=highest)
    grad_rows = grad_sum.reshape(rows_dev, width).astype(jnp.bfloat16)
    weight_term = lax.dot_general(
        feats, grad_rows, (((0,), (0,)), ((), ())), preferred_element_type=jnp.float32
    )
    grad_scale = 1.0 / math.sqrt(rows_dev * n_blocks * n_groups)
    grad_weight = weight_sum(weight_term, n_groups, n_blocks) * grad_scale
    grad_feats = lax.dot_general(
        grad_rows, weight, (((1,), (1,)), ((), ())), preferred_element_type=jnp.float32
    ).astype(jnp.bfloat16)
    return (layer_out, grad_feats, grad_weight)


def solution(mesh):
    in_specs = (
        P(("grp", "blk"), None),
        P(),
        P(("grp", "blk"), None),
        P(("grp", "blk")),
        P("grp", "blk", None, None, None, None),
        P("grp", "blk", None, None),
        P("grp", "blk", None, None),
        P("grp", "blk", None),
        P("grp", "blk", None, None, None),
        P("grp", "blk", None),
        P(None, "blk", None, None),
        P(None, "blk", None),
    )
    out_specs = (P(("grp", "blk"), None), P(("grp", "blk"), None), P())
    return jax.shard_map(local, mesh=mesh, in_specs=in_specs, out_specs=out_specs, check_vma=False)
```

```python
import functools
import math

import jax
import jax.numpy as jnp
from jax import lax
from jax.experimental import pallas as pl
from jax.experimental.pallas import tpu as pltpu
from jax.sharding import PartitionSpec as P


UNROLL = 16


def grouped_slots(count, slots, visit):
    def body(g, carry):
        terms = []
        for j in range(UNROLL):
            t = g * UNROLL + j
            terms.append((t, t < count))
        visit(terms)
        return carry

    lax.fori_loop(0, (count + UNROLL - 1) // UNROLL, body, 0)


def clamp_tile(index, limit):
    return jnp.minimum(jnp.maximum(index, 0), limit - 1)


def forward_kernel(rows_ref, cols_ref, count_ref, vals_ref, panel_ref, out_ref):
    c = pl.program_id(0)
    slots = vals_ref.shape[1]
    row_tiles = out_ref.shape[0]

    @pl.when(c == 0)
    def _():
        out_ref[...] = jnp.zeros_like(out_ref)

    def visit(terms):
        parts = []
        for t, valid in terms:
            r = clamp_tile(rows_ref[c * slots + t], row_tiles)
            k = clamp_tile(cols_ref[c * slots + t], row_tiles)
            prod = jnp.dot(vals_ref[0, t], panel_ref[0, k], preferred_element_type=jnp.float32)
            parts.append((r, jnp.where(valid, prod, 0.0)))
        for r, prod in parts:
            out_ref[r] += prod

    grouped_slots(count_ref[c], slots, visit)


def backward_kernel(rows_ref, cols_ref, count_ref, core_ref, vals_ref, grad_ref, keep_ref, send_ref, acc_ref):
    i = pl.program_id(0)
    half = pl.num_programs(0) // 2
    p = i // half
    c = 2 * ((i % half + core_ref[1]) % half) + (p + core_ref[0]) % 2
    slots = vals_ref.shape[1]
    row_tiles = grad_ref.shape[0]
    acc_ref[...] = jnp.zeros_like(acc_ref)

    def visit(terms):
        parts = []
        for t, valid in terms:
            r = clamp_tile(rows_ref[c * slots + t], row_tiles)
            k = clamp_tile(cols_ref[c * slots + t], row_tiles)
            prod = lax.dot_general(
                vals_ref[0, t], grad_ref[r], (((0,), (0,)), ((), ())), preferred_element_type=jnp.float32
            )
            parts.append((k, jnp.where(valid, prod, 0.0)))
        for k, prod in parts:
            acc_ref[k] += prod

    grouped_slots(count_ref[c], slots, visit)

    @pl.when(p == 0)
    def _():
        keep_ref[0] = acc_ref[...]

    @pl.when(p == 1)
    def _():
        send_ref[0] = acc_ref[...].astype(send_ref.dtype)


def tile_forward(rows, cols, count, vals, panels):
    n_src, slots, tile, _ = vals.shape
    row_tiles, width = panels.shape[1], panels.shape[3]
    grid_spec = pltpu.PrefetchScalarGridSpec(
        num_scalar_prefetch=3,
        grid=(n_src,),
        in_specs=[
            pl.BlockSpec((1, slots, tile, tile), lambda c, *_: (c, 0, 0, 0)),
            pl.BlockSpec((1, row_tiles, tile, width), lambda c, *_: (c, 0, 0, 0)),
        ],
        out_specs=pl.BlockSpec((row_tiles, tile, width), lambda c, *_: (0, 0, 0)),
    )
    flops = 2 * n_src * slots * tile * tile * width
    return pl.pallas_call(
        forward_kernel,
        out_shape=jax.ShapeDtypeStruct((row_tiles, tile, width), jnp.float32),
        grid_spec=grid_spec,
        cost_estimate=pl.CostEstimate(
            flops=flops, transcendentals=0, bytes_accessed=vals.size * 2 + panels.size * 2
        ),
    )(rows, cols, count, vals, panels)


def tile_backward(rows, cols, count, vals, grad_tiles, core):
    n_src, slots, tile, _ = vals.shape
    row_tiles, width = grad_tiles.shape[0], grad_tiles.shape[2]
    half = n_src // 2

    def source(i, core_ref):
        return 2 * ((i % half + core_ref[1]) % half) + (i // half + core_ref[0]) % 2

    grid_spec = pltpu.PrefetchScalarGridSpec(
        num_scalar_prefetch=4,
        grid=(n_src,),
        in_specs=[
            pl.BlockSpec((1, slots, tile, tile), lambda i, r, k, n, core_ref: (source(i, core_ref), 0, 0, 0)),
            pl.BlockSpec((row_tiles, tile, width), lambda i, *_: (0, 0, 0)),
        ],
        out_specs=[
            pl.BlockSpec((1, row_tiles, tile, width), lambda i, *_: (jnp.minimum(i, half - 1), 0, 0, 0)),
            pl.BlockSpec((1, row_tiles, tile, width), lambda i, *_: (jnp.maximum(i - half, 0), 0, 0, 0)),
        ],
        scratch_shapes=[pltpu.VMEM((row_tiles, tile, width), jnp.float32)],
    )
    flops = 2 * n_src * slots * tile * tile * width
    part = jax.ShapeDtypeStruct((half, row_tiles, tile, width), jnp.float32)
    part_out = jax.ShapeDtypeStruct((half, row_tiles, tile, width), jnp.bfloat16)
    return pl.pallas_call(
        backward_kernel,
        out_shape=(part, part_out),
        grid_spec=grid_spec,
        cost_estimate=pl.CostEstimate(
            flops=flops, transcendentals=0, bytes_accessed=vals.size * 2 + n_src * row_tiles * tile * width * 4
        ),
    )(rows, cols, count, core, vals, grad_tiles)


MESH_ID = pl.DeviceIdType.MESH


def weight_sum_kernel(n_grp, n_blk, x_ref, out_ref, part, grp_part, whole, sems):
    g = lax.axis_index("grp")
    b = lax.axis_index("blk")
    send1, recv1, send2, recv2, send3, recv3 = sems
    barrier = pltpu.get_barrier_semaphore()
    for i in range(1, n_blk):
        pl.semaphore_signal(barrier, 1, device_id=(g, (b + i) % n_blk), device_id_type=MESH_ID)
    for i in range(1, n_grp):
        pl.semaphore_signal(barrier, 1, device_id=((g + i) % n_grp, b), device_id_type=MESH_ID)
    pl.semaphore_wait(barrier, n_blk - 1 + n_grp - 1)

    def blk_copy(src, dst, send, recv, to, slot):
        return pltpu.make_async_remote_copy(
            src_ref=src, dst_ref=dst, send_sem=send.at[to], recv_sem=recv.at[slot],
            device_id=(g, to), device_id_type=MESH_ID,
        )

    def grp_copy(src, dst, send, recv, to, slot):
        return pltpu.make_async_remote_copy(
            src_ref=src, dst_ref=dst, send_sem=send.at[to], recv_sem=recv.at[slot],
            device_id=(to, b), device_id_type=MESH_ID,
        )

    out1 = []
    for i in range(1, n_blk):
        to = (b + i) % n_blk
        cp = blk_copy(x_ref.at[to], part.at[b], send1, recv1, to, b)
        cp.start()
        out1.append(cp)
    part[b] = x_ref[b]
    for i in range(1, n_blk):
        src = (b + n_blk - i) % n_blk
        blk_copy(x_ref.at[b], part.at[src], send1, recv1, src, src).wait_recv()
    for cp in out1:
        cp.wait_send()
    acc = part[0]
    for j in range(1, n_blk):
        acc = acc + part[j]
    grp_part[g] = acc

    out2 = []
    for i in range(1, n_grp):
        to = (g + i) % n_grp
        cp = grp_copy(grp_part.at[g], grp_part.at[g], send2, recv2, to, g)
        cp.start()
        out2.append(cp)
    for i in range(1, n_grp):
        src = (g + n_grp - i) % n_grp
        grp_copy(grp_part.at[src], grp_part.at[src], send2, recv2, src, src).wait_recv()
    for cp in out2:
        cp.wait_send()
    acc = grp_part[0]
    for j in range(1, n_grp):
        acc = acc + grp_part[j]
    whole[b] = acc

    out3 = []
    for i in range(1, n_blk):
        to = (b + i) % n_blk
        cp = blk_copy(whole.at[b], whole.at[b], send3, recv3, to, b)
        cp.start()
        out3.append(cp)
    for i in range(1, n_blk):
        src = (b + n_blk - i) % n_blk
        blk_copy(whole.at[src], whole.at[src], send3, recv3, src, src).wait_recv()
    for cp in out3:
        cp.wait_send()
    out_ref[...] = whole[...]


def weight_sum(term, n_grp, n_blk):
    rows, cols = term.shape
    chunk = rows * cols // (n_blk * 128)
    x = term.reshape(n_blk, chunk, 128)
    vmem = pl.BlockSpec(memory_space=pltpu.VMEM)
    out = pl.pallas_call(
        functools.partial(weight_sum_kernel, n_grp, n_blk),
        out_shape=jax.ShapeDtypeStruct(x.shape, jnp.float32),
        in_specs=[vmem],
        out_specs=vmem,
        scratch_shapes=[
            pltpu.VMEM(x.shape, jnp.float32),
            pltpu.VMEM((n_grp, chunk, 128), jnp.float32),
            pltpu.VMEM(x.shape, jnp.float32),
            [pltpu.SemaphoreType.DMA((n_blk,)), pltpu.SemaphoreType.DMA((n_blk,)),
             pltpu.SemaphoreType.DMA((n_grp,)), pltpu.SemaphoreType.DMA((n_grp,)),
             pltpu.SemaphoreType.DMA((n_blk,)), pltpu.SemaphoreType.DMA((n_blk,))],
        ],
        compiler_params=pltpu.CompilerParams(collective_id=0, has_side_effects=True),
    )(x)
    return out.reshape(rows, cols)


def exchange_kernel(n_blk, by_dest, src_ref, out_ref, send, recv, own):
    g = lax.axis_index("grp")
    b = lax.axis_index("blk")
    barrier = pltpu.get_barrier_semaphore()
    for i in range(1, n_blk):
        pl.semaphore_signal(barrier, 1, device_id=(g, (b + i) % n_blk), device_id_type=MESH_ID)
    pl.semaphore_wait(barrier, n_blk - 1)

    def piece(to):
        return src_ref.at[to] if by_dest else src_ref

    def remote(to, slot):
        return pltpu.make_async_remote_copy(
            src_ref=piece(to), dst_ref=out_ref.at[slot], send_sem=send.at[to], recv_sem=recv.at[slot],
            device_id=(g, to), device_id_type=MESH_ID,
        )

    local = pltpu.make_async_copy(piece(b), out_ref.at[b], own)
    local.start()
    sent = []
    for i in range(1, n_blk):
        cp = remote((b + i) % n_blk, b)
        cp.start()
        sent.append(cp)
    for i in range(1, n_blk):
        src = (b + n_blk - i) % n_blk
        remote(src, src).wait_recv()
    for cp in sent:
        cp.wait_send()
    local.wait()


def exchange(src, n_blk, by_dest, collective):
    shape = src.shape[1:] if by_dest else src.shape
    any_space = pl.BlockSpec(memory_space=pl.ANY)
    return pl.pallas_call(
        functools.partial(exchange_kernel, n_blk, by_dest),
        out_shape=jax.ShapeDtypeStruct((n_blk,) + shape, src.dtype),
        in_specs=[any_space],
        out_specs=any_space,
        scratch_shapes=[
            pltpu.SemaphoreType.DMA((n_blk,)),
            pltpu.SemaphoreType.DMA((n_blk,)),
            pltpu.SemaphoreType.DMA,
        ],
        compiler_params=pltpu.CompilerParams(collective_id=collective, has_side_effects=True),
    )(src)


def local(
    feats,
    weight,
    cotangent,
    labels,
    tile_vals,
    tile_row,
    tile_col,
    tile_count,
    hub_vals,
    hub_col,
    hub_dest,
    hub_row,
):
    n_blocks = lax.axis_size("blk")
    n_groups = lax.axis_size("grp")
    my_group = lax.axis_index("grp")
    rows_dev = feats.shape[0]
    width = feats.shape[1]
    tile_size = tile_vals.shape[-1]
    row_tiles = rows_dev // tile_size
    hub_count = hub_vals.shape[2]
    capacity = max(2, hub_count // 4)
    highest = lax.Precision.HIGHEST
    dev_vals = tile_vals[0, 0]
    dev_rows = tile_row[0, 0].reshape(-1)
    dev_cols = tile_col[0, 0].reshape(-1)
    dev_count = tile_count[0, 0]
    tile_range = jnp.arange(row_tiles, dtype=jnp.int32)
    proj = jnp.dot(feats, weight, preferred_element_type=jnp.float32).astype(jnp.bfloat16)
    own_panel = proj.reshape(row_tiles, tile_size, width)

    core = lax.axis_index("blk") % 2
    core_groups = [[i for i in range(n_blocks) if i % 2 == k] for k in range(2)]
    sibling = [(i, i ^ 1) for i in range(n_blocks)]
    panels = lax.all_gather(proj, "blk", axis=0, tiled=True)
    panels = panels.reshape(n_blocks, row_tiles, tile_size, width)
    agg_sum = tile_forward(dev_rows, dev_cols, dev_count, dev_vals, panels)

    dest_all = hub_dest[:, 0, :, 0]
    hub_rows_all = hub_row[:, 0, :]
    hub_range = jnp.arange(hub_count, dtype=jnp.int32)
    earlier = hub_range[None, :] < hub_range[:, None]
    same_dest = dest_all[:, :, None] == dest_all[:, None, :]
    rank_all = jnp.sum((same_dest & earlier[None, :, :]).astype(jnp.int32), axis=-1)
    my_dest = lax.dynamic_index_in_dim(dest_all, my_group, 0, keepdims=False)
    my_rank = lax.dynamic_index_in_dim(rank_all, my_group, 0, keepdims=False)
    slot_of = my_dest * capacity + my_rank
    send_place = (
        slot_of[:, None] == jnp.arange(n_groups * capacity, dtype=jnp.int32)[None, :]
    ).astype(jnp.float32)
    hub_tiles = hub_vals[0, 0]
    hub_cols = hub_col[0, 0]
    hub_src = jnp.take(own_panel, hub_cols, axis=0)
    hub_part = jnp.einsum("hij,hjf->hif", hub_tiles, hub_src, preferred_element_type=jnp.float32)
    send_buf = jnp.einsum(
        "hs,hif->sif", send_place.astype(jnp.bfloat16), hub_part.astype(jnp.bfloat16),
        preferred_element_type=jnp.float32,
    ).astype(jnp.bfloat16)
    send_buf = send_buf.reshape(n_groups, capacity, tile_size, width)
    received = lax.all_to_all(send_buf, "grp", split_axis=0, concat_axis=0, tiled=True)
    chosen = (dest_all == my_group).astype(jnp.float32)
    slot_hot = (rank_all[..., None] == jnp.arange(capacity, dtype=jnp.int32)).astype(
        jnp.float32
    ) * chosen[..., None]
    row_hot = (hub_rows_all[..., None] == tile_range).astype(jnp.float32)
    routing = jnp.einsum("shc,shr->scr", slot_hot, row_hot, precision=highest)
    agg_sum = agg_sum + jnp.einsum(
        "scr,scif->rif", routing.astype(jnp.bfloat16), received, preferred_element_type=jnp.float32
    )
    agg_rows = agg_sum.reshape(rows_dev, width)
    layer_out = jax.nn.silu(agg_rows).astype(jnp.bfloat16)
    sigmoid_z = jax.nn.sigmoid(agg_rows)
    slope = sigmoid_z * (1.0 + agg_rows * (1.0 - sigmoid_z))
    keep = (labels >= 0).astype(jnp.float32)[:, None]
    grad_agg = (cotangent.astype(jnp.float32) * keep * slope).astype(jnp.bfloat16)
    grad_tiles = grad_agg.reshape(row_tiles, tile_size, width)

    keep, send = tile_backward(
        dev_rows, dev_cols, dev_count, dev_vals, grad_tiles, jnp.stack([core, lax.axis_index("blk") // 2])
    )
    from_sibling = lax.ppermute(send, "blk", sibling)
    pair_sum = (keep + from_sibling.astype(jnp.float32)).astype(jnp.bfloat16)
    grad_sum = pair_sum[0].astype(jnp.float32)
    for k in range(1, n_blocks // 2):
        shift = [(i, (i + 2 * k) % n_blocks) for i in range(n_blocks)]
        grad_sum = grad_sum + lax.ppermute(pair_sum[k], "blk", shift).astype(jnp.float32)

    rotation = (my_group + jnp.arange(n_groups, dtype=jnp.int32)) % n_groups
    back_send = jnp.einsum(
        "scr,rif->scif",
        jnp.take(routing, rotation, axis=0).astype(jnp.bfloat16),
        grad_tiles,
        preferred_element_type=jnp.float32,
    ).astype(jnp.bfloat16)
    pieces = [back_send[0]] + [
        lax.ppermute(back_send[k], "grp", [(i, (i + k) % n_groups) for i in range(n_groups)])
        for k in range(1, n_groups)
    ]
    back_slot = ((my_group - my_dest) % n_groups) * capacity + my_rank
    own_sum = None
    for k, piece in enumerate(pieces):
        place_k = (
            back_slot[:, None] == (k * capacity + jnp.arange(capacity, dtype=jnp.int32))[None, :]
        ).astype(jnp.bfloat16)
        term = jnp.einsum("hc,cif->hif", place_k, piece, preferred_element_type=jnp.float32)
        own_sum = term if own_sum is None else own_sum + term
    own_pick = own_sum.astype(jnp.bfloat16)
    hub_back = jnp.einsum("hij,hif->hjf", hub_tiles, own_pick, preferred_element_type=jnp.float32)
    col_hot = (hub_cols[:, None] == tile_range[None, :]).astype(jnp.float32)
    grad_sum = grad_sum + jnp.einsum("hr,hjf->rjf", col_hot, hub_back, precision=highest)
    grad_rows = grad_sum.reshape(rows_dev, width).astype(jnp.bfloat16)
    weight_term = lax.dot_general(
        feats, grad_rows, (((0,), (0,)), ((), ())), preferred_element_type=jnp.float32
    )
    grad_scale = 1.0 / math.sqrt(rows_dev * n_blocks * n_groups)
    grad_weight = weight_sum(weight_term, n_groups, n_blocks) * grad_scale
    grad_feats = lax.dot_general(
        grad_rows, weight, (((1,), (1,)), ((), ())), preferred_element_type=jnp.float32
    ).astype(jnp.bfloat16)
    return (layer_out, grad_feats, grad_weight)


def solution(mesh):
    in_specs = (
        P(("grp", "blk"), None),
        P(),
        P(("grp", "blk"), None),
        P(("grp", "blk")),
        P("grp", "blk", None, None, None, None),
        P("grp", "blk", None, None),
        P("grp", "blk", None, None),
        P("grp", "blk", None),
        P("grp", "blk", None, None, None),
        P("grp", "blk", None),
        P(None, "blk", None, None),
        P(None, "blk", None),
    )
    out_specs = (P(("grp", "blk"), None), P(("grp", "blk"), None), P())
    return jax.shard_map(local, mesh=mesh, in_specs=in_specs, out_specs=out_specs, check_vma=False)
```

```python
import functools
import math

import jax
import jax.numpy as jnp
from jax import lax
from jax.experimental import pallas as pl
from jax.experimental.pallas import tpu as pltpu
from jax.sharding import PartitionSpec as P


UNROLL = 16


def grouped_slots(count, slots, visit):
    def body(g, carry):
        terms = []
        for j in range(UNROLL):
            t = g * UNROLL + j
            terms.append((t, t < count))
        visit(terms)
        return carry

    lax.fori_loop(0, (count + UNROLL - 1) // UNROLL, body, 0)


def clamp_tile(index, limit):
    return jnp.minimum(jnp.maximum(index, 0), limit - 1)


def forward_kernel(rows_ref, cols_ref, count_ref, vals_ref, panel_ref, out_ref):
    c = pl.program_id(0)
    slots = vals_ref.shape[1]
    row_tiles = out_ref.shape[0]

    @pl.when(c == 0)
    def _():
        out_ref[...] = jnp.zeros_like(out_ref)

    def visit(terms):
        parts = []
        for t, valid in terms:
            r = clamp_tile(rows_ref[c * slots + t], row_tiles)
            k = clamp_tile(cols_ref[c * slots + t], row_tiles)
            prod = jnp.dot(vals_ref[0, t], panel_ref[0, k], preferred_element_type=jnp.float32)
            parts.append((r, jnp.where(valid, prod, 0.0)))
        for r, prod in parts:
            out_ref[r] += prod

    grouped_slots(count_ref[c], slots, visit)


def backward_kernel(rows_ref, cols_ref, count_ref, core_ref, vals_ref, grad_ref, keep_ref, send_ref, acc_ref):
    i = pl.program_id(0)
    half = pl.num_programs(0) // 2
    p = i // half
    c = 2 * (i % half) + (p + core_ref[0]) % 2
    slots = vals_ref.shape[1]
    row_tiles = grad_ref.shape[0]
    acc_ref[...] = jnp.zeros_like(acc_ref)

    def visit(terms):
        parts = []
        for t, valid in terms:
            r = clamp_tile(rows_ref[c * slots + t], row_tiles)
            k = clamp_tile(cols_ref[c * slots + t], row_tiles)
            prod = lax.dot_general(
                vals_ref[0, t], grad_ref[r], (((0,), (0,)), ((), ())), preferred_element_type=jnp.float32
            )
            parts.append((k, jnp.where(valid, prod, 0.0)))
        for k, prod in parts:
            acc_ref[k] += prod

    grouped_slots(count_ref[c], slots, visit)

    @pl.when(p == 0)
    def _():
        keep_ref[0] = acc_ref[...].astype(keep_ref.dtype)

    @pl.when(p == 1)
    def _():
        send_ref[0] = acc_ref[...].astype(send_ref.dtype)


def tile_forward(rows, cols, count, vals, panels):
    n_src, slots, tile, _ = vals.shape
    row_tiles, width = panels.shape[1], panels.shape[3]
    grid_spec = pltpu.PrefetchScalarGridSpec(
        num_scalar_prefetch=3,
        grid=(n_src,),
        in_specs=[
            pl.BlockSpec((1, slots, tile, tile), lambda c, *_: (c, 0, 0, 0)),
            pl.BlockSpec((1, row_tiles, tile, width), lambda c, *_: (c, 0, 0, 0)),
        ],
        out_specs=pl.BlockSpec((row_tiles, tile, width), lambda c, *_: (0, 0, 0)),
    )
    flops = 2 * n_src * slots * tile * tile * width
    return pl.pallas_call(
        forward_kernel,
        out_shape=jax.ShapeDtypeStruct((row_tiles, tile, width), jnp.float32),
        grid_spec=grid_spec,
        cost_estimate=pl.CostEstimate(
            flops=flops, transcendentals=0, bytes_accessed=vals.size * 2 + panels.size * 2
        ),
    )(rows, cols, count, vals, panels)


def tile_backward(rows, cols, count, vals, grad_tiles, core):
    n_src, slots, tile, _ = vals.shape
    row_tiles, width = grad_tiles.shape[0], grad_tiles.shape[2]
    half = n_src // 2

    def source(i, core_ref):
        return 2 * (i % half) + (i // half + core_ref[0]) % 2

    grid_spec = pltpu.PrefetchScalarGridSpec(
        num_scalar_prefetch=4,
        grid=(n_src,),
        in_specs=[
            pl.BlockSpec((1, slots, tile, tile), lambda i, r, k, n, core_ref: (source(i, core_ref), 0, 0, 0)),
            pl.BlockSpec((row_tiles, tile, width), lambda i, *_: (0, 0, 0)),
        ],
        out_specs=[
            pl.BlockSpec((1, row_tiles, tile, width), lambda i, *_: (jnp.minimum(i, half - 1), 0, 0, 0)),
            pl.BlockSpec((1, row_tiles, tile, width), lambda i, *_: (jnp.maximum(i - half, 0), 0, 0, 0)),
        ],
        scratch_shapes=[pltpu.VMEM((row_tiles, tile, width), jnp.float32)],
    )
    flops = 2 * n_src * slots * tile * tile * width
    part_out = jax.ShapeDtypeStruct((half, row_tiles, tile, width), jnp.bfloat16)
    return pl.pallas_call(
        backward_kernel,
        out_shape=(part_out, part_out),
        grid_spec=grid_spec,
        cost_estimate=pl.CostEstimate(
            flops=flops, transcendentals=0, bytes_accessed=vals.size * 2 + n_src * row_tiles * tile * width * 4
        ),
    )(rows, cols, count, core, vals, grad_tiles)


MESH_ID = pl.DeviceIdType.MESH


def weight_sum_kernel(n_grp, n_blk, x_ref, out_ref, part, grp_part, whole, sems):
    g = lax.axis_index("grp")
    b = lax.axis_index("blk")
    send1, recv1, send2, recv2, send3, recv3 = sems
    barrier = pltpu.get_barrier_semaphore()
    for i in range(1, n_blk):
        pl.semaphore_signal(barrier, 1, device_id=(g, (b + i) % n_blk), device_id_type=MESH_ID)
    for i in range(1, n_grp):
        pl.semaphore_signal(barrier, 1, device_id=((g + i) % n_grp, b), device_id_type=MESH_ID)
    pl.semaphore_wait(barrier, n_blk - 1 + n_grp - 1)

    def blk_copy(src, dst, send, recv, to, slot):
        return pltpu.make_async_remote_copy(
            src_ref=src, dst_ref=dst, send_sem=send.at[to], recv_sem=recv.at[slot],
            device_id=(g, to), device_id_type=MESH_ID,
        )

    def grp_copy(src, dst, send, recv, to, slot):
        return pltpu.make_async_remote_copy(
            src_ref=src, dst_ref=dst, send_sem=send.at[to], recv_sem=recv.at[slot],
            device_id=(to, b), device_id_type=MESH_ID,
        )

    out1 = []
    for i in range(1, n_blk):
        to = (b + i) % n_blk
        cp = blk_copy(x_ref.at[to], part.at[b], send1, recv1, to, b)
        cp.start()
        out1.append(cp)
    part[b] = x_ref[b]
    for i in range(1, n_blk):
        src = (b + n_blk - i) % n_blk
        blk_copy(x_ref.at[b], part.at[src], send1, recv1, src, src).wait_recv()
    for cp in out1:
        cp.wait_send()
    acc = part[0]
    for j in range(1, n_blk):
        acc = acc + part[j]
    grp_part[g] = acc

    out2 = []
    for i in range(1, n_grp):
        to = (g + i) % n_grp
        cp = grp_copy(grp_part.at[g], grp_part.at[g], send2, recv2, to, g)
        cp.start()
        out2.append(cp)
    for i in range(1, n_grp):
        src = (g + n_grp - i) % n_grp
        grp_copy(grp_part.at[src], grp_part.at[src], send2, recv2, src, src).wait_recv()
    for cp in out2:
        cp.wait_send()
    acc = grp_part[0]
    for j in range(1, n_grp):
        acc = acc + grp_part[j]
    whole[b] = acc

    out3 = []
    for i in range(1, n_blk):
        to = (b + i) % n_blk
        cp = blk_copy(whole.at[b], whole.at[b], send3, recv3, to, b)
        cp.start()
        out3.append(cp)
    for i in range(1, n_blk):
        src = (b + n_blk - i) % n_blk
        blk_copy(whole.at[src], whole.at[src], send3, recv3, src, src).wait_recv()
    for cp in out3:
        cp.wait_send()
    out_ref[...] = whole[...]


def weight_sum(term, n_grp, n_blk):
    rows, cols = term.shape
    chunk = rows * cols // (n_blk * 128)
    x = term.reshape(n_blk, chunk, 128)
    vmem = pl.BlockSpec(memory_space=pltpu.VMEM)
    out = pl.pallas_call(
        functools.partial(weight_sum_kernel, n_grp, n_blk),
        out_shape=jax.ShapeDtypeStruct(x.shape, jnp.float32),
        in_specs=[vmem],
        out_specs=vmem,
        scratch_shapes=[
            pltpu.VMEM(x.shape, jnp.float32),
            pltpu.VMEM((n_grp, chunk, 128), jnp.float32),
            pltpu.VMEM(x.shape, jnp.float32),
            [pltpu.SemaphoreType.DMA((n_blk,)), pltpu.SemaphoreType.DMA((n_blk,)),
             pltpu.SemaphoreType.DMA((n_grp,)), pltpu.SemaphoreType.DMA((n_grp,)),
             pltpu.SemaphoreType.DMA((n_blk,)), pltpu.SemaphoreType.DMA((n_blk,))],
        ],
        compiler_params=pltpu.CompilerParams(collective_id=0, has_side_effects=True),
    )(x)
    return out.reshape(rows, cols)


def exchange_kernel(n_blk, by_dest, src_ref, out_ref, send, recv, own):
    g = lax.axis_index("grp")
    b = lax.axis_index("blk")
    barrier = pltpu.get_barrier_semaphore()
    for i in range(1, n_blk):
        pl.semaphore_signal(barrier, 1, device_id=(g, (b + i) % n_blk), device_id_type=MESH_ID)
    pl.semaphore_wait(barrier, n_blk - 1)

    def piece(to):
        return src_ref.at[to] if by_dest else src_ref

    def remote(to, slot):
        return pltpu.make_async_remote_copy(
            src_ref=piece(to), dst_ref=out_ref.at[slot], send_sem=send.at[to], recv_sem=recv.at[slot],
            device_id=(g, to), device_id_type=MESH_ID,
        )

    local = pltpu.make_async_copy(piece(b), out_ref.at[b], own)
    local.start()
    sent = []
    for i in range(1, n_blk):
        cp = remote((b + i) % n_blk, b)
        cp.start()
        sent.append(cp)
    for i in range(1, n_blk):
        src = (b + n_blk - i) % n_blk
        remote(src, src).wait_recv()
    for cp in sent:
        cp.wait_send()
    local.wait()


def exchange(src, n_blk, by_dest, collective):
    shape = src.shape[1:] if by_dest else src.shape
    any_space = pl.BlockSpec(memory_space=pl.ANY)
    return pl.pallas_call(
        functools.partial(exchange_kernel, n_blk, by_dest),
        out_shape=jax.ShapeDtypeStruct((n_blk,) + shape, src.dtype),
        in_specs=[any_space],
        out_specs=any_space,
        scratch_shapes=[
            pltpu.SemaphoreType.DMA((n_blk,)),
            pltpu.SemaphoreType.DMA((n_blk,)),
            pltpu.SemaphoreType.DMA,
        ],
        compiler_params=pltpu.CompilerParams(collective_id=collective, has_side_effects=True),
    )(src)


def local(
    feats,
    weight,
    cotangent,
    labels,
    tile_vals,
    tile_row,
    tile_col,
    tile_count,
    hub_vals,
    hub_col,
    hub_dest,
    hub_row,
):
    n_blocks = lax.axis_size("blk")
    n_groups = lax.axis_size("grp")
    my_group = lax.axis_index("grp")
    rows_dev = feats.shape[0]
    width = feats.shape[1]
    tile_size = tile_vals.shape[-1]
    row_tiles = rows_dev // tile_size
    hub_count = hub_vals.shape[2]
    capacity = max(2, hub_count // 4)
    highest = lax.Precision.HIGHEST
    dev_vals = tile_vals[0, 0]
    dev_rows = tile_row[0, 0].reshape(-1)
    dev_cols = tile_col[0, 0].reshape(-1)
    dev_count = tile_count[0, 0]
    tile_range = jnp.arange(row_tiles, dtype=jnp.int32)
    proj = jnp.dot(feats, weight, preferred_element_type=jnp.float32).astype(jnp.bfloat16)
    own_panel = proj.reshape(row_tiles, tile_size, width)

    core = lax.axis_index("blk") % 2
    core_groups = [[i for i in range(n_blocks) if i % 2 == k] for k in range(2)]
    sibling = [(i, i ^ 1) for i in range(n_blocks)]
    panels = lax.all_gather(proj, "blk", axis=0, tiled=True)
    panels = panels.reshape(n_blocks, row_tiles, tile_size, width)
    agg_sum = tile_forward(dev_rows, dev_cols, dev_count, dev_vals, panels)

    dest_all = hub_dest[:, 0, :, 0]
    hub_rows_all = hub_row[:, 0, :]
    hub_range = jnp.arange(hub_count, dtype=jnp.int32)
    earlier = hub_range[None, :] < hub_range[:, None]
    same_dest = dest_all[:, :, None] == dest_all[:, None, :]
    rank_all = jnp.sum((same_dest & earlier[None, :, :]).astype(jnp.int32), axis=-1)
    my_dest = lax.dynamic_index_in_dim(dest_all, my_group, 0, keepdims=False)
    my_rank = lax.dynamic_index_in_dim(rank_all, my_group, 0, keepdims=False)
    slot_of = my_dest * capacity + my_rank
    send_place = (
        slot_of[:, None] == jnp.arange(n_groups * capacity, dtype=jnp.int32)[None, :]
    ).astype(jnp.float32)
    hub_tiles = hub_vals[0, 0]
    hub_cols = hub_col[0, 0]
    hub_src = jnp.take(own_panel, hub_cols, axis=0)
    hub_part = jnp.einsum("hij,hjf->hif", hub_tiles, hub_src, preferred_element_type=jnp.float32)
    send_buf = jnp.einsum(
        "hs,hif->sif", send_place.astype(jnp.bfloat16), hub_part.astype(jnp.bfloat16),
        preferred_element_type=jnp.float32,
    ).astype(jnp.bfloat16)
    send_buf = send_buf.reshape(n_groups, capacity, tile_size, width)
    received = lax.all_to_all(send_buf, "grp", split_axis=0, concat_axis=0, tiled=True)
    chosen = (dest_all == my_group).astype(jnp.float32)
    slot_hot = (rank_all[..., None] == jnp.arange(capacity, dtype=jnp.int32)).astype(
        jnp.float32
    ) * chosen[..., None]
    row_hot = (hub_rows_all[..., None] == tile_range).astype(jnp.float32)
    routing = jnp.einsum("shc,shr->scr", slot_hot, row_hot, precision=highest)
    agg_sum = agg_sum + jnp.einsum(
        "scr,scif->rif", routing.astype(jnp.bfloat16), received, preferred_element_type=jnp.float32
    )
    agg_rows = agg_sum.reshape(rows_dev, width)
    layer_out = jax.nn.silu(agg_rows).astype(jnp.bfloat16)
    sigmoid_z = jax.nn.sigmoid(agg_rows)
    slope = sigmoid_z * (1.0 + agg_rows * (1.0 - sigmoid_z))
    keep = (labels >= 0).astype(jnp.float32)[:, None]
    grad_agg = (cotangent.astype(jnp.float32) * keep * slope).astype(jnp.bfloat16)
    grad_tiles = grad_agg.reshape(row_tiles, tile_size, width)

    keep, send = tile_backward(dev_rows, dev_cols, dev_count, dev_vals, grad_tiles, core.reshape(1))
    from_sibling = lax.ppermute(send, "blk", sibling)
    pair_sum = (keep.astype(jnp.float32) + from_sibling.astype(jnp.float32)).astype(jnp.bfloat16)
    received_parts = lax.all_to_all(
        pair_sum, "blk", split_axis=0, concat_axis=0, tiled=True, axis_index_groups=core_groups
    )
    grad_sum = jnp.sum(received_parts.astype(jnp.float32), axis=0)

    rotation = (my_group + jnp.arange(n_groups, dtype=jnp.int32)) % n_groups
    back_send = jnp.einsum(
        "scr,rif->scif",
        jnp.take(routing, rotation, axis=0).astype(jnp.bfloat16),
        grad_tiles,
        preferred_element_type=jnp.float32,
    ).astype(jnp.bfloat16)
    pieces = [back_send[0]] + [
        lax.ppermute(back_send[k], "grp", [(i, (i + k) % n_groups) for i in range(n_groups)])
        for k in range(1, n_groups)
    ]
    back_slot = ((my_group - my_dest) % n_groups) * capacity + my_rank
    own_sum = None
    for k, piece in enumerate(pieces):
        place_k = (
            back_slot[:, None] == (k * capacity + jnp.arange(capacity, dtype=jnp.int32))[None, :]
        ).astype(jnp.bfloat16)
        term = jnp.einsum("hc,cif->hif", place_k, piece, preferred_element_type=jnp.float32)
        own_sum = term if own_sum is None else own_sum + term
    own_pick = own_sum.astype(jnp.bfloat16)
    hub_back = jnp.einsum("hij,hif->hjf", hub_tiles, own_pick, preferred_element_type=jnp.float32)
    col_hot = (hub_cols[:, None] == tile_range[None, :]).astype(jnp.float32)
    grad_sum = grad_sum + jnp.einsum("hr,hjf->rjf", col_hot, hub_back, precision=highest)
    grad_rows = grad_sum.reshape(rows_dev, width).astype(jnp.bfloat16)
    weight_term = lax.dot_general(
        feats, grad_rows, (((0,), (0,)), ((), ())), preferred_element_type=jnp.float32
    )
    grad_scale = 1.0 / math.sqrt(rows_dev * n_blocks * n_groups)
    grad_weight = weight_sum(weight_term, n_groups, n_blocks) * grad_scale
    grad_feats = lax.dot_general(
        grad_rows, weight, (((1,), (1,)), ((), ())), preferred_element_type=jnp.float32
    ).astype(jnp.bfloat16)
    return (layer_out, grad_feats, grad_weight)


def solution(mesh):
    in_specs = (
        P(("grp", "blk"), None),
        P(),
        P(("grp", "blk"), None),
        P(("grp", "blk")),
        P("grp", "blk", None, None, None, None),
        P("grp", "blk", None, None),
        P("grp", "blk", None, None),
        P("grp", "blk", None),
        P("grp", "blk", None, None, None),
        P("grp", "blk", None),
        P(None, "blk", None, None),
        P(None, "blk", None),
    )
    out_specs = (P(("grp", "blk"), None), P(("grp", "blk"), None), P())
    return jax.shard_map(local, mesh=mesh, in_specs=in_specs, out_specs=out_specs, check_vma=False)
```
